32 devices in a mesh: seq: 8 (over z, x), wa: 4 (over y, core).
Axes of the slice: x: 2, y: 2, z: 4, core: 2. Of those that a mesh axis runs over, the one named last changes fastest.
Arguments:
- tokens: bfloat16 [2048, 1024], P('seq'), may hold values from -6 to 6
- gain_mix: float32 [1024], replicated, may hold values from 0.5 to 1.5
- w_z: bfloat16 [1024, 1536], P('seq', 'wa'), may hold values from -0.1875 to 0.1875
- w_x: bfloat16 [1024, 1536], P('seq', 'wa'), may hold values from -0.1875 to 0.1875
- w_bc: bfloat16 [1024, 256], P('seq'), may hold values from -0.046875 to 0.046875
- w_dt: bfloat16 [1024, 24], P('seq', 'wa'), may hold values from -0.1875 to 0.1875
- conv_x: float32 [4, 1536], P(None, 'wa'), may hold values from -3 to 3
- conv_bc: float32 [4, 256], replicated, may hold values from -3 to 3
- dt_bias: float32 [24], P('wa'), may hold values from -1 to 1
- a_log: float32 [24], P('wa'), may hold values from -10.5 to -3
- d_skip: float32 [24], P('wa'), may hold values from 0.5 to 1.5
- w_out: bfloat16 [1536, 1024], P('wa', 'seq'), may hold values from -0.0390625 to 0.0390625
- w_q: bfloat16 [1024, 512], P('seq', 'wa'), may hold values from -0.1875 to 0.1875
- w_kv: bfloat16 [1024, 256], P('seq'), may hold values from -0.1875 to 0.1875
- w_o: bfloat16 [512, 1024], P('wa', 'seq'), may hold values from -1 to 1
- gain_ffn: float32 [1024], replicated, may hold values from 0.5 to 1.5
- w_gate: bfloat16 [1024, 2048], P('seq', 'wa'), may hold values from -0.1875 to 0.1875
- w_up: bfloat16 [1024, 2048], P('seq', 'wa'), may hold values from -0.1875 to 0.1875
- w_down: bfloat16 [2048, 1024], P('wa', 'seq'), may hold values from -0.125 to 0.125
- cotangent: bfloat16 [2048, 1024], P('seq'), may hold values from -6 to 6
Outputs:
- output: bfloat16 [2048, 1024], P('seq', 'wa')
- grad_tokens: float32 [2048, 1024], P('seq')
- grad_gain_mix: float32 [1024], replicated
- grad_w_z: float32 [1024, 1536], P('seq', 'wa')
- grad_w_x: float32 [1024, 1536], P('seq', 'wa')
- grad_w_bc: float32 [1024, 256], P('seq')
- grad_w_dt: float32 [1024, 24], P('seq', 'wa')
- grad_conv_x: float32 [4, 1536], P(None, 'wa')
- grad_conv_bc: float32 [4, 256], replicated
- grad_dt_bias: float32 [24], P('wa')
- grad_a_log: float32 [24], P('wa')
- grad_d_skip: float32 [24], P('wa')
- grad_w_out: float32 [1536, 1024], P('wa', 'seq')
- grad_w_q: float32 [1024, 512], P('seq', 'wa')
- grad_w_kv: float32 [1024, 256], P('seq')
- grad_w_o: float32 [512, 1024], P('wa', 'seq')
- grad_gain_ffn: float32 [1024], replicated
- grad_w_gate: float32 [1024, 2048], P('seq', 'wa')
- grad_w_up: float32 [1024, 2048], P('seq', 'wa')
- grad_w_down: float32 [2048, 1024], P('wa', 'seq')
The draws below stay inside these ranges and needn't reach their ends.
All inputs are finite; a program needn't handle non-finite values.
Results may differ from the reference program's by a relative error of at most 0.012.
Values may be sent and summed in bfloat16 or wider, within the bound.
A program may use at most 128 MiB of HBM per device.

```python
import jax
import jax.numpy as jnp
from jax import lax

D = 1024
MH = 24
SH = 64
NS = 128
CONVK = 4
QH = 8
KVH = 2
HD = 64
FF = 2048
TOK_DEV = 256
DI = 1536
TOKENS = 2048


def draw_a_log(key, part):
    slow_key = jax.random.fold_in(key, 31)
    fast_key = jax.random.fold_in(key, 32)
    order_key = jax.random.fold_in(key, 33)
    slow_rates = jax.random.uniform(slow_key, (MH,), jnp.float32, -10.5, -8.7)
    fast_rates = jax.random.uniform(fast_key, (MH,), jnp.float32, -5.5, -3.0)
    ranking = jax.random.permutation(order_key, MH)
    slow_count = MH // 2
    return jnp.where(ranking < slow_count, slow_rates, fast_rates).astype(jnp.float32)


def shard_levels(key, shape, shards, smallest, high):
    factor_of = 1.0
    for position, blocks in shards:
        heights = jax.random.uniform(jax.random.fold_in(jax.random.fold_in(key, 6), position), (blocks,), jnp.float32, smallest / len(shards), high / len(shards))
        factor_of = factor_of * jnp.repeat(jnp.exp(heights), shape[position] // blocks).reshape((-1,) + (1,) * (len(shape) - 1 - position))
    return factor_of


def bell_draw(stream_key, extent, scale, bound, split=(), held_as=jnp.bfloat16):
    factor_of = shard_levels(stream_key, extent, split, -0.22, 0.18) if split else 1.0
    values = jax.random.normal(stream_key, extent, jnp.float32) * scale * factor_of
    return jnp.minimum(jnp.maximum(values, -bound), bound).astype(held_as)


def setup_inputs(seed: int = 0) -> dict:
    seeds = jax.random.split(jax.random.key(seed), 21)
    return {
        "tokens": bell_draw(seeds[0], (TOKENS, D), 1.0, 6.0, ((0, 8),)),
        "gain_mix": jnp.clip(1.0 + 0.1 * jax.random.normal(seeds[1], (D,), jnp.float32), 0.5, 1.5),
        "w_z": bell_draw(seeds[2], (D, DI), D ** -0.5, 0.1875, ((0, 8), (1, 4))),
        "w_x": bell_draw(seeds[3], (D, DI), D ** -0.5, 0.1875, ((0, 8), (1, 4))),
        "w_bc": bell_draw(seeds[4], (D, 2 * NS), (16 * D) ** -0.5, 0.046875, ((0, 8),)),
        "w_dt": bell_draw(seeds[5], (D, MH), D ** -0.5, 0.1875, ((0, 8), (1, 4))),
        "conv_x": bell_draw(seeds[6], (CONVK, DI), CONVK ** -0.5, 3.0, ((1, 4),), jnp.float32),
        "conv_bc": bell_draw(seeds[7], (CONVK, 2 * NS), CONVK ** -0.5, 3.0, (), jnp.float32),
        "dt_bias": jnp.clip(jax.random.uniform(seeds[8], (MH,), jnp.float32, -1.0, 1.0) * shard_levels(seeds[8], (MH,), ((0, 4),), -0.4, 0.0), -1.0, 1.0),
        "a_log": draw_a_log(jax.random.fold_in(seeds[20], 71), 0),
        "d_skip": jnp.clip(0.5 + 1.0 * jax.random.uniform(seeds[10], (MH,), jnp.float32) ** shard_levels(seeds[10], (MH,), ((0, 4),), -0.2, 0.2), 0.5, 1.5),
        "w_out": bell_draw(seeds[11], (DI, D), (16 * DI) ** -0.5, 0.0390625, ((0, 4), (1, 8))),
        "w_q": bell_draw(seeds[12], (D, QH * HD), D ** -0.5, 0.1875, ((0, 8), (1, 4))),
        "w_kv": bell_draw(seeds[13], (D, 2 * KVH * HD), D ** -0.5, 0.1875, ((0, 8),)),
        "w_o": bell_draw(seeds[14], (QH * HD, D), (QH * HD // 16) ** -0.5, 1.0, ((0, 4), (1, 8))),
        "gain_ffn": jnp.clip(1.0 + 0.1 * jax.random.normal(seeds[15], (D,), jnp.float32), 0.5, 1.5),
        "w_gate": bell_draw(seeds[16], (D, FF), D ** -0.5, 0.1875, ((0, 8), (1, 4))),
        "w_up": bell_draw(seeds[17], (D, FF), D ** -0.5, 0.1875, ((0, 8), (1, 4))),
        "w_down": bell_draw(seeds[18], (FF, D), FF ** -0.5, 0.125, ((0, 4), (1, 8))),
        "cotangent": bell_draw(seeds[19], (TOKENS, D), 1.0, 6.0, ((0, 8),)),
    }


EPS = 1e-05
ROPE_BASE = 100000000000.0
highest = lax.Precision.HIGHEST

def bf16_keep(values):
    return lax.optimization_barrier(values.astype(jnp.bfloat16))

def project(left_side, right_side):
    return jnp.dot(left_side, right_side, preferred_element_type=jnp.float32)

def rms_scale(row_values):
    return lax.rsqrt(lax.optimization_barrier(jnp.mean(row_values * row_values, axis=-1, keepdims=True)) + EPS)

def rope_tables(positions):
    frequency = ROPE_BASE ** (-(jnp.arange(HD // 2, dtype=jnp.float32) * 2.0 / HD))
    angles = positions.astype(jnp.float32)[:, None] * frequency[None, :]
    return (jnp.cos(angles), jnp.sin(angles))

def rotate(values, cosine, sine):
    half_width = values.shape[-1] // 2
    first_half = values[..., :half_width]
    second_half = values[..., half_width:]
    cos_part = cosine[:, None, :]
    sin_part = sine[:, None, :]
    return jnp.concatenate([first_half * cos_part - second_half * sin_part, second_half * cos_part + first_half * sin_part], axis=-1)

def unrotate(gradients, cosine, sine):
    half_width = gradients.shape[-1] // 2
    first_half = gradients[..., :half_width]
    second_half = gradients[..., half_width:]
    cos_part = cosine[:, None, :]
    sin_part = sine[:, None, :]
    return jnp.concatenate([first_half * cos_part + second_half * sin_part, second_half * cos_part - first_half * sin_part], axis=-1)

def conv_silu(pre_values, kernel, edge_rows):
    length = pre_values.shape[0]
    padded = jnp.concatenate([edge_rows, pre_values], axis=0)
    running = kernel[0] * padded[0:length]
    for offset in range(1, CONVK):
        running = running + kernel[offset] * padded[offset:offset + length]
    return jax.nn.silu(running)

def prepare(x_input, bc_input, dt_input, edge_x, edge_bc, conv_x, conv_bc, dt_bias, a_log):
    length = x_input.shape[0]
    head_count = a_log.shape[0]
    x_conv = conv_silu(x_input, conv_x, edge_x).reshape(length, head_count, -1)
    bc_conv = conv_silu(bc_input, conv_bc, edge_bc)
    step_size = jax.nn.softplus(dt_input + dt_bias[None, :])
    log_decay = -jnp.exp(a_log)[None, :] * step_size
    return (x_conv, bc_conv[:, :NS], bc_conv[:, NS:], step_size, log_decay)

def ssd_state(x_conv, b_mat, step_size, log_decay):
    cumulative = jnp.cumsum(log_decay, axis=0)
    tail_weight = jnp.exp(cumulative[-1][None, :] - cumulative) * step_size
    local_state = jnp.einsum('sh,shp,sn->hpn', tail_weight, x_conv, b_mat, precision=highest)
    return (jnp.exp(cumulative[-1]), local_state)

def ssd_output(x_conv, b_mat, c_mat, step_size, log_decay, start_state):
    cumulative = jnp.cumsum(log_decay, axis=0)
    length = x_conv.shape[0]
    causal = jnp.arange(length, dtype=jnp.int32)[:, None] >= jnp.arange(length, dtype=jnp.int32)[None, :]
    gap_sums = cumulative[:, None, :] - cumulative[None, :, :]
    decays = jnp.exp(jnp.where(causal[:, :, None], gap_sums, -1e+30))
    intersections = jnp.dot(c_mat, b_mat.T, precision=highest)
    mixing = decays * intersections[:, :, None] * step_size[None, :, :]
    inner_part = jnp.einsum('tsh,shp->thp', mixing, x_conv, precision=highest)
    carried = jnp.einsum('tn,hpn->thp', c_mat, start_state, precision=highest) * jnp.exp(cumulative)[:, :, None]
    return inner_part + carried

def mixer_reference(z_proj, x_proj, bc_proj, dt_proj, conv_x, conv_bc, dt_bias, a_log, d_skip):
    edge_x = jnp.zeros((CONVK - 1, x_proj.shape[1]), jnp.float32)
    edge_bc = jnp.zeros((CONVK - 1, bc_proj.shape[1]), jnp.float32)
    x_conv, b_mat, c_mat, step_size, log_decay = prepare(x_proj, bc_proj, dt_proj, edge_x, edge_bc, conv_x, conv_bc, dt_bias, a_log)
    blocks = TOKENS // TOK_DEV

    def advance(state_now, pieces):
        x_block, b_block, c_block, step_block, decay_block = pieces
        outputs = ssd_output(x_block, b_block, c_block, step_block, decay_block, state_now)
        decay_total, local_state = ssd_state(x_block, b_block, step_block, decay_block)
        return (decay_total[:, None, None] * state_now + local_state, outputs)
    stacked = (x_conv.reshape(blocks, TOK_DEV, MH, SH), b_mat.reshape(blocks, TOK_DEV, NS), c_mat.reshape(blocks, TOK_DEV, NS), step_size.reshape(blocks, TOK_DEV, MH), log_decay.reshape(blocks, TOK_DEV, MH))
    _, outputs = lax.scan(advance, jnp.zeros((MH, SH, NS), jnp.float32), stacked)
    ssm_out = outputs.reshape(TOKENS, MH, SH) + d_skip[None, :, None] * x_conv
    return ssm_out.reshape(TOKENS, DI) * jax.nn.silu(z_proj)

def attention_forward(q_rot, k_rot, v_val):
    group_size = QH // KVH
    key_rows = jnp.repeat(k_rot, group_size, axis=1).astype(jnp.float32)
    value_rows = jnp.repeat(v_val, group_size, axis=1).astype(jnp.float32)
    block_size = 512 if TOKENS % 512 == 0 else TOKENS
    inv_root = HD ** (-0.5)
    key_pos = jnp.arange(TOKENS, dtype=jnp.int32)

    def one_block(start_row):
        queries = lax.dynamic_slice_in_dim(q_rot, start_row, block_size, 0).astype(jnp.float32)
        query_pos = start_row + jnp.arange(block_size, dtype=jnp.int32)
        scores = jnp.einsum('tgd,ngd->gtn', queries, key_rows) * inv_root
        allowed = key_pos[None, None, :] <= query_pos[None, :, None]
        row_max = lax.optimization_barrier(jnp.max(jnp.where(allowed, scores, -1e+30), axis=-1))
        weights = jnp.where(allowed, jnp.exp(scores - row_max[:, :, None]), 0.0)
        row_sum = lax.optimization_barrier(jnp.sum(weights, axis=-1))
        rounded = bf16_keep(weights).astype(jnp.float32)
        weighted_sum = jnp.einsum('gtn,ngd->tgd', rounded, value_rows)
        attn_block = bf16_keep(weighted_sum / row_sum.T[:, :, None])
        return (attn_block, (row_max + jnp.log(row_sum)).T)
    starts = jnp.arange(TOKENS // block_size, dtype=jnp.int32) * block_size
    attn_heads, log_sums = lax.map(one_block, starts)
    return (attn_heads.reshape(TOKENS, QH, HD), log_sums.reshape(TOKENS, QH))

def attention_backward(q_rot, k_rot, v_val, d_attn, log_sums, out_delta):
    group_size = QH // KVH
    key_rows = jnp.repeat(k_rot, group_size, axis=1).astype(jnp.float32)
    value_rows = jnp.repeat(v_val, group_size, axis=1).astype(jnp.float32)
    block_size = 512 if TOKENS % 512 == 0 else TOKENS
    inv_root = HD ** (-0.5)
    key_pos = jnp.arange(TOKENS, dtype=jnp.int32)

    def visit_block(totals, start_row):
        key_total, value_total = totals
        queries = lax.dynamic_slice_in_dim(q_rot, start_row, block_size, 0).astype(jnp.float32)
        grads_in = lax.dynamic_slice_in_dim(d_attn, start_row, block_size, 0).astype(jnp.float32)
        sums_in = lax.dynamic_slice_in_dim(log_sums, start_row, block_size, 0)
        delta_in = lax.dynamic_slice_in_dim(out_delta, start_row, block_size, 0)
        query_pos = start_row + jnp.arange(block_size, dtype=jnp.int32)
        scores = jnp.einsum('tgd,ngd->gtn', queries, key_rows) * inv_root
        allowed = key_pos[None, None, :] <= query_pos[None, :, None]
        probability = jnp.where(allowed, jnp.exp(scores - sums_in.T[:, :, None]), 0.0)
        d_probs = jnp.einsum('tgd,ngd->gtn', grads_in, value_rows)
        d_scores = bf16_keep(probability * (d_probs - delta_in.T[:, :, None])).astype(jnp.float32)
        probs_b = bf16_keep(probability).astype(jnp.float32)
        d_query = jnp.einsum('gtn,ngd->tgd', d_scores, key_rows) * inv_root
        key_total = key_total + jnp.einsum('gtn,tgd->ngd', d_scores, queries) * inv_root
        value_total = value_total + jnp.einsum('gtn,tgd->ngd', probs_b, grads_in)
        return ((key_total, value_total), d_query)
    starts = jnp.arange(TOKENS // block_size, dtype=jnp.int32) * block_size
    zeros_heads = jnp.zeros((TOKENS, QH, HD), jnp.float32)
    (key_total, value_total), d_query = lax.scan(visit_block, (zeros_heads, zeros_heads), starts)
    d_key = key_total.reshape(TOKENS, KVH, group_size, HD).sum(axis=2)
    d_value = value_total.reshape(TOKENS, KVH, group_size, HD).sum(axis=2)
    return (d_query.reshape(TOKENS, QH, HD), d_key, d_value)

def reference(tokens, gain_mix, w_z, w_x, w_bc, w_dt, conv_x, conv_bc, dt_bias, a_log, d_skip, w_out, w_q, w_kv, w_o, gain_ffn, w_gate, w_up, w_down, cotangent):
    tokens_wide = tokens.astype(jnp.float32)
    scale_mix = rms_scale(tokens_wide)
    normed = bf16_keep(tokens_wide * scale_mix * gain_mix)
    z_proj = project(normed, w_z)
    x_proj = project(normed, w_x)
    bc_proj = project(normed, w_bc)
    dt_proj = project(normed, w_dt)
    ssm_gated, pull_mixer = jax.vjp(mixer_reference, z_proj, x_proj, bc_proj, dt_proj, conv_x, conv_bc, dt_bias, a_log, d_skip)
    gated = bf16_keep(ssm_gated)
    positions = jnp.arange(TOKENS, dtype=jnp.int32)
    cosine, sine = rope_tables(positions)
    q_proj = project(normed, w_q).reshape(TOKENS, QH, HD)
    kv_proj = project(normed, w_kv)
    k_proj = kv_proj[:, :KVH * HD].reshape(TOKENS, KVH, HD)
    v_val = bf16_keep(kv_proj[:, KVH * HD:].reshape(TOKENS, KVH, HD))
    q_rot = bf16_keep(rotate(q_proj, cosine, sine))
    k_rot = bf16_keep(rotate(k_proj, cosine, sine))
    attn_heads, log_sums = attention_forward(q_rot, k_rot, v_val)
    attn_out = attn_heads.reshape(TOKENS, QH * HD)
    hidden = tokens_wide + project(gated, w_out) + project(attn_out, w_o)
    scale_ffn = rms_scale(hidden)
    hnormed = bf16_keep(hidden * scale_ffn * gain_ffn)
    gate_proj = project(hnormed, w_gate)
    up_proj = project(hnormed, w_up)
    activated = bf16_keep(jax.nn.silu(gate_proj) * up_proj)
    output = (hidden + project(activated, w_down)).astype(jnp.bfloat16)
    cot_wide = cotangent.astype(jnp.float32)
    d_act = project(cotangent, w_down.T)
    sigmoid_gate = jax.nn.sigmoid(gate_proj)
    d_gate = bf16_keep(d_act * up_proj * sigmoid_gate * (1.0 + gate_proj * (1.0 - sigmoid_gate)))
    d_up = bf16_keep(d_act * gate_proj * sigmoid_gate)
    d_hnormed = project(d_gate, w_gate.T) + project(d_up, w_up.T)
    hidden_hat = hidden * scale_ffn
    weighted_ffn = d_hnormed * gain_ffn
    d_hidden = cot_wide + scale_ffn * (weighted_ffn - hidden_hat * lax.optimization_barrier(jnp.mean(weighted_ffn * hidden_hat, axis=-1, keepdims=True)))
    grad_gain_ffn = lax.optimization_barrier(jnp.sum(d_hnormed * hidden_hat, axis=0))
    d_hidden_b = bf16_keep(d_hidden)
    d_gated = project(d_hidden_b, w_out.T)
    d_attn = bf16_keep(project(d_hidden_b, w_o.T)).reshape(TOKENS, QH, HD)
    out_delta = lax.optimization_barrier(jnp.sum(d_attn.astype(jnp.float32) * attn_heads.astype(jnp.float32), axis=-1))
    d_q_rot, d_k_rot, d_value = attention_backward(q_rot, k_rot, v_val, d_attn, log_sums, out_delta)
    d_q = bf16_keep(unrotate(d_q_rot, cosine, sine).reshape(TOKENS, QH * HD))
    d_kv = bf16_keep(jnp.concatenate([unrotate(d_k_rot, cosine, sine).reshape(TOKENS, KVH * HD), d_value.reshape(TOKENS, KVH * HD)], axis=1))
    d_z, d_x, d_bc, d_dt, grad_conv_x, grad_conv_bc, grad_dt_bias, grad_a_log, grad_d_skip = pull_mixer(d_gated)
    d_z_b = bf16_keep(d_z)
    d_x_b = bf16_keep(d_x)
    d_bc_b = bf16_keep(d_bc)
    d_dt_b = bf16_keep(d_dt)
    d_normed = project(d_z_b, w_z.T) + project(d_x_b, w_x.T) + project(d_bc_b, w_bc.T) + project(d_dt_b, w_dt.T) + project(d_q, w_q.T) + project(d_kv, w_kv.T)
    tokens_hat = tokens_wide * scale_mix
    weighted_mix = d_normed * gain_mix
    grad_tokens = d_hidden + scale_mix * (weighted_mix - tokens_hat * lax.optimization_barrier(jnp.mean(weighted_mix * tokens_hat, axis=-1, keepdims=True)))
    grad_gain_mix = lax.optimization_barrier(jnp.sum(d_normed * tokens_hat, axis=0))
    return (output, grad_tokens, grad_gain_mix, project(normed.T, d_z_b), project(normed.T, d_x_b), project(normed.T, d_bc_b), project(normed.T, d_dt_b), grad_conv_x, grad_conv_bc, grad_dt_bias, grad_a_log, grad_d_skip, project(gated.T, d_hidden_b), project(normed.T, d_q), project(normed.T, d_kv), project(attn_out.T, d_hidden_b), grad_gain_ffn, project(hnormed.T, d_gate), project(hnormed.T, d_up), project(activated.T, cotangent))
```

```python
import functools

import jax
import jax.numpy as jnp
from jax import lax
from jax.experimental import pallas as pl
from jax.experimental.pallas import tpu as pltpu
from jax.sharding import PartitionSpec as P

NS = 128
CONVK = 4
QH = 8
KVH = 2
HD = 64


EPS = 1e-05
ROPE_BASE = 100000000000.0
highest = lax.Precision.HIGHEST


def passed_along(value, axis, steps):
    count = lax.axis_size(axis)
    leading, last = (max(0, -steps), min(count, count - steps))
    return lax.ppermute(value, axis, [(source, source + steps) for source in range(leading, last)])


def project(left_side, right_side):
    return jnp.dot(left_side, right_side, preferred_element_type=jnp.float32)


def rms_scale(row_values):
    return lax.rsqrt(jnp.mean(row_values * row_values, axis=-1, keepdims=True) + EPS)


def rope_tables(positions):
    frequency = ROPE_BASE ** (-(jnp.arange(HD // 2, dtype=jnp.float32) * 2.0 / HD))
    angles = positions.astype(jnp.float32)[:, None] * frequency[None, :]
    return (jnp.cos(angles), jnp.sin(angles))


def rotate(values, cosine, sine):
    half_width = values.shape[-1] // 2
    first_half = values[..., :half_width]
    second_half = values[..., half_width:]
    cos_part = cosine[:, None, :]
    sin_part = sine[:, None, :]
    return jnp.concatenate(
        [
            first_half * cos_part - second_half * sin_part,
            second_half * cos_part + first_half * sin_part,
        ],
        axis=-1,
    )


def unrotate(gradients, cosine, sine):
    half_width = gradients.shape[-1] // 2
    first_half = gradients[..., :half_width]
    second_half = gradients[..., half_width:]
    cos_part = cosine[:, None, :]
    sin_part = sine[:, None, :]
    return jnp.concatenate(
        [
            first_half * cos_part + second_half * sin_part,
            second_half * cos_part - first_half * sin_part,
        ],
        axis=-1,
    )


HALO = 16
SUM_TYPE = jnp.bfloat16
LANES = 128


def rounded_up(width):
    return -(-width // LANES) * LANES


def prepare(x_rows, bc_rows, dt_input, conv_x, conv_bc, dt_bias, a_log):
    length, head_count = dt_input.shape

    def conv_silu(padded, kernel):
        first = padded.shape[0] - length - CONVK + 1
        running = kernel[0] * padded[first : first + length]
        for offset in range(1, CONVK):
            running = running + kernel[offset] * padded[first + offset : first + offset + length]
        return jax.nn.silu(running)

    x_heads = conv_silu(x_rows, conv_x).reshape(length, head_count, -1).transpose(1, 0, 2)
    bc_conv = conv_silu(bc_rows, conv_bc)
    step_size = jax.nn.softplus(dt_input + dt_bias[None, :]).T
    log_decay = -jnp.exp(a_log)[:, None] * step_size
    ticks = jnp.arange(length, dtype=jnp.int32)
    upto = (ticks[:, None] <= ticks[None, :]).astype(jnp.float32)
    cumulative = jnp.dot(log_decay, upto, precision=highest)
    return (x_heads, bc_conv[:, :NS], bc_conv[:, NS:], step_size, cumulative)


def ssd_state(x_heads, b_mat, step_size, cumulative):
    tail_weight = jnp.exp(cumulative[:, -1:] - cumulative) * step_size
    local_state = jnp.einsum(
        "hsp,sn->hpn", x_heads * tail_weight[:, :, None], b_mat, precision=highest
    )
    return (cumulative[:, -1], local_state)


def ssd_gated(z_input, x_heads, b_mat, c_mat, step_size, cumulative, d_skip, start_state):
    head_count, length, _ = x_heads.shape
    ticks = jnp.arange(length, dtype=jnp.int32)
    causal = ticks[:, None] >= ticks[None, :]
    gap_sums = cumulative[:, :, None] - cumulative[:, None, :]
    decays = jnp.exp(jnp.where(causal[None], gap_sums, -1e30))
    intersections = lax.dot_general(c_mat, b_mat, (((1,), (1,)), ((), ())), precision=highest)
    mixing = decays * intersections[None] * step_size[:, None, :]
    inner_part = jnp.einsum("hts,hsp->htp", mixing, x_heads, precision=highest)
    carried = (
        jnp.einsum("tn,hpn->htp", c_mat, start_state, precision=highest)
        * jnp.exp(cumulative)[:, :, None]
    )
    ssm_out = inner_part + carried + d_skip[:, None, None] * x_heads
    return ssm_out.transpose(1, 0, 2).reshape(length, -1) * jax.nn.silu(z_input)


def times(left_side, right_side, left_dim, right_dim):
    return lax.dot_general(
        left_side,
        right_side,
        (((left_dim,), (right_dim,)), ((), ())),
        preferred_element_type=jnp.float32,
    )


def split_columns(packed, widths):
    pieces, at = ([], 0)
    for width in widths:
        pieces.append(packed[:, at : at + width])
        at += rounded_up(width)
    return pieces


def padded_columns(values):
    return jnp.pad(values, ((0, 0), (0, rounded_up(values.shape[1]) - values.shape[1])))


def pack_columns(pieces):
    return jnp.concatenate([padded_columns(piece) for piece in pieces], axis=1)


MESH = pl.DeviceIdType.MESH
HBM = pl.BlockSpec(memory_space=pl.ANY)
VMEM = pl.BlockSpec(memory_space=pltpu.VMEM)
VMEM_LIMIT = 60 * 1024 * 1024


def ring_place(index, count):
    odd = lax.rem(index, 2)
    half = lax.div(index, 2)
    return (1 - odd) * half + odd * (count - 1 - half)


def ring_index(place, count):
    place = lax.rem(place + 2 * count, count)
    upper = lax.div(place, count // 2)
    return (1 - upper) * 2 * place + upper * (2 * (count - place) - 1)


def greet(peers):
    barrier = pltpu.get_barrier_semaphore()
    for peer in peers:
        pl.semaphore_signal(barrier, inc=1, device_id=peer, device_id_type=MESH)
    pl.semaphore_wait(barrier, len(peers))


def remote(source, target, send, receive, peer):
    return pltpu.make_async_remote_copy(
        src_ref=source,
        dst_ref=target,
        send_sem=send,
        recv_sem=receive,
        device_id=peer,
        device_id_type=MESH,
    )


def comm_params(collective_id):
    return pltpu.CompilerParams(
        collective_id=collective_id, has_side_effects=True, vmem_limit_bytes=VMEM_LIMIT
    )


def gather_kernel(count, chunks, has_halo, *refs):
    ins, refs = refs[:chunks], refs[chunks:]
    if has_halo:
        halo_in, refs = refs[0], refs[1:]
    outs, refs = refs[:chunks], refs[chunks:]
    if has_halo:
        halo_out, refs = refs[0], refs[1:]
    send, receive, local = refs[:3]
    seq = lax.axis_index("seq")
    place = ring_place(seq, count)
    sides = [{"seq": ring_index(place + 1, count)}, {"seq": ring_index(place - 1, count)}]
    following = {"seq": lax.rem(seq + 1, count)}
    preceding = {"seq": lax.rem(seq + count - 1, count)}
    greet(sides + ([following, preceding] if has_halo else []))
    steps = count // 2
    pending = []
    if has_halo:
        halo = remote(halo_in, halo_out, refs[3].at[0], refs[3].at[1], following)
        halo.start()
    for c in range(chunks):
        keep = pltpu.make_async_copy(ins[c], outs[c].at[seq], local.at[c])
        keep.start()
        pending.append(keep)

    def piece(c, owner, side, step):
        if step < steps - 1:
            return outs[c].at[owner]
        rows = ins[c].shape[0] // 2
        return outs[c].at[owner, pl.ds(side * rows, rows)]

    def source(c, side, step):
        if step < steps - 1:
            return ins[c]
        rows = ins[c].shape[0] // 2
        return ins[c].at[pl.ds(side * rows, rows)]

    def transfer(c, side, step):
        owner = ring_index(place + (step if side else -step), count)
        target = piece(c, owner, side, step)
        origin = source(c, side, step) if step == 0 else target
        return remote(
            origin, target, send.at[c, side, step], receive.at[c, side, step], sides[side]
        )

    def arrival(c, side, step):
        owner = ring_index(place + (step + 1 if side else -step - 1), count)
        target = piece(c, owner, side, step)
        return remote(
            target, target, send.at[c, side, step], receive.at[c, side, step], sides[side]
        )

    for step in range(steps):
        for c in range(chunks):
            for side in range(2):
                if step:
                    arrival(c, side, step - 1).wait_recv()
                transfer(c, side, step).start()
    for c in range(chunks):
        for side in range(2):
            arrival(c, side, steps - 1).wait_recv()
            for step in range(steps):
                transfer(c, side, step).wait_send()
    for keep in pending:
        keep.wait()
    if has_halo:
        halo.wait()


def ring_gather(arrays, collective_id, halo=None):
    count = lax.axis_size("seq")
    chunks = len(arrays)
    shapes = [jax.ShapeDtypeStruct((count, *a.shape), a.dtype) for a in arrays]
    inputs = list(arrays)
    scratch = [
        pltpu.SemaphoreType.DMA((chunks, 2, count // 2)),
        pltpu.SemaphoreType.DMA((chunks, 2, count // 2)),
        pltpu.SemaphoreType.DMA((chunks,)),
    ]
    if halo is not None:
        inputs.append(halo)
        shapes.append(jax.ShapeDtypeStruct(halo.shape, halo.dtype))
        scratch.append(pltpu.SemaphoreType.DMA((2,)))
    return pl.pallas_call(
        functools.partial(gather_kernel, count, chunks, halo is not None),
        out_shape=shapes,
        in_specs=[HBM] * len(inputs),
        out_specs=[HBM] * len(shapes),
        scratch_shapes=scratch,
        compiler_params=comm_params(collective_id),
    )(*inputs)


def scatter_kernel(count, chunks, has_small, *refs):
    ins, refs = refs[:chunks], refs[chunks:]
    if has_small:
        small_in, refs = refs[0], refs[1:]
    outs, refs = refs[:chunks], refs[chunks:]
    if has_small:
        small_out, refs = refs[0], refs[1:]
    slots, refs = refs[:chunks], refs[chunks:]
    holds, refs = refs[:chunks], refs[chunks:]
    send, receive = refs[:2]
    seq = lax.axis_index("seq")
    place = ring_place(seq, count)
    sides = [{"seq": ring_index(place + 1, count)}, {"seq": ring_index(place - 1, count)}]
    others = [{"seq": lax.rem(seq + offset, count)} for offset in range(1, count)]
    greet(sides + (others if has_small else []))
    steps = count // 2
    small_copies = []
    if has_small:
        small_slots, small_send, small_receive = refs[2:5]
        for offset in range(1, count):
            copy = remote(
                small_in,
                small_slots.at[seq],
                small_send.at[offset - 1],
                small_receive.at[offset - 1],
                others[offset - 1],
            )
            copy.start()
            small_copies.append(copy)

    def mine(c, side, step):
        owner = ring_index(place + (step if side == 0 else -step), count)
        return ins[c].at[owner]

    def transfer(c, side, step):
        rows = ins[c].shape[1] // 2
        if step == steps:
            origin = mine(c, side, step).at[pl.ds(side * rows, rows)]
            target = slots[c].at[side, step - 1, pl.ds(side * rows, rows)]
        else:
            origin = holds[c].at[side, step - 1]
            target = slots[c].at[side, step - 1]
        return remote(
            origin,
            target,
            send.at[c, side, step - 1],
            receive.at[c, side, step - 1],
            sides[side],
        )

    for step in range(steps, 0, -1):
        for c in range(chunks):
            for side in range(2):
                if step < steps:
                    transfer(c, side, step + 1).wait_recv()
                    own = mine(c, side, step)
                    hold = holds[c].at[side, step - 1]
                    rows = ins[c].shape[1] // 2
                    if step == steps - 1:
                        near = pl.ds(side * rows, rows)
                        far = pl.ds((1 - side) * rows, rows)
                        hold[far, :] = own[far, :]
                        hold[near, :] = (
                            own[near, :].astype(jnp.float32)
                            + slots[c][side, step, near, :].astype(jnp.float32)
                        ).astype(hold.dtype)
                    else:
                        hold[...] = (
                            own[...].astype(jnp.float32)
                            + slots[c][side, step].astype(jnp.float32)
                        ).astype(hold.dtype)
                transfer(c, side, step).start()
    if has_small:
        for copy in small_copies:
            copy.wait()
        small_slots[pl.ds(seq, 1)] = small_in[...][None]
        total = small_slots[0]
        for other in range(1, count):
            total = total + small_slots[other]
        small_out[...] = total
    for c in range(chunks):
        for side in range(2):
            transfer(c, side, 1).wait_recv()
        outs[c][...] = (
            ins[c][seq].astype(jnp.float32)
            + slots[c][0, 0].astype(jnp.float32)
            + slots[c][1, 0].astype(jnp.float32)
        )
        for side in range(2):
            for step in range(1, steps + 1):
                transfer(c, side, step).wait_send()


def ring_scatter(arrays, collective_id, small=None):
    count = lax.axis_size("seq")
    chunks = len(arrays)
    shapes = [jax.ShapeDtypeStruct(a.shape[1:], jnp.float32) for a in arrays]
    inputs = list(arrays)
    scratch = [pltpu.VMEM((2, count // 2, *a.shape[1:]), a.dtype) for a in arrays] + [
        pltpu.VMEM((2, count // 2 - 1, *a.shape[1:]), a.dtype) for a in arrays
    ]
    scratch += [
        pltpu.SemaphoreType.DMA((chunks, 2, count // 2)),
        pltpu.SemaphoreType.DMA((chunks, 2, count // 2)),
    ]
    if small is not None:
        inputs.append(small)
        shapes.append(jax.ShapeDtypeStruct(small.shape, small.dtype))
        scratch += [
            pltpu.VMEM((count, *small.shape), small.dtype),
            pltpu.SemaphoreType.DMA((count - 1,)),
            pltpu.SemaphoreType.DMA((count - 1,)),
        ]
    return pl.pallas_call(
        functools.partial(scatter_kernel, count, chunks, small is not None),
        out_shape=shapes,
        in_specs=[VMEM] * len(inputs),
        out_specs=[VMEM] * len(shapes),
        scratch_shapes=scratch,
        compiler_params=comm_params(collective_id),
    )(*inputs)


def wa_kernel(pieces, has_part, *refs):
    value, refs = refs[0], refs[1:]
    if has_part:
        part, refs = refs[0], refs[1:]
    out, refs = refs[0], refs[1:]
    if has_part:
        part_out, refs = refs[0], refs[1:]
    near, far_send, far, send, receive = refs[:5]
    wa = lax.axis_index("wa")
    core = lax.rem(wa, 2)
    row = lax.div(wa, 2)
    mate = {"wa": 2 * row + 1 - core}
    across = {"wa": 2 * (1 - row) + core}
    greet([mate, across])
    rows = value.shape[0] // 2
    step = rows // pieces

    def first(p):
        return remote(
            value.at[pl.ds(pl.multiple_of((1 - core) * rows + p * step, step), step)],
            near.at[pl.ds(p * step, step)],
            send.at[0, p],
            receive.at[0, p],
            mate,
        )

    def second(p):
        at = pl.ds(p * step, step)
        return remote(far_send.at[at], far.at[at], send.at[1, p], receive.at[1, p], across)

    def third(p):
        at = pl.ds(pl.multiple_of(core * rows + p * step, step), step)
        return remote(out.at[at], out.at[at], send.at[2, p], receive.at[2, p], mate)

    def third_arrival(p):
        at = pl.ds(pl.multiple_of((1 - core) * rows + p * step, step), step)
        return remote(out.at[at], out.at[at], send.at[2, p], receive.at[2, p], mate)

    for p in range(pieces):
        first(p).start()
    if has_part:
        part_near, part_send, part_far, part_sems = refs[5:9]
        width = part.shape[1] // 4
        part_first = []
        for r in range(2):
            copy = remote(
                part.at[:, pl.ds(pl.multiple_of((2 * r + 1 - core) * width, 128), width)],
                part_near.at[r],
                part_sems.at[0, r],
                part_sems.at[1, r],
                mate,
            )
            copy.start()
            part_first.append(copy)
    for p in range(pieces):
        first(p).wait_recv()
        at = pl.ds(p * step, step)
        own = pl.ds(pl.multiple_of(core * rows + p * step, step), step)
        far_send[at, :] = (value[own, :] + near[at, :]).astype(far_send.dtype)
        second(p).start()
    if has_part:
        for copy in part_first:
            copy.wait_recv()
        other = pl.ds(pl.multiple_of((2 * (1 - row) + core) * width, 128), width)
        kept = pl.ds(pl.multiple_of((2 * row + core) * width, 128), width)
        part_send[...] = (part[:, other] + part_near[1 - row]).astype(part_send.dtype)
        part_second = remote(
            part_send, part_far, part_sems.at[0, 2], part_sems.at[1, 2], across
        )
        part_second.start()
    for p in range(pieces):
        second(p).wait_recv()
        at = pl.ds(p * step, step)
        own = pl.ds(pl.multiple_of(core * rows + p * step, step), step)
        out[own, :] = far_send[at, :].astype(jnp.float32) + far[at, :].astype(jnp.float32)
        third(p).start()
    if has_part:
        part_second.wait_recv()
        part_out[...] = part[:, kept] + part_near[row] + part_far[...].astype(jnp.float32)
        for copy in part_first:
            copy.wait_send()
        part_second.wait_send()
    for p in range(pieces):
        third_arrival(p).wait_recv()
        first(p).wait_send()
        second(p).wait_send()
        third(p).wait_send()


def wa_total(value, pieces, collective_id, part=None):
    rows, width = value.shape
    shapes = [jax.ShapeDtypeStruct(value.shape, value.dtype)]
    inputs = [value]
    scratch = [
        pltpu.VMEM((rows // 2, width), value.dtype),
        pltpu.VMEM((rows // 2, width), SUM_TYPE),
        pltpu.VMEM((rows // 2, width), SUM_TYPE),
        pltpu.SemaphoreType.DMA((3, pieces)),
        pltpu.SemaphoreType.DMA((3, pieces)),
    ]
    if part is not None:
        inputs.append(part)
        block = (part.shape[0], part.shape[1] // 4)
        shapes.append(jax.ShapeDtypeStruct(block, part.dtype))
        scratch += [
            pltpu.VMEM((2, *block), part.dtype),
            pltpu.VMEM(block, SUM_TYPE),
            pltpu.VMEM(block, SUM_TYPE),
            pltpu.SemaphoreType.DMA((2, 3)),
        ]
    outs = pl.pallas_call(
        functools.partial(wa_kernel, pieces, part is not None),
        out_shape=shapes,
        in_specs=[VMEM] * len(inputs),
        out_specs=[VMEM] * len(shapes),
        scratch_shapes=scratch,
        compiler_params=comm_params(collective_id),
    )(*inputs)
    return outs if part is not None else outs[0]


def split_three(values):
    high = values.astype(jnp.bfloat16)
    left = values - lax.reduce_precision(values, 8, 7)
    middle = left.astype(jnp.bfloat16)
    low = (left - lax.reduce_precision(left, 8, 7)).astype(jnp.bfloat16)
    return (high, middle, low)


def per_device(
    tokens,
    gain_mix,
    w_z,
    w_x,
    w_bc,
    w_dt,
    conv_x,
    conv_bc,
    dt_bias,
    a_log,
    d_skip,
    w_out,
    w_q,
    w_kv,
    w_o,
    gain_ffn,
    w_gate,
    w_up,
    w_down,
    cotangent,
):
    rows, width = tokens.shape
    seq_count = lax.axis_size("seq")
    seq_index = lax.axis_index("seq")
    wa_index = lax.axis_index("wa")
    head_count = a_log.shape[0]
    state_rows = head_count * (w_x.shape[1] // head_count)
    weights = (w_z, w_x, w_bc, w_q, w_kv, w_dt, w_gate, w_up, w_out.T, w_o.T, w_down.T)
    widths = [w.shape[1] for w in weights]
    first_width = sum(rounded_up(w) for w in widths[:6])
    groups = ring_gather(
        [pack_columns(weights[:6]), pack_columns(weights[8:10]), pack_columns(weights[6:8]), w_down.T],
        0,
        tokens[rows - HALO :],
    )
    full_first, full_mixed, full_ffn, full_down = [
        g.reshape(g.shape[0] * g.shape[1], g.shape[2]) for g in groups[:4]
    ]
    before = jnp.where(seq_index > 0, groups[4], 0)

    def normalised(values):
        wide = values.astype(jnp.float32)
        return (wide * rms_scale(wide) * gain_mix).astype(jnp.bfloat16)

    tokens_wide = tokens.astype(jnp.float32)
    scale_mix = rms_scale(tokens_wide)
    normed = (tokens_wide * scale_mix * gain_mix).astype(jnp.bfloat16)
    extended = jnp.concatenate([normalised(before), normed], axis=0)
    projected = project(extended, full_first)
    z_rows, x_rows, bc_rows, q_rows, kv_rows, dt_rows = split_columns(projected, widths[:6])
    z_proj = z_rows[HALO:]
    mixer_inputs = (x_rows, bc_rows, dt_rows[HALO:], conv_x, conv_bc, dt_bias, a_log)
    prepared, pull_prepare = jax.vjp(prepare, *mixer_inputs)
    x_heads, b_mat, c_mat, step_size, cumulative = prepared
    (log_total, local_state), pull_state = jax.vjp(
        ssd_state, x_heads, b_mat, step_size, cumulative
    )

    local_query = w_q.shape[1] // HD
    kv_head = wa_index * local_query // (QH // KVH)
    positions = seq_index * rows + jnp.arange(rows, dtype=jnp.int32)
    cosine, sine = rope_tables(positions)
    q_proj = q_rows[HALO:].reshape(rows, local_query, HD)
    kv_proj = kv_rows[HALO:]
    k_proj = lax.dynamic_slice_in_dim(kv_proj, kv_head * HD, HD, 1)
    v_proj = lax.dynamic_slice_in_dim(kv_proj, KVH * HD + kv_head * HD, HD, 1)
    q_rot = rotate(q_proj, cosine, sine).astype(jnp.bfloat16).transpose(1, 0, 2)
    k_rot = rotate(k_proj[:, None, :], cosine, sine)[:, 0, :]
    total_rows = jnp.pad(
        jnp.stack(split_three(log_total)), ((0, 2 * HALO - 3), (0, LANES - head_count))
    )
    state_sent = jnp.concatenate(
        [local_state.reshape(state_rows, NS).astype(jnp.bfloat16), total_rows], axis=0
    )
    key_arrived, state_arrived = ring_gather(
        [jnp.concatenate([k_rot, v_proj], axis=1).astype(jnp.bfloat16), state_sent], 1
    )
    key_all = key_arrived[:, :, :HD].reshape(seq_count * rows, HD)
    value_all = key_arrived[:, :, HD:].reshape(seq_count * rows, HD)
    states = state_arrived[:, :state_rows].astype(jnp.float32)
    totals = jnp.sum(
        state_arrived[:, state_rows : state_rows + 3, :head_count].astype(jnp.float32), axis=1
    )
    blocks = jnp.arange(seq_count, dtype=jnp.int32)
    low_end = jnp.minimum(blocks, seq_index)
    high_end = jnp.maximum(blocks, seq_index)
    between = (blocks[None, :] > low_end[:, None]) & (blocks[None, :] < high_end[:, None])
    path_decay = jnp.exp(jnp.sum(jnp.where(between[:, :, None], totals[None], 0.0), axis=1))
    earlier = jnp.where((blocks < seq_index)[:, None], path_decay, 0.0)
    later = jnp.where((blocks < seq_index)[:, None], path_decay, 0.0)
    shape_all = (seq_count, head_count, state_rows // head_count, NS)
    start_state = jnp.sum(earlier[:, :, None, None] * states.reshape(shape_all), axis=0)
    ssm_gated, pull_output = jax.vjp(
        ssd_gated, z_proj, x_heads, b_mat, c_mat, step_size, cumulative, d_skip, start_state
    )
    gated = ssm_gated.astype(jnp.bfloat16)

    key_pos = jnp.arange(seq_count * rows, dtype=jnp.int32)
    allowed = (key_pos[None, :] <= positions[:, None])[None]

    def per_head(left_side, right_side, left_dim, right_dim):
        return jnp.stack(
            [times(left_side[g], right_side, left_dim, right_dim) for g in range(local_query)]
        )

    scores = jnp.where(allowed, per_head(q_rot, key_all, 1, 1) * HD ** (-0.5), -1e30)
    row_max = jnp.max(scores, axis=-1, keepdims=True)
    attn_weights = jnp.exp(scores - row_max)
    row_sum = jnp.sum(attn_weights, axis=-1, keepdims=True)
    weighted_sum = per_head(attn_weights.astype(jnp.bfloat16), value_all, 1, 0)
    attn_heads = (weighted_sum / row_sum).astype(jnp.bfloat16)
    log_sums = row_max + jnp.log(row_sum)
    attn_out = attn_heads.transpose(1, 0, 2).reshape(rows, local_query * HD)
    mixed = jnp.concatenate([gated, attn_out], axis=1)
    hidden = tokens_wide + wa_total(times(mixed, full_mixed, 1, 1), 4, 2)
    scale_ffn = rms_scale(hidden)
    hnormed = (hidden * scale_ffn * gain_ffn).astype(jnp.bfloat16)
    ffn_width = widths[6]
    ffn_proj = project(hnormed, full_ffn)
    gate_proj = ffn_proj[:, :ffn_width]
    up_proj = ffn_proj[:, ffn_width:]
    activated = (jax.nn.silu(gate_proj) * up_proj).astype(jnp.bfloat16)
    ffn_part = times(activated, full_down, 1, 1)
    cot_wide = cotangent.astype(jnp.float32)
    d_act = project(cotangent, full_down)
    sigmoid_gate = jax.nn.sigmoid(gate_proj)
    d_gate = d_act * up_proj * sigmoid_gate * (1.0 + gate_proj * (1.0 - sigmoid_gate))
    d_up = d_act * gate_proj * sigmoid_gate
    d_ffn = jnp.concatenate([d_gate.astype(jnp.bfloat16), d_up.astype(jnp.bfloat16)], axis=1)
    d_hnormed, ffn_own = wa_total(times(d_ffn, full_ffn, 1, 1), 4, 3, ffn_part)
    hidden_hat = hidden * scale_ffn
    weighted_ffn = d_hnormed * gain_ffn
    d_hidden = cot_wide + scale_ffn * (
        weighted_ffn - hidden_hat * jnp.mean(weighted_ffn * hidden_hat, axis=-1, keepdims=True)
    )
    grad_gain_ffn = jnp.sum(d_hnormed * hidden_hat, axis=0)
    d_hidden_b = d_hidden.astype(jnp.bfloat16)
    d_mixed = project(d_hidden_b, full_mixed)
    inner_width = widths[8]
    d_gated = d_mixed[:, :inner_width]
    d_attn_heads = (
        d_mixed[:, inner_width:]
        .astype(jnp.bfloat16)
        .reshape(rows, local_query, HD)
        .transpose(1, 0, 2)
    )
    out_grads = pull_output(d_gated)
    direct = out_grads[7]
    out_delta = jnp.sum(
        d_attn_heads.astype(jnp.float32) * attn_heads.astype(jnp.float32), axis=-1, keepdims=True
    )
    probability = jnp.exp(scores - log_sums)
    d_probs = per_head(d_attn_heads, value_all, 1, 1)
    d_scores = (probability * (d_probs - out_delta)).astype(jnp.bfloat16)
    flat_rows = (local_query * rows, -1)
    d_key = times(d_scores.reshape(flat_rows), q_rot.reshape(flat_rows), 0, 0) * HD ** (-0.5)
    d_value = times(
        probability.astype(jnp.bfloat16).reshape(flat_rows), d_attn_heads.reshape(flat_rows), 0, 0
    )
    key_parts = jnp.concatenate([d_key, d_value], axis=1).reshape(seq_count, rows, 2 * HD)
    state_parts = (later[:, :, None, None] * direct[None]).reshape(seq_count, state_rows, NS)
    own_keys, own_states = ring_scatter(
        [key_parts.astype(SUM_TYPE), state_parts.astype(SUM_TYPE)], 4
    )
    d_q_rot = per_head(d_scores, key_all, 1, 0) * HD ** (-0.5)
    d_q = unrotate(d_q_rot.transpose(1, 0, 2), cosine, sine).reshape(rows, -1).astype(jnp.bfloat16)
    d_key_own = unrotate(own_keys[:, None, :HD], cosine, sine)[:, 0, :]
    d_value_own = own_keys[:, HD:]
    d_end = own_states.reshape(direct.shape)
    d_total = jnp.exp(log_total) * jnp.sum(d_end * start_state, axis=(1, 2))
    state_grads = pull_state((d_total, d_end))
    merged = (
        out_grads[1] + state_grads[0],
        out_grads[2] + state_grads[1],
        out_grads[3],
        out_grads[4] + state_grads[2],
        out_grads[5] + state_grads[3],
    )
    (
        d_x_rows,
        d_bc_rows,
        d_dt_in,
        grad_conv_x,
        grad_conv_bc,
        grad_dt_bias,
        grad_a_log,
    ) = pull_prepare(merged)
    x_width = widths[1]
    edge_back = passed_along(
        jnp.concatenate([d_x_rows[:HALO], d_bc_rows[:HALO]], axis=1), "seq", -1
    )
    d_x_in = d_x_rows[HALO:].at[rows - HALO :].add(edge_back[:, :x_width])
    d_bc_in = d_bc_rows[HALO:].at[rows - HALO :].add(edge_back[:, x_width:])
    d_z_b = out_grads[0].astype(jnp.bfloat16)
    d_x_b = d_x_in.astype(jnp.bfloat16)
    d_dt_b = d_dt_in.astype(jnp.bfloat16)
    head_pick = (jnp.arange(KVH, dtype=jnp.int32) == kv_head).astype(jnp.float32)
    d_kv_part = jnp.concatenate(
        [head_pick[k] * part for part in (d_key_own, d_value_own) for k in range(KVH)], axis=1
    )
    full_z, full_x, full_bc, full_q, full_kv, full_dt = split_columns(full_first, widths[:6])
    d_normed_part = (
        times(jnp.concatenate([d_z_b, d_x_b], axis=1), full_first[:, : widths[0] + x_width], 1, 1)
        + times(d_dt_b, full_dt, 1, 1)
        + times(d_q, full_q, 1, 1)
    )
    shared = jnp.concatenate([d_normed_part, d_bc_in, d_kv_part], axis=1)
    conv_rows = jnp.pad(
        grad_conv_bc, ((0, 2 * HALO - CONVK), (0, shared.shape[1] - grad_conv_bc.shape[1]))
    )
    shared = wa_total(jnp.concatenate([shared, conv_rows], axis=0), 3, 5)
    d_normed_sum = shared[:rows, :width]
    d_bckv_b = shared[:rows, width:].astype(jnp.bfloat16)
    grad_conv_bc = shared[rows : rows + CONVK, : grad_conv_bc.shape[1]]
    d_bc_b = d_bckv_b[:, : widths[2]]
    d_kv_b = d_bckv_b[:, widths[2] :]
    d_normed = d_normed_sum + times(d_bc_b, full_bc, 1, 1) + times(d_kv_b, full_kv, 1, 1)
    tokens_hat = tokens_wide * scale_mix
    weighted_mix = d_normed * gain_mix
    grad_tokens = d_hidden + scale_mix * (
        weighted_mix - tokens_hat * jnp.mean(weighted_mix * tokens_hat, axis=-1, keepdims=True)
    )
    grad_gain_mix = jnp.sum(d_normed * tokens_hat, axis=0)
    own_width = ffn_own.shape[1]
    hidden_own = lax.dynamic_slice_in_dim(hidden, wa_index * own_width, own_width, 1)
    output = (hidden_own + ffn_own).astype(jnp.bfloat16)
    d_first = pack_columns([d_z_b, d_x_b, d_bc_b, d_q, d_kv_b, d_dt_b])
    small = (
        grad_gain_mix,
        grad_gain_ffn,
        grad_conv_x.reshape(-1),
        grad_conv_bc.reshape(-1),
        grad_dt_bias,
        grad_a_log,
        out_grads[6],
    )
    flat = jnp.concatenate(small)
    small_rows = 8 * (-(-flat.shape[0] // (8 * LANES)))
    flat = jnp.pad(flat, (0, small_rows * LANES - flat.shape[0])).reshape(small_rows, LANES)

    def blocks_of(left_side, right_side):
        product = times(left_side, right_side, 0, 0).astype(SUM_TYPE)
        return product.reshape(seq_count, product.shape[0] // seq_count, product.shape[1])

    own_first, own_mixed, own_ffn, own_down, small_sum = ring_scatter(
        [
            blocks_of(normed, d_first),
            blocks_of(d_hidden_b, mixed),
            blocks_of(hnormed, d_ffn),
            blocks_of(cotangent, activated),
        ],
        6,
        flat,
    )
    small_sum = small_sum.reshape(-1)
    grads = (
        split_columns(own_first, widths[:6])
        + split_columns(own_ffn, widths[6:8])
        + split_columns(own_mixed, widths[8:10])
        + [own_down]
    )
    sums, at = ([], 0)
    for piece in small:
        sums.append(small_sum[at : at + piece.shape[0]])
        at += piece.shape[0]
    return (
        output,
        grad_tokens,
        sums[0],
        grads[0],
        grads[1],
        grads[2],
        grads[5],
        sums[2].reshape(conv_x.shape),
        sums[3].reshape(conv_bc.shape),
        sums[4],
        sums[5],
        sums[6],
        grads[8].T,
        grads[3],
        grads[4],
        grads[9].T,
        sums[1],
        grads[6],
        grads[7],
        grads[10].T,
    )


def solution(mesh):
    placed = (
        P("seq", None),
        P(),
        P("seq", "wa"),
        P("seq", "wa"),
        P("seq", None),
        P("seq", "wa"),
        P(None, "wa"),
        P(),
        P("wa"),
        P("wa"),
        P("wa"),
        P("wa", "seq"),
        P("seq", "wa"),
        P("seq", None),
        P("wa", "seq"),
        P(),
        P("seq", "wa"),
        P("seq", "wa"),
        P("wa", "seq"),
        P("seq", None),
    )
    return jax.shard_map(
        per_device,
        mesh=mesh,
        in_specs=placed,
        out_specs=(
            P("seq", "wa"),
            P("seq", None),
            P(),
            P("seq", "wa"),
            P("seq", "wa"),
            P("seq", None),
            P("seq", "wa"),
            P(None, "wa"),
            P(),
            P("wa"),
            P("wa"),
            P("wa"),
            P("wa", "seq"),
            P("seq", "wa"),
            P("seq", None),
            P("wa", "seq"),
            P(),
            P("seq", "wa"),
            P("seq", "wa"),
            P("wa", "seq"),
        ),
        check_vma=False,
    )
```

```python
import functools
import types

import jax
import jax.numpy as jnp
from jax import lax
from jax.experimental import pallas as pl
from jax.experimental.pallas import tpu as pltpu
from jax.sharding import PartitionSpec as P

NS = 128
CONVK = 4
QH = 8
KVH = 2
HD = 64
SH = 64
HALO = 16
LANES = 128
EPS = 1e-05
ROPE_BASE = 100000000000.0
MASKED = -1e30
SUM_TYPE = jnp.bfloat16
MESH = pl.DeviceIdType.MESH
VMEM_LIMIT = 62 * 1024 * 1024
EDGE = CONVK - 1
f32 = jnp.float32
bf16 = jnp.bfloat16
highest = lax.Precision.HIGHEST

GATHERED = ("zx", "rest", "mixed", "ffn", "down", "kv", "state")
SCATTERED = ("zx", "rest", "mixed", "ffn", "down", "kv", "state")


def rope_tables(positions):
    frequency = ROPE_BASE ** (-(jnp.arange(HD // 2, dtype=f32) * 2.0 / HD))
    angles = positions.astype(f32)[:, None] * frequency[None, :]
    return (jnp.cos(angles), jnp.sin(angles))


def ring_place(index, count):
    odd = lax.rem(index, 2)
    half = lax.div(index, 2)
    return (1 - odd) * half + odd * (count - 1 - half)


def ring_index(place, count):
    place = lax.rem(place + 2 * count, count)
    upper = lax.div(place, count // 2)
    return (1 - upper) * 2 * place + upper * (2 * (count - place) - 1)


def dot(left, right, left_dim=1, right_dim=0, precision=None):
    return lax.dot_general(
        left,
        right,
        (((left_dim,), (right_dim,)), ((), ())),
        precision=precision,
        preferred_element_type=f32,
    )


def remote(source, target, send, receive, peer):
    return pltpu.make_async_remote_copy(
        src_ref=source,
        dst_ref=target,
        send_sem=send,
        recv_sem=receive,
        device_id=peer,
        device_id_type=MESH,
    )


def sigmoid(values):
    return 1.0 / (1.0 + jnp.exp(-values))


def softplus(values):
    return jnp.maximum(values, 0.0) + jnp.log1p(jnp.exp(-jnp.abs(values)))


def rms_scale(rows):
    return lax.rsqrt(jnp.mean(rows * rows, axis=-1, keepdims=True) + EPS)


def lanes_of(shape):
    return lax.broadcasted_iota(jnp.int32, shape, 1)


def swapped(values):
    lane = lax.rem(lanes_of(values.shape), HD)
    ahead = pltpu.roll(values, LANES - HD // 2, 1)
    behind = pltpu.roll(values, HD // 2, 1)
    return jnp.where(lane < HD // 2, ahead, behind)


def half_turned(values):
    return pltpu.roll(values, HD, 1)


class Ring:
    def __init__(self, count, bufs, parts, slots, halves, holds, sems):
        self.count = count
        self.steps = count // 2
        self.seq = lax.axis_index("seq")
        self.place = ring_place(self.seq, count)
        self.sides = [
            {"seq": ring_index(self.place + 1, count)},
            {"seq": ring_index(self.place - 1, count)},
        ]
        self.bufs, self.parts, self.slots = bufs, parts, slots
        self.halves, self.holds = halves, holds
        self.gather_send, self.gather_receive, self.send, self.receive = sems

    def owner(self, offset):
        return ring_index(self.place + offset, self.count)

    def gather_copy(self, name, side, step, arriving):
        c = GATHERED.index(name)
        back = step + 1 if arriving else step
        owner = self.owner(back if side else -back)
        buf = self.bufs[name]
        if step < self.steps - 1:
            piece = buf.at[owner]
        else:
            rows = buf.shape[1] // 2
            piece = buf.at[owner, pl.ds(side * rows, rows)]
        return remote(
            piece,
            piece,
            self.gather_send.at[c, side, step],
            self.gather_receive.at[c, side, step],
            self.sides[side],
        )

    def gather_step(self, name, step):
        for side in range(2):
            if step:
                self.gather_copy(name, side, step - 1, True).wait_recv()
            self.gather_copy(name, side, step, False).start()

    def gather_rest(self, name, first):
        for step in range(first, self.steps):
            self.gather_step(name, step)

    def gather_end(self, name):
        for side in range(2):
            self.gather_copy(name, side, self.steps - 1, True).wait_recv()

    def gather_sent(self, name):
        for side in range(2):
            for step in range(self.steps):
                self.gather_copy(name, side, step, False).wait_send()

    def mine(self, name, side, step):
        rows = self.halves[name].shape[0]
        return self.parts[name].at[self.owner(-step if side else step), pl.ds(0, rows)]

    def slot(self, name, side, step):
        if step < self.steps:
            return self.slots[name].at[side, step - 1]
        rows = self.halves[name].shape[0] // 2
        return self.halves[name].at[pl.ds(side * rows, rows)]

    def scatter_copy(self, name, side, step):
        c = SCATTERED.index(name)
        if step == self.steps:
            rows = self.halves[name].shape[0] // 2
            origin = self.mine(name, side, step).at[pl.ds(side * rows, rows)]
        elif step == self.steps - 1:
            origin = self.holds[name].at[side]
        else:
            origin = self.slot(name, side, step + 1)
        return remote(
            origin,
            self.slot(name, side, step),
            self.send.at[c, side, step - 1],
            self.receive.at[c, side, step - 1],
            self.sides[side],
        )

    def scatter_step(self, name, turn):
        step = self.steps - turn
        rows = self.halves[name].shape[0] // 2
        for side in range(2):
            if turn:
                self.scatter_copy(name, side, step + 1).wait_recv()
                own = self.mine(name, side, step)
                slot = self.slot(name, side, step + 1)
                if turn == 1:
                    hold = self.holds[name].at[side]
                    near = pl.ds(side * rows, rows)
                    away = pl.ds((1 - side) * rows, rows)
                    hold[away, :] = own[away, :]
                    hold[near, :] = (own[near, :].astype(f32) + slot[...].astype(f32)).astype(
                        hold.dtype
                    )
                else:
                    slot[...] = (own[...].astype(f32) + slot[...].astype(f32)).astype(slot.dtype)
            self.scatter_copy(name, side, step).start()

    def scatter_rest(self, name, first):
        for turn in range(first, self.steps):
            self.scatter_step(name, turn)

    def scatter_end(self, name):
        for side in range(2):
            self.scatter_copy(name, side, 1).wait_recv()
        slots = self.slots[name]
        total = (
            self.parts[name][self.seq, pl.ds(0, self.halves[name].shape[0])].astype(f32)
            + slots[0, 0].astype(f32)
            + slots[1, 0].astype(f32)
        )
        return total

    def scatter_sent(self, name):
        for side in range(2):
            for step in range(1, self.steps + 1):
                self.scatter_copy(name, side, step).wait_send()


class Across:
    def __init__(self, value, out, near, far_send, far, send, receive, index, pieces):
        self.wa = lax.axis_index("wa")
        self.core = lax.rem(self.wa, 2)
        self.row = lax.div(self.wa, 2)
        self.mate = {"wa": 2 * self.row + 1 - self.core}
        self.across = {"wa": 2 * (1 - self.row) + self.core}
        self.value, self.out, self.near, self.far_send, self.far = value, out, near, far_send, far
        self.send, self.receive, self.index, self.pieces = send, receive, index, pieces
        self.rows = value.shape[0] // 2
        self.step = self.rows // pieces

    def half(self, core, p):
        return pl.ds(pl.multiple_of(core * self.rows + p * self.step, self.step), self.step)

    def sems(self, stage, p):
        return (self.send.at[self.index, stage, p], self.receive.at[self.index, stage, p])

    def first(self, p):
        at = pl.ds(p * self.step, self.step)
        return remote(
            self.value.at[self.half(1 - self.core, p)],
            self.near.at[at],
            *self.sems(0, p),
            self.mate,
        )

    def second(self, p):
        at = pl.ds(p * self.step, self.step)
        return remote(self.far_send.at[at], self.far.at[at], *self.sems(1, p), self.across)

    def third(self, p, arriving):
        at = self.half(1 - self.core if arriving else self.core, p)
        return remote(self.out.at[at], self.out.at[at], *self.sems(2, p), self.mate)

    def begin(self):
        for p in range(self.pieces):
            self.first(p).start()

    def middle(self):
        for p in range(self.pieces):
            self.first(p).wait_recv()
            at = pl.ds(p * self.step, self.step)
            own = self.half(self.core, p)
            self.far_send[at, :] = (self.value[own, :] + self.near[at, :]).astype(SUM_TYPE)
            self.second(p).start()

    def finish(self):
        for p in range(self.pieces):
            self.second(p).wait_recv()
            at = pl.ds(p * self.step, self.step)
            own = self.half(self.core, p)
            self.out[own, :] = self.far_send[at, :].astype(f32) + self.far[at, :].astype(f32)
            self.third(p, False).start()

    def arrived(self):
        for p in range(self.pieces):
            self.third(p, True).wait_recv()

    def sent(self):
        for p in range(self.pieces):
            self.first(p).wait_send()
            self.second(p).wait_send()
            self.third(p, False).wait_send()


SMALL_ROWS = 40


def layer_kernel(count, names, *refs):
    r = types.SimpleNamespace(**dict(zip(names, refs)))
    seq = lax.axis_index("seq")
    wa = lax.axis_index("wa")
    rows, width = r.tokens.shape
    inner = r.w_z.shape[1]
    heads = inner // SH
    pairs = heads // 2
    lane_h = lanes_of((rows, LANES))
    low_half = lane_h < HD
    kv_head = lax.div(wa * (r.w_q.shape[1] // HD), QH // KVH)

    def family(prefix):
        return {name: getattr(r, prefix + name) for name in GATHERED}

    r.p_kv, r.p_state = r.f_kv, r.f_state

    ring = Ring(
        count,
        *(family(prefix) for prefix in ("f_", "p_", "s_", "e_", "h_")),
        (r.gather_send, r.gather_receive, r.scatter_send, r.scatter_receive),
    )
    hidden_sum = Across(r.part1, r.total1, r.near1, r.fars1, r.far1, r.wa_send, r.wa_receive, 0, 4)
    hnormed_sum = Across(r.part1, r.total1, r.near1, r.fars1, r.far2, r.wa_send, r.wa_receive, 1, 4)
    shared_sum = Across(r.part3, r.total3, r.near3, r.fars3, r.far3, r.wa_send, r.wa_receive, 2, 3)
    mate, across = hidden_sum.mate, hidden_sum.across
    core, row = hidden_sum.core, hidden_sum.row
    others = [{"seq": lax.rem(seq + offset, count)} for offset in range(1, count)]
    following, preceding = others[0], others[-1]
    barrier = pltpu.get_barrier_semaphore()
    peers = others + [mate, across]
    for peer in peers:
        pl.semaphore_signal(barrier, inc=1, device_id=peer, device_id_type=MESH)

    r.f_zx[seq] = jnp.concatenate([r.w_z[...], r.w_x[...]], axis=1)
    r.f_rest[seq] = jnp.concatenate([r.w_bc[...], r.w_q[...], r.w_kv[...], r.w_dt[...]], axis=1)
    pl.semaphore_wait(barrier, len(peers))
    halo = remote(
        r.tokens.at[pl.ds(rows - HALO, HALO)], r.halo, r.edge_sems.at[0], r.edge_sems.at[1], following
    )
    halo.start()
    ring.gather_step("rest", 0)
    ring.gather_step("zx", 0)
    depth = r.w_out.shape[1]
    eye = (
        lax.broadcasted_iota(jnp.int32, (depth, depth), 0) == lanes_of((depth, depth))
    ).astype(bf16)
    r.f_mixed[seq] = jnp.concatenate(
        [dot(eye, r.w_out[...], 1, 1).astype(bf16), dot(eye, r.w_o[...], 1, 1).astype(bf16)], axis=1
    )
    r.f_down[seq] = dot(eye, r.w_down[...], 1, 1).astype(bf16)
    r.f_ffn[seq] = jnp.concatenate([r.w_gate[...], r.w_up[...]], axis=1)
    tokens_wide = r.tokens[...].astype(f32)
    scale_mix = rms_scale(tokens_wide)
    r.normed[pl.ds(HALO, rows), :] = (tokens_wide * scale_mix * r.gain_mix[...]).astype(bf16)
    halo.wait_recv()
    before = jnp.where(seq > 0, r.halo[...].astype(f32), 0.0)
    r.normed[pl.ds(0, HALO), :] = (before * rms_scale(before) * r.gain_mix[...]).astype(bf16)
    for step in range(1, ring.steps):
        ring.gather_step("rest", step)
        ring.gather_step("zx", step)
    for name in ("mixed", "ffn", "down"):
        ring.gather_step(name, 0)

    bc_width = r.conv_bc.shape[1]
    ring.gather_end("rest")
    flat = (width, r.f_rest.shape[2])
    rest = dot(r.normed[...], r.f_rest[...].reshape(flat))
    r.bc_rows[...] = rest[:, :bc_width]
    q_at = bc_width
    kv_at = q_at + LANES
    dt_at = kv_at + 2 * LANES
    cosine, sine = r.cosine[...], r.sine[...]

    def turned(values):
        return values * cosine + swapped(values) * sine

    def unturned(values):
        return values * cosine - swapped(values) * sine

    q_rot = (turned(rest[HALO:, q_at:kv_at]) * HD ** (-0.5)).astype(bf16).astype(f32)
    r.q_pad[pl.ds(0, rows), :] = jnp.where(low_half, q_rot, 0.0).astype(bf16)
    r.q_pad[pl.ds(rows, rows), :] = jnp.where(low_half, half_turned(q_rot), 0.0).astype(bf16)
    keys = turned(rest[HALO:, kv_at : kv_at + LANES])
    values = rest[HALO:, kv_at + LANES : dt_at]
    first_head = kv_head == 0
    r.f_kv[seq] = jnp.where(
        low_half,
        jnp.where(first_head, keys, half_turned(keys)),
        jnp.where(first_head, half_turned(values), values),
    ).astype(bf16)
    ring.gather_step("kv", 0)
    r.dt_in[...] = rest[HALO:, dt_at:]
    ring.gather_end("zx")
    zx = dot(r.normed[...], r.f_zx[...].reshape(width, 2 * inner))
    r.z_proj[...] = zx[HALO:, :inner]
    r.x_rows[...] = zx[:, inner:]

    def convolved(source, taps):
        running = taps[0:1, :] * source[pl.ds(HALO - EDGE, rows), :]
        for k in range(1, CONVK):
            running = running + taps[k : k + 1, :] * source[pl.ds(HALO - EDGE + k, rows), :]
        return running

    x_pre = convolved(r.x_rows, r.conv_x[...])
    bc_pre = convolved(r.bc_rows, r.conv_bc[...])
    r.x_pre[...] = x_pre
    r.bc_pre[...] = bc_pre
    x_conv = x_pre * sigmoid(x_pre)
    r.x_conv[...] = x_conv
    bc_conv = bc_pre * sigmoid(bc_pre)
    r.b_mat[...] = bc_conv[:, :NS].astype(bf16)
    r.c_mat[...] = bc_conv[:, NS:].astype(bf16)
    rate = -jnp.exp(r.head_rows[1:2, :])
    step_size = softplus(r.dt_in[...] + r.head_rows[0:1, :])
    r.step_size[...] = step_size
    tick_t = lax.broadcasted_iota(jnp.int32, (rows, rows), 0)
    tick_s = lanes_of((rows, rows))
    causal = tick_t >= tick_s
    cumulative = dot(causal.astype(f32), rate * step_size, precision=highest)
    r.cumulative[...] = cumulative
    r.cum_t[...] = cumulative.T
    r.step_t[...] = step_size.T
    pick_row = lax.broadcasted_iota(jnp.int32, (LANES, inner), 0)
    pick_lane = lax.div(lanes_of((LANES, inner)), SH)
    pick = (pick_row == pick_lane).astype(f32)

    def spread(per_head):
        return dot(per_head, pick, precision=highest)

    def head_sums(wide):
        return dot(wide, pick, 1, 1, precision=highest)

    last = cumulative[rows - 1 : rows, :]
    tail_decay = jnp.exp(last - cumulative)
    tail = spread(tail_decay * step_size)
    r.tail[...] = tail
    x_tail = (x_conv * tail).astype(bf16)
    r.x_tail[...] = x_tail
    local_state = dot(x_tail, r.b_mat[...], 0, 0)
    high = last.astype(bf16).astype(f32)
    middle = (last - high).astype(bf16).astype(f32)
    low = last - high - middle
    row_of = lax.broadcasted_iota(jnp.int32, (2 * HALO, LANES), 0)
    split_rows = jnp.where(
        row_of == 0, high, jnp.where(row_of == 1, middle, jnp.where(row_of == 2, low, 0.0))
    )
    r.f_state[seq, pl.ds(0, inner), :] = local_state.astype(bf16)
    r.f_state[seq, pl.ds(inner, 2 * HALO), :] = split_rows.astype(bf16)
    ring.gather_step("state", 0)
    for step in range(1, ring.steps):
        ring.gather_step("kv", step)
        ring.gather_step("state", step)
        if step < 3:
            for name in ("mixed", "ffn", "down"):
                ring.gather_step(name, step)

    overlap = dot(r.c_mat[...], r.b_mat[...], 1, 1)
    x_bf = x_conv.astype(bf16)
    r.x_bf[...] = x_bf

    def decays(h):
        gap = r.cumulative[:, h : h + 1] - r.cum_t[h : h + 1, :]
        return jnp.exp(jnp.where(causal, gap, MASKED))

    for p in range(pairs):
        at = pl.ds(p * LANES, LANES)
        outs = []
        for h in (2 * p, 2 * p + 1):
            mixing = (decays(h) * overlap * r.step_t[h : h + 1, :]).astype(bf16)
            r.mixing[h] = mixing
            outs.append(dot(mixing, r.x_bf[:, at]))
        r.ssm[:, at] = jnp.where(low_half, outs[0], outs[1])

    ring.gather_end("kv")

    def block_scores(block):
        scores = dot(r.q_pad[...], r.f_kv[block], 1, 1)
        shape = (2 * rows, rows)
        query = seq * rows + lax.rem(lax.broadcasted_iota(jnp.int32, shape, 0), rows)
        key = block * rows + lanes_of(shape)
        return jnp.where(key <= query, scores, MASKED)

    r.row_max[...] = jnp.full_like(r.row_max, MASKED)
    r.row_sum[...] = jnp.zeros_like(r.row_sum)
    r.attn_acc[...] = jnp.zeros_like(r.attn_acc)

    def visit(block, carry):
        scores = block_scores(block)
        old = r.row_max[...]
        new = jnp.maximum(old, jnp.max(scores, axis=1, keepdims=True))
        weights = jnp.exp(scores - new)
        shrink = jnp.exp(old - new)
        r.row_sum[...] = r.row_sum[...] * shrink + jnp.sum(weights, axis=1, keepdims=True)
        r.attn_acc[...] = r.attn_acc[...] * shrink + dot(weights.astype(bf16), r.f_kv[block])
        r.row_max[...] = new
        return carry

    lax.fori_loop(0, seq + 1, visit, 0)
    attn = r.attn_acc[...] / r.row_sum[...]
    r.row_max[...] = r.row_max[...] + jnp.log(r.row_sum[...])
    attn_out = jnp.where(low_half, half_turned(attn[:rows]), attn[rows:])
    r.mixed[:, pl.ds(inner, LANES)] = attn_out.astype(bf16)

    ring.gather_end("state")
    reach = jnp.zeros((1, LANES), f32)
    for block in range(count - 1, -1, -1):
        earlier = block < seq
        r.factors[block : block + 1, :] = jnp.where(earlier, jnp.exp(reach), 0.0)
        totals = jnp.sum(
            r.f_state[block, pl.ds(inner, HALO), :].astype(f32), axis=0, keepdims=True
        )
        reach = reach + jnp.where(earlier, totals, 0.0)
    r.start_state[...] = jnp.zeros_like(r.start_state)

    def tall(per_head_row):
        return jnp.concatenate(
            [jnp.broadcast_to(per_head_row[:, h : h + 1], (SH, NS)) for h in range(heads)], axis=0
        )

    def add_state(block, carry):
        factor = tall(r.factors[pl.ds(block, 1), :])
        r.start_state[...] = r.start_state[...] + factor * r.f_state[
            block, pl.ds(0, inner), :
        ].astype(f32)
        return carry

    lax.fori_loop(0, seq, add_state, 0)
    start_b = r.start_state[...].astype(bf16)
    reached = dot(r.c_mat[...], start_b, 1, 1)
    grown = spread(jnp.exp(r.cumulative[...]))
    r.grown[...] = grown
    carried = reached * grown
    r.carried[...] = carried
    ssm = r.ssm[...] + carried + r.skip_row[...] * r.x_conv[...]
    r.ssm[...] = ssm
    z_proj = r.z_proj[...]
    r.mixed[:, pl.ds(0, inner)] = (ssm * (z_proj * sigmoid(z_proj))).astype(bf16)

    for name in ("mixed", "ffn", "down"):
        ring.gather_rest(name, min(3, ring.steps))
    ring.gather_end("mixed")
    mixed_shape = (width, r.f_mixed.shape[2])
    r.part1[...] = dot(r.mixed[...], r.f_mixed[...].reshape(mixed_shape), 1, 1)
    hidden_sum.begin()
    ring.gather_end("down")
    down_shape = (width, r.f_down.shape[2])
    hidden_sum.middle()
    d_act = dot(r.cotangent[...], r.f_down[...].reshape(down_shape))
    r.d_act[...] = d_act
    hidden_sum.finish()
    ring.gather_end("ffn")
    ffn_shape = (width, r.f_ffn.shape[2])
    ffn_width = r.f_down.shape[2]
    hidden_sum.arrived()

    hidden_sum.sent()

    hidden = r.tokens[...].astype(f32) + r.total1[...]
    r.hidden[...] = hidden
    scale_ffn = rms_scale(hidden)
    r.hnormed[...] = (hidden * scale_ffn * r.gain_ffn[...]).astype(bf16)
    gate_up = dot(r.hnormed[...], r.f_ffn[...].reshape(ffn_shape))
    gate, up = gate_up[:, :ffn_width], gate_up[:, ffn_width:]
    open_gate = sigmoid(gate)
    d_act = r.d_act[...]
    r.d_ffn[:, pl.ds(0, ffn_width)] = (
        d_act * up * open_gate * (1.0 + gate * (1.0 - open_gate))
    ).astype(bf16)
    r.d_ffn[:, pl.ds(ffn_width, ffn_width)] = (d_act * gate * open_gate).astype(bf16)
    r.activated[...] = (gate * open_gate * up).astype(bf16)
    r.part1[...] = dot(r.d_ffn[...], r.f_ffn[...].reshape(ffn_shape), 1, 1)
    hnormed_sum.begin()
    r.ffn_part[...] = dot(r.activated[...], r.f_down[...].reshape(down_shape), 1, 1)
    own_width = width // 4
    part_first = []
    for other_row in range(2):
        columns = pl.ds(pl.multiple_of((2 * other_row + 1 - core) * own_width, LANES), own_width)
        copy = remote(
            r.ffn_part.at[:, columns],
            r.ffn_near.at[other_row],
            r.ffn_sems.at[0, other_row],
            r.ffn_sems.at[1, other_row],
            mate,
        )
        copy.start()
        part_first.append(copy)
    hnormed_sum.middle()

    def fill(name, left, right):
        shape = getattr(r, "p_" + name).shape
        getattr(r, "p_" + name)[...] = dot(left, right, 0, 0).astype(SUM_TYPE).reshape(shape)

    fill("down", r.cotangent[...], r.activated[...])
    ring.scatter_step("down", 0)
    hnormed_sum.finish()
    for copy in part_first:
        copy.wait_recv()
    theirs = pl.ds(pl.multiple_of((2 * (1 - row) + core) * own_width, LANES), own_width)
    kept = pl.ds(pl.multiple_of((2 * row + core) * own_width, LANES), own_width)
    r.ffn_send[...] = (r.ffn_part[:, theirs] + r.ffn_near[1 - row]).astype(SUM_TYPE)
    part_second = remote(r.ffn_send, r.ffn_far, r.ffn_sems.at[0, 2], r.ffn_sems.at[1, 2], across)
    part_second.start()
    fill("ffn", r.hnormed[...], r.d_ffn[...])
    ring.scatter_step("ffn", 0)
    hnormed_sum.arrived()

    hidden = r.hidden[...]
    scale_ffn = rms_scale(hidden)
    hidden_hat = hidden * scale_ffn
    d_hnormed = r.total1[...]
    weighted = d_hnormed * r.gain_ffn[...]
    d_hidden = r.cotangent[...].astype(f32) + scale_ffn * (
        weighted - hidden_hat * jnp.mean(weighted * hidden_hat, axis=-1, keepdims=True)
    )
    r.d_hidden[...] = d_hidden
    r.d_hidden_b[...] = d_hidden.astype(bf16)
    gain_ffn_grad = jnp.sum(d_hnormed * hidden_hat, axis=0, keepdims=True)
    chunks = width // LANES
    for k in range(chunks):
        r.small[chunks + k : chunks + k + 1, :] = gain_ffn_grad[:, k * LANES : (k + 1) * LANES]
    d_mixed = dot(r.d_hidden_b[...], r.f_mixed[...].reshape(mixed_shape))
    d_gated = d_mixed[:, :inner]
    d_attn = d_mixed[:, inner:].astype(bf16).astype(f32)

    r.do_pad[pl.ds(0, rows), :] = jnp.where(low_half, 0.0, half_turned(d_attn)).astype(bf16)
    r.do_pad[pl.ds(rows, rows), :] = jnp.where(low_half, 0.0, d_attn).astype(bf16)
    attn_b = r.mixed[:, pl.ds(inner, LANES)].astype(f32)
    products = d_attn * attn_b
    r.delta[pl.ds(0, rows), :] = jnp.sum(jnp.where(low_half, products, 0.0), axis=1, keepdims=True)
    r.delta[pl.ds(rows, rows), :] = jnp.sum(
        jnp.where(low_half, 0.0, products), axis=1, keepdims=True
    )
    r.attn_acc[...] = jnp.zeros_like(r.attn_acc)
    own_state = pl.ds(0, inner)
    for name in ("kv", "state"):
        ring.gather_sent(name)

    def revisit(block, carry):
        probability = jnp.exp(block_scores(block) - r.row_max[...])
        keys_values = r.f_kv[block]
        d_probs = dot(r.do_pad[...], keys_values, 1, 1)
        d_scores = (probability * (d_probs - r.delta[...])).astype(bf16)
        r.attn_acc[...] = r.attn_acc[...] + dot(d_scores, keys_values)
        r.p_kv[block] = (
            dot(d_scores, r.q_pad[...], 0, 0)
            + dot(probability.astype(bf16), r.do_pad[...], 0, 0)
        ).astype(SUM_TYPE)
        return carry

    def blank(block, carry):
        r.p_kv[block] = jnp.zeros_like(r.p_kv[block])
        r.p_state[block, own_state, :] = jnp.zeros((inner, LANES), SUM_TYPE)
        return carry

    lax.fori_loop(0, seq + 1, revisit, 0)
    lax.fori_loop(seq + 1, count, blank, 0)
    r.p_state[seq, own_state, :] = jnp.zeros((inner, LANES), SUM_TYPE)
    ring.scatter_step("kv", 0)
    d_q = r.attn_acc[...] * HD ** (-0.5)
    d_q = jnp.where(low_half, d_q[:rows], half_turned(d_q[rows:]))
    r.d_rest[:, pl.ds(q_at, LANES)] = unturned(d_q).astype(bf16)

    z_proj = r.z_proj[...]
    open_z = sigmoid(z_proj)
    r.d_zx[:, pl.ds(0, inner)] = (
        d_gated * r.ssm[...] * open_z * (1.0 + z_proj * (1.0 - open_z))
    ).astype(bf16)
    d_ssm = d_gated * (z_proj * open_z)
    d_grown = d_ssm * r.grown[...]
    d_grown_b = d_grown.astype(bf16)
    direct = dot(d_grown_b, r.c_mat[...], 0, 0)
    r.direct[...] = direct

    def spread_state(block, carry):
        factor = tall(r.factors[pl.ds(block, 1), :])
        r.p_state[block, own_state, :] = (factor * r.direct[...]).astype(SUM_TYPE)
        return carry

    lax.fori_loop(0, seq, spread_state, 0)
    ring.scatter_step("state", 0)
    fill("mixed", r.d_hidden_b[...], r.mixed[...])
    ring.scatter_step("mixed", 0)
    ring.scatter_step("kv", 1)
    ring.scatter_step("state", 1)

    r.d_cum[...] = head_sums(d_ssm * r.carried[...])
    skip_sums = jnp.sum(d_ssm * r.x_conv[...], axis=0, keepdims=True)
    skip_grad = head_sums(skip_sums)
    r.d_c[...] = dot(d_grown_b, r.start_state[...].astype(bf16))
    d_ssm_b = d_ssm.astype(bf16)
    r.d_x[...] = r.skip_row[...] * d_ssm
    r.d_overlap[...] = jnp.zeros_like(r.d_overlap)
    r.d_rows[...] = jnp.zeros_like(r.d_rows)
    r.d_cum_rows[...] = jnp.zeros_like(r.d_cum_rows)
    overlap = dot(r.c_mat[...], r.b_mat[...], 1, 1)
    for p in range(pairs):
        at = pl.ds(p * LANES, LANES)
        x_pair = r.x_bf[:, at]
        d_pair = jnp.zeros((rows, LANES), f32)
        for h in (2 * p, 2 * p + 1):
            own = low_half if h == 2 * p else jnp.logical_not(low_half)
            d_head = jnp.where(own, d_ssm[:, p * LANES : (p + 1) * LANES], 0.0).astype(bf16)
            d_mixing = dot(d_head, x_pair, 1, 1) * decays(h)
            step_row = r.step_t[h : h + 1, :]
            weighted = d_mixing * overlap
            from_step = jnp.sum(weighted, axis=0, keepdims=True)
            r.d_rows[h : h + 1, :] = from_step
            r.d_cum_rows[h : h + 1, :] = -from_step * step_row
            row_total = jnp.sum(weighted * step_row, axis=1, keepdims=True)
            r.d_cum[...] = r.d_cum[...] + jnp.where(lane_h == h, row_total, 0.0)
            r.d_overlap[...] = r.d_overlap[...] + d_mixing * step_row
            d_pair = d_pair + dot(r.mixing[h], d_head, 0, 0)
        r.d_x[:, at] = r.d_x[:, at] + d_pair
        if p == 0:
            ring.scatter_step("down", 1)
            ring.scatter_step("ffn", 1)
    d_overlap_b = r.d_overlap[...].astype(bf16)
    r.d_c[...] = r.d_c[...] + dot(d_overlap_b, r.b_mat[...])
    r.d_b[...] = dot(d_overlap_b, r.c_mat[...], 0, 0)
    for turn in range(2, ring.steps):
        ring.scatter_step("kv", turn)
        ring.scatter_step("state", turn)
        if turn == 2:
            ring.scatter_step("mixed", 1)
            ring.scatter_step("down", 2)

    own_keys = ring.scatter_end("kv")
    unturned_keys = unturned(own_keys)
    zero = jnp.zeros((rows, LANES), f32)
    d_keys = jnp.where(low_half, unturned_keys, 0.0)
    d_values = jnp.where(low_half, 0.0, own_keys)
    d_keys = jnp.where(first_head, d_keys, half_turned(d_keys))
    d_values = jnp.where(first_head, half_turned(d_values), d_values)
    d_end = ring.scatter_end("state")
    d_end_b = d_end.astype(bf16)
    tail = r.tail[...]
    from_end = dot(r.b_mat[...], d_end_b, 1, 1)
    d_x = r.d_x[...] + from_end * tail
    d_tail = head_sums(from_end * r.x_conv[...])
    r.d_b[...] = r.d_b[...] + dot(r.x_tail[...], d_end_b)
    cumulative = r.cumulative[...]
    step_size = r.step_size[...]
    last = cumulative[rows - 1 : rows, :]
    tail_decay = jnp.exp(last - cumulative)
    through = d_tail * tail_decay * step_size
    held = jnp.sum(d_end * r.start_state[...], axis=1, keepdims=True)
    head_row = lax.broadcasted_iota(jnp.int32, (inner, LANES), 0)
    held_heads = jnp.sum(
        jnp.where(lax.div(head_row, SH) == lanes_of((inner, LANES)), held, 0.0),
        axis=0,
        keepdims=True,
    )
    d_last = jnp.sum(through, axis=0, keepdims=True) + jnp.exp(last) * held_heads
    tick_row = lax.broadcasted_iota(jnp.int32, (rows, LANES), 0)
    d_cum = r.d_cum[...] + r.d_cum_rows[...].T - through
    d_cum = d_cum + jnp.where(tick_row == rows - 1, d_last, 0.0)
    d_step = r.d_rows[...].T + d_tail * tail_decay
    rate = -jnp.exp(r.head_rows[1:2, :])
    upto = (tick_s >= tick_t).astype(f32)
    d_log_decay = dot(upto, d_cum, precision=highest)
    d_step = d_step + d_log_decay * rate
    d_dt = d_step * sigmoid(r.dt_in[...] + r.head_rows[0:1, :])
    d_dt = jnp.where(lane_h < heads, d_dt, 0.0)
    r.d_rest[:, pl.ds(dt_at, LANES)] = d_dt.astype(bf16)
    small_at = 2 * chunks + CONVK * (inner // LANES + bc_width // LANES)
    r.small[small_at : small_at + 1, :] = jnp.sum(d_dt, axis=0, keepdims=True)
    r.small[small_at + 1 : small_at + 2, :] = (
        jnp.sum(d_log_decay * step_size, axis=0, keepdims=True) * rate
    )
    r.small[small_at + 2 : small_at + 3, :] = skip_grad

    def silu_back(grad, pre):
        opened = sigmoid(pre)
        return grad * opened * (1.0 + pre * (1.0 - opened))

    pad = jnp.zeros((HALO, inner), f32)
    pad_bc = jnp.zeros((HALO, bc_width), f32)
    r.x_back[pl.ds(0, HALO), :] = pad
    r.x_back[pl.ds(HALO, rows), :] = silu_back(d_x, r.x_pre[...])
    r.x_back[pl.ds(HALO + rows, HALO), :] = pad
    d_bc = jnp.concatenate([r.d_b[...], r.d_c[...]], axis=1)
    r.bc_back[pl.ds(0, HALO), :] = pad_bc
    r.bc_back[pl.ds(HALO, rows), :] = silu_back(d_bc, r.bc_pre[...])
    r.bc_back[pl.ds(HALO + rows, HALO), :] = pad_bc

    def back(source, taps, start, length):
        running = taps[0:1, :] * source[pl.ds(start + EDGE, length), :]
        for k in range(1, CONVK):
            running = running + taps[k : k + 1, :] * source[pl.ds(start + EDGE - k, length), :]
        return running

    r.edge_out[:, pl.ds(0, inner)] = back(r.x_back, r.conv_x[...], 0, HALO)
    r.edge_out[:, pl.ds(inner, bc_width)] = back(r.bc_back, r.conv_bc[...], 0, HALO)
    edge = remote(r.edge_out, r.edge_in, r.edge_sems.at[2], r.edge_sems.at[3], preceding)
    edge.start()
    r.part3[pl.ds(rows, 2 * HALO), :] = jnp.zeros((2 * HALO, r.part3.shape[1]), f32)
    for k in range(CONVK):
        x_tap = jnp.sum(
            r.x_back[pl.ds(HALO, rows), :] * r.x_rows[pl.ds(HALO - EDGE + k, rows), :],
            axis=0,
            keepdims=True,
        )
        for m in range(inner // LANES):
            at = 2 * chunks + k * (inner // LANES) + m
            r.small[at : at + 1, :] = x_tap[:, m * LANES : (m + 1) * LANES]
        r.part3[rows + k : rows + k + 1, pl.ds(0, bc_width)] = jnp.sum(
            r.bc_back[pl.ds(HALO, rows), :] * r.bc_rows[pl.ds(HALO - EDGE + k, rows), :],
            axis=0,
            keepdims=True,
        )
    d_x_in = back(r.x_back, r.conv_x[...], HALO, rows)
    d_bc_in = back(r.bc_back, r.conv_bc[...], HALO, rows)
    edge.wait_recv()
    edges = jnp.where(seq < count - 1, r.edge_in[...], 0.0)
    above = rows - HALO
    r.d_zx[pl.ds(0, above), pl.ds(inner, inner)] = d_x_in[:above].astype(bf16)
    r.d_zx[pl.ds(above, HALO), pl.ds(inner, inner)] = (d_x_in[above:] + edges[:, :inner]).astype(
        bf16
    )
    r.part3[pl.ds(0, above), pl.ds(width, bc_width)] = d_bc_in[:above]
    r.part3[pl.ds(above, HALO), pl.ds(width, bc_width)] = d_bc_in[above:] + edges[:, inner:]
    r.part3[pl.ds(0, rows), pl.ds(width + bc_width, LANES)] = d_keys
    r.part3[pl.ds(0, rows), pl.ds(width + bc_width + LANES, LANES)] = d_values

    def rest_columns(start, wide):
        return r.f_rest[:, :, pl.ds(start, wide)].reshape(width, wide)

    r.part3[pl.ds(0, rows), pl.ds(0, width)] = (
        dot(r.d_zx[...], r.f_zx[...].reshape(width, 2 * inner), 1, 1)
        + dot(r.d_rest[:, pl.ds(q_at, LANES)], rest_columns(q_at, LANES), 1, 1)
        + dot(r.d_rest[:, pl.ds(dt_at, LANES)], rest_columns(dt_at, LANES), 1, 1)
    )
    shared_sum.begin()
    own_normed = pl.ds(HALO, rows)
    fill("zx", r.normed[own_normed, :], r.d_zx[...])
    ring.scatter_step("zx", 0)
    shared_sum.middle()
    for name in ("mixed", "ffn", "down"):
        ring.scatter_rest(name, {"mixed": 2, "ffn": 2, "down": 3}[name])
    shared_sum.finish()
    ring.scatter_step("zx", 1)
    shared_sum.arrived()
    r.d_rest[:, pl.ds(0, bc_width)] = r.total3[pl.ds(0, rows), pl.ds(width, bc_width)].astype(bf16)
    r.d_rest[:, pl.ds(kv_at, 2 * LANES)] = r.total3[
        pl.ds(0, rows), pl.ds(width + bc_width, 2 * LANES)
    ].astype(bf16)
    fill("rest", r.normed[own_normed, :], r.d_rest[...])
    ring.scatter_step("rest", 0)
    bc_taps = r.total3[pl.ds(rows, 2 * CONVK), pl.ds(0, bc_width)]
    for k in range(CONVK):
        for m in range(bc_width // LANES):
            at = 2 * chunks + CONVK * (inner // LANES) + k * (bc_width // LANES) + m
            r.small[at : at + 1, :] = bc_taps[k : k + 1, m * LANES : (m + 1) * LANES]
    d_normed = (
        r.total3[pl.ds(0, rows), pl.ds(0, width)]
        + dot(r.d_rest[:, pl.ds(0, bc_width)], rest_columns(0, bc_width), 1, 1)
        + dot(r.d_rest[:, pl.ds(kv_at, 2 * LANES)], rest_columns(kv_at, 2 * LANES), 1, 1)
    )
    tokens_wide = r.tokens[...].astype(f32)
    scale_mix = rms_scale(tokens_wide)
    tokens_hat = tokens_wide * scale_mix
    weighted = d_normed * r.gain_mix[...]
    r.grad_tokens[...] = r.d_hidden[...] + scale_mix * (
        weighted - tokens_hat * jnp.mean(weighted * tokens_hat, axis=-1, keepdims=True)
    )
    gain_mix_grad = jnp.sum(d_normed * tokens_hat, axis=0, keepdims=True)
    for k in range(chunks):
        r.small[k : k + 1, :] = gain_mix_grad[:, k * LANES : (k + 1) * LANES]
    used = small_at + 3
    r.small[used:SMALL_ROWS, :] = jnp.zeros((SMALL_ROWS - used, LANES), f32)
    small_copies = []
    for offset in range(1, count):
        copy = remote(
            r.small,
            r.small_slots.at[seq],
            r.small_send.at[offset - 1],
            r.small_receive.at[offset - 1],
            others[offset - 1],
        )
        copy.start()
        small_copies.append(copy)
    part_second.wait_recv()
    r.output[...] = (
        r.hidden[:, kept] + r.ffn_part[:, kept] + r.ffn_near[row] + r.ffn_far[...].astype(f32)
    ).astype(bf16)
    for name in ("mixed", "ffn", "down"):
        getattr(r, "g_" + name)[...] = ring.scatter_end(name)
    for step in range(2, ring.steps + 1):
        if step < ring.steps:
            ring.scatter_step("zx", step)
        ring.scatter_step("rest", step - 1)
    r.g_zx[...] = ring.scatter_end("zx")
    for copy in small_copies:
        copy.wait()
    r.small_slots[pl.ds(seq, 1)] = r.small[...][None]
    total = r.small_slots[0]
    for other in range(1, count):
        total = total + r.small_slots[other]
    r.small_sum[...] = total
    r.g_rest[...] = ring.scatter_end("rest")

    halo.wait_send()
    edge.wait_send()
    for copy in part_first:
        copy.wait_send()
    part_second.wait_send()
    for name in GATHERED[:5]:
        ring.gather_sent(name)
    for name in SCATTERED:
        ring.scatter_sent(name)
    for sums in (hnormed_sum, shared_sum):
        sums.sent()


def finish_kernel(*refs):
    g_zx, g_rest, g_mixed, g_ffn, g_down = refs[:5]
    z, x, bc, dt, out, q, kv, o, gate, up, down = refs[5:]
    inner = z.shape[1]
    at = 0
    for target, source in ((z, g_zx), (x, g_zx)):
        target[...] = source[:, pl.ds(at, inner)]
        at += inner
    at = 0
    for target in (bc, q, kv):
        target[...] = g_rest[:, pl.ds(at, target.shape[1])]
        at += target.shape[1]
    dt[...] = g_rest[:, pl.ds(at, LANES)][:, : dt.shape[1]]
    ffn_width = gate.shape[1]
    gate[...] = g_ffn[:, pl.ds(0, ffn_width)]
    up[...] = g_ffn[:, pl.ds(ffn_width, ffn_width)]
    out[...] = g_mixed[:, pl.ds(0, inner)].T
    o[...] = g_mixed[:, pl.ds(inner, LANES)].T
    down[...] = g_down[...].T


def per_device(
    tokens,
    gain_mix,
    w_z,
    w_x,
    w_bc,
    w_dt,
    conv_x,
    conv_bc,
    dt_bias,
    a_log,
    d_skip,
    w_out,
    w_q,
    w_kv,
    w_o,
    gain_ffn,
    w_gate,
    w_up,
    w_down,
    cotangent,
):
    count = lax.axis_size("seq")
    rows, width = tokens.shape
    depth = w_z.shape[0]
    inner = w_z.shape[1]
    heads = a_log.shape[0]
    ffn = w_gate.shape[1]
    bc_width = w_bc.shape[1]
    positions = lax.axis_index("seq") * rows + jnp.arange(rows, dtype=jnp.int32)
    cosine, sine = rope_tables(positions)
    head_rows = jnp.pad(jnp.stack([dt_bias, a_log]), ((0, 6), (0, LANES - heads)))
    inputs = dict(
        tokens=tokens,
        gain_mix=gain_mix[None],
        w_z=w_z,
        w_x=w_x,
        w_bc=w_bc,
        w_dt=jnp.pad(w_dt, ((0, 0), (0, LANES - heads))),
        conv_x=conv_x,
        conv_bc=conv_bc,
        head_rows=head_rows,
        skip_row=jnp.repeat(d_skip, SH)[None],
        w_out=w_out,
        w_q=w_q,
        w_kv=w_kv,
        w_o=w_o,
        gain_ffn=gain_ffn[None],
        w_gate=w_gate,
        w_up=w_up,
        w_down=w_down,
        cotangent=cotangent,
        cosine=jnp.concatenate([cosine] * 4, axis=1),
        sine=jnp.concatenate([-sine, sine] * 2, axis=1),
    )
    rest = bc_width + w_q.shape[1] + w_kv.shape[1] + LANES
    mixed = inner + w_o.shape[0]

    def shape(*dims, dtype=f32):
        return jax.ShapeDtypeStruct(dims, dtype)

    outputs = dict(
        output=shape(rows, width // 4, dtype=bf16),
        grad_tokens=shape(rows, width),
        small_sum=shape(SMALL_ROWS, LANES),
        g_zx=shape(depth, 2 * inner),
        g_rest=shape(depth, rest),
        g_mixed=shape(depth, mixed),
        g_ffn=shape(depth, 2 * ffn),
        g_down=shape(depth, ffn),
    )
    scratch = {}

    def room(name, *dims, dtype=f32):
        scratch[name] = pltpu.VMEM(dims, dtype)

    state_rows = inner + 2 * HALO
    for name, dims in dict(
        zx=(depth, 2 * inner),
        rest=(depth, rest),
        mixed=(depth, mixed),
        ffn=(depth, 2 * ffn),
        down=(depth, ffn),
        kv=(rows, LANES),
        state=(state_rows, LANES),
    ).items():
        room("f_" + name, count, *dims, dtype=bf16)
        if name == "state":
            dims = (inner, LANES)
        if name not in ("kv", "state"):
            room("p_" + name, count, *dims, dtype=SUM_TYPE)
        room("s_" + name, 2, count // 2 - 1, *dims, dtype=SUM_TYPE)
        room("e_" + name, *dims, dtype=SUM_TYPE)
        room("h_" + name, 2, *dims, dtype=SUM_TYPE)
    shared_rows, shared_width = rows + 2 * HALO, width + bc_width + 2 * LANES
    for k, tall_rows, wide in ((1, rows, width), (3, shared_rows, shared_width)):
        room(f"part{k}", tall_rows, wide)
        room(f"total{k}", tall_rows, wide)
        room(f"near{k}", tall_rows // 2, wide)
        room(f"fars{k}", tall_rows // 2, wide, dtype=SUM_TYPE)
        room(f"far{k}", tall_rows // 2, wide, dtype=SUM_TYPE)
    room("far2", rows // 2, width, dtype=SUM_TYPE)
    room("halo", HALO, width, dtype=bf16)
    room("normed", rows + HALO, width, dtype=bf16)
    room("bc_rows", rows + HALO, bc_width)
    room("x_rows", rows + HALO, inner)
    room("q_pad", 2 * rows, LANES, dtype=bf16)
    room("do_pad", 2 * rows, LANES, dtype=bf16)
    for name in ("dt_in", "step_size", "cumulative", "d_cum", "d_b", "d_c"):
        room(name, rows, LANES)
    for name in ("z_proj", "x_pre", "x_conv", "tail", "ssm", "grown", "carried", "d_x"):
        room(name, rows, inner)
    room("bc_pre", rows, bc_width)
    for name in ("b_mat", "c_mat"):
        room(name, rows, NS, dtype=bf16)
    for name in ("cum_t", "step_t", "d_rows", "d_cum_rows"):
        room(name, LANES, rows)
    for name in ("x_tail", "x_bf"):
        room(name, rows, inner, dtype=bf16)
    room("mixing", heads, rows, rows, dtype=bf16)
    room("d_overlap", rows, rows)
    for name in ("row_max", "row_sum", "delta"):
        room(name, 2 * rows, 1)
    room("attn_acc", 2 * rows, LANES)
    room("mixed", rows, mixed, dtype=bf16)
    room("factors", max(8, count), LANES)
    for name in ("start_state", "direct"):
        room(name, inner, NS)
    for name in ("hidden", "d_hidden", "ffn_part"):
        room(name, rows, width)
    for name in ("hnormed", "d_hidden_b"):
        room(name, rows, width, dtype=bf16)
    room("d_act", rows, ffn)
    room("d_ffn", rows, 2 * ffn, dtype=bf16)
    room("activated", rows, ffn, dtype=bf16)
    room("ffn_near", 2, rows, width // 4)
    room("ffn_send", rows, width // 4, dtype=SUM_TYPE)
    room("ffn_far", rows, width // 4, dtype=SUM_TYPE)
    room("d_zx", rows, 2 * inner, dtype=bf16)
    room("d_rest", rows, rest, dtype=bf16)
    room("x_back", rows + 2 * HALO, inner)
    room("bc_back", rows + 2 * HALO, bc_width)
    room("edge_out", HALO, inner + bc_width)
    room("edge_in", HALO, inner + bc_width)
    room("small", SMALL_ROWS, LANES)
    room("small_slots", count, SMALL_ROWS, LANES)
    sems = pltpu.SemaphoreType.DMA
    for name in ("gather_send", "gather_receive", "scatter_send", "scatter_receive"):
        scratch[name] = sems((len(GATHERED), 2, count // 2))
    for name in ("wa_send", "wa_receive"):
        scratch[name] = sems((3, 3, 4))
    scratch["edge_sems"] = sems((4,))
    scratch["ffn_sems"] = sems((2, 3))
    scratch["small_send"] = sems((count - 1,))
    scratch["small_receive"] = sems((count - 1,))
    vmem = pl.BlockSpec(memory_space=pltpu.VMEM)
    results = pl.pallas_call(
        functools.partial(layer_kernel, count, (*inputs, *outputs, *scratch)),
        out_shape=list(outputs.values()),
        in_specs=[vmem] * len(inputs),
        out_specs=[vmem] * len(outputs),
        scratch_shapes=list(scratch.values()),
        compiler_params=pltpu.CompilerParams(
            collective_id=0, has_side_effects=True, vmem_limit_bytes=VMEM_LIMIT
        ),
    )(*inputs.values())
    output, grad_tokens, small_sum = results[:3]
    placed = [w_z, w_x, w_bc, w_dt, w_out, w_q, w_kv, w_o, w_gate, w_up, w_down]
    grads = pl.pallas_call(
        finish_kernel,
        out_shape=[shape(*w.shape) for w in placed],
        in_specs=[vmem] * 5,
        out_specs=[vmem] * len(placed),
        compiler_params=pltpu.CompilerParams(vmem_limit_bytes=VMEM_LIMIT),
    )(*results[3:])
    g_z, g_x, g_bc, g_dt, g_out, g_q, g_kv, g_o, g_gate, g_up, g_down = grads
    chunks = width // LANES
    flat = small_sum.reshape(-1)
    conv_at = 2 * chunks
    bc_at = conv_at + CONVK * (inner // LANES)
    head_at = bc_at + CONVK * (bc_width // LANES)
    return (
        output,
        grad_tokens,
        flat[:width],
        g_z,
        g_x,
        g_bc,
        g_dt,
        flat[conv_at * LANES : bc_at * LANES].reshape(conv_x.shape),
        flat[bc_at * LANES : head_at * LANES].reshape(conv_bc.shape),
        small_sum[head_at, :heads],
        small_sum[head_at + 1, :heads],
        small_sum[head_at + 2, :heads],
        g_out,
        g_q,
        g_kv,
        g_o,
        flat[width : 2 * width],
        g_gate,
        g_up,
        g_down,
    )


def solution(mesh):
    placed = (
        P("seq", None),
        P(),
        P("seq", "wa"),
        P("seq", "wa"),
        P("seq", None),
        P("seq", "wa"),
        P(None, "wa"),
        P(),
        P("wa"),
        P("wa"),
        P("wa"),
        P("wa", "seq"),
        P("seq", "wa"),
        P("seq", None),
        P("wa", "seq"),
        P(),
        P("seq", "wa"),
        P("seq", "wa"),
        P("wa", "seq"),
        P("seq", None),
    )
    return jax.shard_map(
        per_device,
        mesh=mesh,
        in_specs=placed,
        out_specs=(
            P("seq", "wa"),
            P("seq", None),
            P(),
            P("seq", "wa"),
            P("seq", "wa"),
            P("seq", None),
            P("seq", "wa"),
            P(None, "wa"),
            P(),
            P("wa"),
            P("wa"),
            P("wa"),
            P("wa", "seq"),
            P("seq", "wa"),
            P("seq", None),
            P("wa", "seq"),
            P(),
            P("seq", "wa"),
            P("seq", "wa"),
            P("wa", "seq"),
        ),
        check_vma=False,
    )
```

```python
import functools
import types

import jax
import jax.numpy as jnp
import numpy as np
from jax import lax
from jax.experimental import pallas as pl
from jax.experimental.pallas import tpu as pltpu
from jax.sharding import PartitionSpec as P

NS = 128
CONVK = 4
QH = 8
KVH = 2
HD = 64
SH = 64
HALO = 16
LANES = 128
EPS = 1e-05
ROPE_BASE = 100000000000.0
MASKED = -1e30
SUM_TYPE = jnp.bfloat16
MESH = pl.DeviceIdType.MESH
VMEM_LIMIT = 62 * 1024 * 1024
EDGE = CONVK - 1
f32 = jnp.float32
bf16 = jnp.bfloat16
highest = lax.Precision.HIGHEST

ZX, REST, MIXED, FFN, DOWN, KV, STATE = GATHERED = (
    "zx",
    "rest",
    "mixed",
    "ffn",
    "down",
    "kv",
    "state",
)
SCATTERED = GATHERED


def ring_place(index, count):
    odd = lax.rem(index, 2)
    half = lax.div(index, 2)
    return (1 - odd) * half + odd * (count - 1 - half)


def ring_index(place, count):
    place = lax.rem(place + 2 * count, count)
    upper = lax.div(place, count // 2)
    return (1 - upper) * 2 * place + upper * (2 * (count - place) - 1)


def dot(left, right, left_dim=1, right_dim=0, precision=None):
    return lax.dot_general(
        left,
        right,
        (((left_dim,), (right_dim,)), ((), ())),
        precision=precision,
        preferred_element_type=f32,
    )


def remote(source, target, send, receive, peer):
    return pltpu.make_async_remote_copy(
        src_ref=source,
        dst_ref=target,
        send_sem=send,
        recv_sem=receive,
        device_id=peer,
        device_id_type=MESH,
    )


def sigmoid(values):
    return 1.0 / (1.0 + jnp.exp(-values))


def softplus(values):
    return jnp.maximum(values, 0.0) + jnp.log1p(jnp.exp(-jnp.abs(values)))


def rms_scale(rows):
    return lax.rsqrt(jnp.mean(rows * rows, axis=-1, keepdims=True) + EPS)


def lanes_of(shape):
    return lax.broadcasted_iota(jnp.int32, shape, 1)


def swapped(values):
    lane = lax.rem(lanes_of(values.shape), HD)
    ahead = pltpu.roll(values, LANES - HD // 2, 1)
    behind = pltpu.roll(values, HD // 2, 1)
    return jnp.where(lane < HD // 2, ahead, behind)


def half_turned(values):
    return pltpu.roll(values, HD, 1)


class Ring:
    def __init__(self, count, bufs, parts, slots, halves, holds, sems):
        self.count = count
        self.steps = count // 2
        self.seq = lax.axis_index("seq")
        self.place = ring_place(self.seq, count)
        self.sides = [
            {"seq": ring_index(self.place + 1, count)},
            {"seq": ring_index(self.place - 1, count)},
        ]
        self.bufs, self.parts, self.slots = bufs, parts, slots
        self.halves, self.holds = halves, holds
        self.gather_send, self.gather_receive, self.send, self.receive = sems

    def owner(self, offset):
        return ring_index(self.place + offset, self.count)

    def gather_copy(self, name, side, step, arriving):
        c = GATHERED.index(name)
        back = step + 1 if arriving else step
        owner = self.owner(back if side else -back)
        buf = self.bufs[name]
        if step < self.steps - 1:
            piece = buf.at[owner]
        else:
            rows = buf.shape[1] // 2
            piece = buf.at[owner, pl.ds(side * rows, rows)]
        return remote(
            piece,
            piece,
            self.gather_send.at[c, side, step],
            self.gather_receive.at[c, side, step],
            self.sides[side],
        )

    def gather_step(self, name, step):
        for side in range(2):
            if step:
                self.gather_copy(name, side, step - 1, True).wait_recv()
            self.gather_copy(name, side, step, False).start()

    def gather_rest(self, name, first):
        for step in range(first, self.steps):
            self.gather_step(name, step)

    def gather_end(self, name):
        for side in range(2):
            self.gather_copy(name, side, self.steps - 1, True).wait_recv()

    def gather_sent(self, name):
        for side in range(2):
            for step in range(self.steps):
                self.gather_copy(name, side, step, False).wait_send()

    def mine(self, name, side, step):
        rows = self.halves[name].shape[0]
        return self.parts[name].at[self.owner(-step if side else step), pl.ds(0, rows)]

    def slot(self, name, side, step):
        if step < self.steps:
            return self.slots[name].at[side, step - 1]
        rows = self.halves[name].shape[0] // 2
        return self.halves[name].at[pl.ds(side * rows, rows)]

    def scatter_copy(self, name, side, step):
        c = SCATTERED.index(name)
        if step == self.steps:
            rows = self.halves[name].shape[0] // 2
            origin = self.mine(name, side, step).at[pl.ds(side * rows, rows)]
        elif step == self.steps - 1:
            origin = self.holds[name].at[side]
        else:
            origin = self.slot(name, side, step + 1)
        return remote(
            origin,
            self.slot(name, side, step),
            self.send.at[c, side, step - 1],
            self.receive.at[c, side, step - 1],
            self.sides[side],
        )

    def scatter_step(self, name, turn):
        step = self.steps - turn
        rows = self.halves[name].shape[0] // 2
        for side in range(2):
            if turn:
                self.scatter_copy(name, side, step + 1).wait_recv()
                own = self.mine(name, side, step)
                slot = self.slot(name, side, step + 1)
                if turn == 1:
                    hold = self.holds[name].at[side]
                    near = pl.ds(side * rows, rows)
                    away = pl.ds((1 - side) * rows, rows)
                    hold[away, :] = own[away, :]
                    hold[near, :] = (own[near, :].astype(f32) + slot[...].astype(f32)).astype(
                        hold.dtype
                    )
                else:
                    slot[...] = (own[...].astype(f32) + slot[...].astype(f32)).astype(slot.dtype)
            self.scatter_copy(name, side, step).start()

    def scatter_rest(self, name, first):
        for turn in range(first, self.steps):
            self.scatter_step(name, turn)

    def scatter_end(self, name):
        for side in range(2):
            self.scatter_copy(name, side, 1).wait_recv()
        slots = self.slots[name]
        total = (
            self.parts[name][self.seq, pl.ds(0, self.halves[name].shape[0])].astype(f32)
            + slots[0, 0].astype(f32)
            + slots[1, 0].astype(f32)
        )
        return total

    def scatter_sent(self, name):
        for side in range(2):
            for step in range(1, self.steps + 1):
                self.scatter_copy(name, side, step).wait_send()


class Across:
    def __init__(self, value, out, near, far_send, far, send, receive, index, pieces):
        self.wa = lax.axis_index("wa")
        self.core = lax.rem(self.wa, 2)
        self.row = lax.div(self.wa, 2)
        self.mate = {"wa": 2 * self.row + 1 - self.core}
        self.across = {"wa": 2 * (1 - self.row) + self.core}
        self.value, self.out, self.near, self.far_send, self.far = value, out, near, far_send, far
        self.send, self.receive, self.index, self.pieces = send, receive, index, pieces
        self.rows = value.shape[0] // 2
        self.step = self.rows // pieces

    def half(self, core, p):
        return pl.ds(pl.multiple_of(core * self.rows + p * self.step, self.step), self.step)

    def sems(self, stage, p):
        return (self.send.at[self.index, stage, p], self.receive.at[self.index, stage, p])

    def first(self, p):
        at = pl.ds(p * self.step, self.step)
        return remote(
            self.value.at[self.half(1 - self.core, p)],
            self.near.at[at],
            *self.sems(0, p),
            self.mate,
        )

    def second(self, p):
        at = pl.ds(p * self.step, self.step)
        return remote(self.far_send.at[at], self.far.at[at], *self.sems(1, p), self.across)

    def third(self, p, arriving):
        at = self.half(1 - self.core if arriving else self.core, p)
        return remote(self.out.at[at], self.out.at[at], *self.sems(2, p), self.mate)

    def begin(self):
        for p in range(self.pieces):
            self.first(p).start()

    def middle(self):
        for p in range(self.pieces):
            self.first(p).wait_recv()
            at = pl.ds(p * self.step, self.step)
            own = self.half(self.core, p)
            self.far_send[at, :] = (self.value[own, :] + self.near[at, :]).astype(SUM_TYPE)
            self.second(p).start()

    def finish(self):
        for p in range(self.pieces):
            self.second(p).wait_recv()
            at = pl.ds(p * self.step, self.step)
            own = self.half(self.core, p)
            self.out[own, :] = self.far_send[at, :].astype(f32) + self.far[at, :].astype(f32)
            self.third(p, False).start()

    def arrived(self):
        for p in range(self.pieces):
            self.third(p, True).wait_recv()

    def sent(self):
        for p in range(self.pieces):
            self.first(p).wait_send()
            self.second(p).wait_send()
            self.third(p, False).wait_send()


class Split:
    def __init__(self, value, near, far_send, far, sems, wa):
        core, row = lax.rem(wa, 2), lax.div(wa, 2)
        mate, across = {"wa": 2 * row + 1 - core}, {"wa": 2 * (1 - row) + core}
        self.value, self.near, self.far_send, self.far, self.row = value, near, far_send, far, row
        wide = far.shape[1]

        def columns(block):
            return pl.ds(pl.multiple_of(block * wide, LANES), wide)

        self.kept, self.theirs = columns(2 * row + core), columns(2 * (1 - row) + core)
        self.firsts = [
            remote(
                value.at[:, columns(2 * k + 1 - core)], near.at[k], sems.at[0, k], sems.at[1, k], mate
            )
            for k in range(2)
        ]
        self.second = remote(far_send, far, sems.at[0, 2], sems.at[1, 2], across)

    def begin(self):
        for copy in self.firsts:
            copy.start()

    def middle(self):
        for copy in self.firsts:
            copy.wait_recv()
        self.far_send[...] = (self.value[:, self.theirs] + self.near[1 - self.row]).astype(SUM_TYPE)
        self.second.start()

    def result(self):
        self.second.wait_recv()
        return self.value[:, self.kept] + self.near[self.row] + self.far[...].astype(f32)

    def sent(self):
        for copy in self.firsts:
            copy.wait_send()
        self.second.wait_send()


class Share:
    def __init__(self, buf, sems, wa):
        core, row = lax.rem(wa, 2), lax.div(wa, 2)
        mate, across = 2 * row + 1 - core, 2 * (1 - row) + core

        def copy(block, k, peer):
            return remote(buf.at[block], buf.at[block], sems.at[0, k], sems.at[1, k], {"wa": peer})

        self.sends = [copy(wa, 0, across), copy(wa, 1, mate), copy(across, 2, mate)]
        self.arrivals = [
            copy(across, 0, across), copy(mate, 1, mate), copy(2 * (1 - row) + 1 - core, 2, mate)
        ]

    def begin(self):
        self.sends[0].start()
        self.sends[1].start()

    def forward(self):
        self.arrivals[0].wait_recv()
        self.sends[2].start()

    def arrived(self):
        self.arrivals[1].wait_recv()
        self.arrivals[2].wait_recv()

    def sent(self):
        for copy in self.sends:
            copy.wait_send()


SMALL_ROWS = 40


def layer_kernel(count, names, *refs):
    r = types.SimpleNamespace(**dict(zip(names, refs)))
    seq = lax.axis_index("seq")
    wa = lax.axis_index("wa")
    rows, width = r.tokens.shape
    inner = r.w_z.shape[1]
    heads = inner // SH
    pairs = heads // 2
    lane_h = lanes_of((rows, LANES))
    low_half = lane_h < HD
    kv_head = lax.div(wa * (r.w_q.shape[1] // HD), QH // KVH)

    def family(prefix):
        return {name: getattr(r, prefix + name) for name in GATHERED}

    r.p_kv, r.p_state = r.f_kv, r.f_state

    ring = Ring(
        count,
        *(family(prefix) for prefix in ("f_", "p_", "s_", "e_", "h_")),
        (r.gather_send, r.gather_receive, r.scatter_send, r.scatter_receive),
    )
    hidden_sum = Across(r.part1, r.total1, r.near1, r.fars1, r.far1, r.wa_send, r.wa_receive, 0, 4)
    hnormed_sum = Across(r.part1, r.total1, r.near1, r.fars1, r.far2, r.wa_send, r.wa_receive, 1, 4)
    shared_sum = Across(r.part3, r.total3, r.near3, r.fars3, r.far3, r.wa_send, r.wa_receive, 2, 3)
    mate, across = hidden_sum.mate, hidden_sum.across
    output_sum = Split(r.ffn_part, r.ffn_near, r.ffn_send, r.ffn_far, r.ffn_sems, wa)
    block_sum = Split(r.d_blocks, r.block_near, r.block_send, r.block_far, r.block_sems, wa)
    projected = Share(r.blocks, r.share_sems, wa)
    block_grads = Share(r.g_blocks, r.grad_sems, wa)
    others = [{"seq": lax.rem(seq + offset, count)} for offset in range(1, count)]
    following, preceding = others[0], others[-1]
    barrier = pltpu.get_barrier_semaphore()
    peers = others + [mate, across]
    for peer in peers:
        pl.semaphore_signal(barrier, inc=1, device_id=peer, device_id_type=MESH)

    r.f_zx[seq] = jnp.concatenate([r.w_z[...], r.w_x[...]], axis=1)
    own_columns = jnp.where(
        wa < 2,
        jnp.where(wa == 0, r.w_bc[:, pl.ds(0, LANES)], r.w_bc[:, pl.ds(LANES, LANES)]),
        jnp.where(wa == 2, r.w_kv[:, pl.ds(0, LANES)], r.w_kv[:, pl.ds(LANES, LANES)]),
    )
    r.f_rest[seq] = jnp.concatenate([r.w_q[...], own_columns, jnp.zeros_like(own_columns)], axis=1)
    r.f_rest[seq, :, pl.ds(2 * LANES, heads)] = r.w_dt[...]
    pl.semaphore_wait(barrier, len(peers))
    halo = remote(
        r.tokens.at[pl.ds(rows - HALO, HALO)], r.halo, r.edge_sems.at[0], r.edge_sems.at[1], following
    )
    halo.start()
    ring.gather_step(REST, 0)
    ring.gather_step(ZX, 0)
    depth = r.w_out.shape[1]
    eye = (
        lax.broadcasted_iota(jnp.int32, (depth, depth), 0) == lanes_of((depth, depth))
    ).astype(bf16)
    r.f_mixed[seq] = jnp.concatenate(
        [dot(eye, r.w_out[...], 1, 1).astype(bf16), dot(eye, r.w_o[...], 1, 1).astype(bf16)], axis=1
    )
    r.f_down[seq] = dot(eye, r.w_down[...], 1, 1).astype(bf16)
    r.f_ffn[seq] = jnp.concatenate([r.w_gate[...], r.w_up[...]], axis=1)
    tokens_wide = r.tokens[...].astype(f32)
    scale_mix = rms_scale(tokens_wide)
    r.normed[pl.ds(HALO, rows), :] = (tokens_wide * scale_mix * r.gain_mix[...]).astype(bf16)
    halo.wait_recv()
    before = jnp.where(seq > 0, r.halo[...].astype(f32), 0.0)
    r.normed[pl.ds(0, HALO), :] = (before * rms_scale(before) * r.gain_mix[...]).astype(bf16)
    positions = seq * rows + lax.broadcasted_iota(jnp.int32, (rows, LANES), 0)
    angles = positions.astype(f32) * r.frequency[...]
    r.cosine[...] = jnp.cos(angles)
    sine = jnp.sin(angles)
    r.sine[...] = jnp.where(lax.rem(lane_h, HD) < HD // 2, -sine, sine)
    r.head_rows[...] = jnp.zeros_like(r.head_rows)
    for k, source in enumerate((r.dt_bias, r.a_log, r.d_skip)):
        r.head_rows[k : k + 1, pl.ds(0, heads)] = source[...]
    for step in range(1, ring.steps):
        ring.gather_step(REST, step)
        ring.gather_step(ZX, step)
    ring.gather_step(MIXED, 0)
    ring.gather_step(FFN, 0)

    bc_width = r.conv_bc.shape[1]
    ring.gather_end(REST)
    rest = dot(r.normed[...], r.f_rest[...].reshape(width, r.f_rest.shape[2]))
    r.blocks[wa] = rest[:, LANES : 2 * LANES]
    projected.begin()
    cosine, sine = r.cosine[...], r.sine[...]

    def turned(values):
        return values * cosine + swapped(values) * sine

    def unturned(values):
        return values * cosine - swapped(values) * sine

    q_rot = (turned(rest[HALO:, :LANES]) * HD ** (-0.5)).astype(bf16).astype(f32)
    r.q_pad[pl.ds(0, rows), :] = jnp.where(low_half, q_rot, 0.0).astype(bf16)
    r.q_pad[pl.ds(rows, rows), :] = jnp.where(low_half, half_turned(q_rot), 0.0).astype(bf16)
    r.dt_in[...] = rest[HALO:, 2 * LANES :]
    projected.forward()
    ring.gather_end(ZX)
    zx = dot(r.normed[...], r.f_zx[...].reshape(width, 2 * inner))
    r.z_proj[...] = zx[HALO:, :inner]
    r.x_rows[...] = zx[:, inner:]
    projected.arrived()
    keys = turned(r.blocks[2, pl.ds(HALO, rows), :])
    values = r.blocks[3, pl.ds(HALO, rows), :]
    first_head = kv_head == 0
    r.f_kv[seq] = jnp.where(
        low_half,
        jnp.where(first_head, keys, half_turned(keys)),
        jnp.where(first_head, half_turned(values), values),
    ).astype(bf16)
    ring.gather_step(KV, 0)
    r.bc_rows[:, pl.ds(0, LANES)] = r.blocks[0]
    r.bc_rows[:, pl.ds(LANES, LANES)] = r.blocks[1]

    def convolved(source, taps):
        running = taps[0:1, :] * source[pl.ds(HALO - EDGE, rows), :]
        for k in range(1, CONVK):
            running = running + taps[k : k + 1, :] * source[pl.ds(HALO - EDGE + k, rows), :]
        return running

    x_pre = convolved(r.x_rows, r.conv_x[...])
    bc_pre = convolved(r.bc_rows, r.conv_bc[...])
    r.x_pre[...] = x_pre
    r.bc_pre[...] = bc_pre
    x_conv = x_pre * sigmoid(x_pre)
    r.x_conv[...] = x_conv
    bc_conv = bc_pre * sigmoid(bc_pre)
    r.b_mat[...] = bc_conv[:, :NS].astype(bf16)
    r.c_mat[...] = bc_conv[:, NS:].astype(bf16)
    rate = -jnp.exp(r.head_rows[1:2, :])
    step_size = softplus(r.dt_in[...] + r.head_rows[0:1, :])
    r.step_size[...] = step_size
    tick_t = lax.broadcasted_iota(jnp.int32, (rows, rows), 0)
    tick_s = lanes_of((rows, rows))
    causal = tick_t >= tick_s
    cumulative = dot(causal.astype(f32), rate * step_size, precision=highest)
    r.cumulative[...] = cumulative
    r.cum_t[...] = cumulative.T
    r.step_t[...] = step_size.T
    pick_row = lax.broadcasted_iota(jnp.int32, (LANES, inner), 0)
    pick_lane = lax.div(lanes_of((LANES, inner)), SH)
    pick = (pick_row == pick_lane).astype(f32)

    def spread(per_head):
        return dot(per_head, pick, precision=highest)

    def head_sums(wide):
        return dot(wide, pick, 1, 1, precision=highest)

    r.skip_row[...] = spread(r.head_rows[...])[2:3, :]
    last = cumulative[rows - 1 : rows, :]
    tail_decay = jnp.exp(last - cumulative)
    tail = spread(tail_decay * step_size)
    r.tail[...] = tail
    x_tail = (x_conv * tail).astype(bf16)
    r.x_tail[...] = x_tail
    local_state = dot(x_tail, r.b_mat[...], 0, 0)
    high = last.astype(bf16).astype(f32)
    middle = (last - high).astype(bf16).astype(f32)
    low = last - high - middle
    row_of = lax.broadcasted_iota(jnp.int32, (2 * HALO, LANES), 0)
    split_rows = jnp.where(
        row_of == 0, high, jnp.where(row_of == 1, middle, jnp.where(row_of == 2, low, 0.0))
    )
    r.f_state[seq, pl.ds(0, inner), :] = local_state.astype(bf16)
    r.f_state[seq, pl.ds(inner, 2 * HALO), :] = split_rows.astype(bf16)
    ring.gather_step(STATE, 0)
    overlap = dot(r.c_mat[...], r.b_mat[...], 1, 1)
    x_bf = x_conv.astype(bf16)
    r.x_bf[...] = x_bf

    def decays(h):
        gap = r.cumulative[:, h : h + 1] - r.cum_t[h : h + 1, :]
        return jnp.exp(jnp.where(causal, gap, MASKED))

    for p in range(pairs):
        at = pl.ds(p * LANES, LANES)
        outs = []
        for h in (2 * p, 2 * p + 1):
            mixing = (decays(h) * overlap * r.step_t[h : h + 1, :]).astype(bf16)
            r.mixing[h] = mixing
            outs.append(dot(mixing, r.x_bf[:, at]))
        r.ssm[:, at] = jnp.where(low_half, outs[0], outs[1])
        if p == 0:
            ring.gather_step(KV, 1)
            ring.gather_step(STATE, 1)
    ring.gather_step(MIXED, 1)
    ring.gather_step(KV, 2)
    ring.gather_step(STATE, 2)
    ring.gather_step(MIXED, 2)
    ring.gather_rest(KV, 3)
    ring.gather_rest(STATE, 3)
    ring.gather_step(FFN, 1)
    ring.gather_step(DOWN, 0)

    ring.gather_end(KV)
    ring.gather_rest(MIXED, 3)

    def block_scores(block):
        scores = dot(r.q_pad[...], r.f_kv[block], 1, 1)
        shape = (2 * rows, rows)
        query = seq * rows + lax.rem(lax.broadcasted_iota(jnp.int32, shape, 0), rows)
        key = block * rows + lanes_of(shape)
        return jnp.where(key <= query, scores, MASKED)

    r.row_max[...] = jnp.full_like(r.row_max, MASKED)
    r.row_sum[...] = jnp.zeros_like(r.row_sum)
    r.attn_acc[...] = jnp.zeros_like(r.attn_acc)

    def visit(block, carry):
        scores = block_scores(block)
        old = r.row_max[...]
        new = jnp.maximum(old, jnp.max(scores, axis=1, keepdims=True))
        weights = jnp.exp(scores - new)
        shrink = jnp.exp(old - new)
        r.row_sum[...] = r.row_sum[...] * shrink + jnp.sum(weights, axis=1, keepdims=True)
        r.attn_acc[...] = r.attn_acc[...] * shrink + dot(weights.astype(bf16), r.f_kv[block])
        r.row_max[...] = new
        return carry

    lax.fori_loop(0, seq + 1, visit, 0)
    ring.gather_step(FFN, 2)
    ring.gather_step(DOWN, 1)
    attn = r.attn_acc[...] / r.row_sum[...]
    r.row_max[...] = r.row_max[...] + jnp.log(r.row_sum[...])
    attn_out = jnp.where(low_half, half_turned(attn[:rows]), attn[rows:])
    r.mixed[:, pl.ds(inner, LANES)] = attn_out.astype(bf16)

    ring.gather_end(STATE)
    reach = jnp.zeros((1, LANES), f32)
    for block in range(count - 1, -1, -1):
        earlier = block < seq
        r.factors[block : block + 1, :] = jnp.where(earlier, jnp.exp(reach), 0.0)
        totals = jnp.sum(
            r.f_state[block, pl.ds(inner, HALO), :].astype(f32), axis=0, keepdims=True
        )
        reach = reach + jnp.where(earlier, totals, 0.0)
    r.start_state[...] = jnp.zeros_like(r.start_state)

    def tall(per_head_row):
        return jnp.concatenate(
            [jnp.broadcast_to(per_head_row[:, h : h + 1], (SH, NS)) for h in range(heads)], axis=0
        )

    def add_state(block, carry):
        factor = tall(r.factors[pl.ds(block, 1), :])
        r.start_state[...] = r.start_state[...] + factor * r.f_state[
            block, pl.ds(0, inner), :
        ].astype(f32)
        return carry

    lax.fori_loop(0, seq, add_state, 0)
    start_b = r.start_state[...].astype(bf16)
    reached = dot(r.c_mat[...], start_b, 1, 1)
    grown = spread(jnp.exp(r.cumulative[...]))
    r.grown[...] = grown
    carried = reached * grown
    r.carried[...] = carried
    ssm = r.ssm[...] + carried + r.skip_row[...] * r.x_conv[...]
    r.ssm[...] = ssm
    z_proj = r.z_proj[...]
    r.mixed[:, pl.ds(0, inner)] = (ssm * (z_proj * sigmoid(z_proj))).astype(bf16)

    ring.gather_end(MIXED)
    mixed_shape = (width, r.f_mixed.shape[2])
    r.part1[...] = dot(r.mixed[...], r.f_mixed[...].reshape(mixed_shape), 1, 1)
    hidden_sum.begin()
    ring.gather_rest(FFN, 3)
    ring.gather_step(DOWN, 2)
    hidden_sum.middle()
    ring.gather_rest(DOWN, 3)
    hidden_sum.finish()
    down_shape = (width, r.f_down.shape[2])
    ffn_shape = (width, r.f_ffn.shape[2])
    ffn_width = r.f_down.shape[2]
    hidden_sum.arrived()
    hidden_sum.sent()

    hidden = r.tokens[...].astype(f32) + r.total1[...]
    r.hidden[...] = hidden
    scale_ffn = rms_scale(hidden)
    r.hnormed[...] = (hidden * scale_ffn * r.gain_ffn[...]).astype(bf16)
    ring.gather_end(FFN)
    gate_up = dot(r.hnormed[...], r.f_ffn[...].reshape(ffn_shape))
    gate, up = gate_up[:, :ffn_width], gate_up[:, ffn_width:]
    open_gate = sigmoid(gate)
    ring.gather_end(DOWN)
    d_act = dot(r.cotangent[...], r.f_down[...].reshape(down_shape))
    r.d_ffn[:, pl.ds(0, ffn_width)] = (
        d_act * up * open_gate * (1.0 + gate * (1.0 - open_gate))
    ).astype(bf16)
    r.d_ffn[:, pl.ds(ffn_width, ffn_width)] = (d_act * gate * open_gate).astype(bf16)
    r.activated[...] = (gate * open_gate * up).astype(bf16)
    r.part1[...] = dot(r.d_ffn[...], r.f_ffn[...].reshape(ffn_shape), 1, 1)
    hnormed_sum.begin()

    def fill(name, left, right):
        parts = getattr(r, "p_" + name)
        parts[...] = dot(left, right, 0, 0).astype(SUM_TYPE).reshape(parts.shape)

    fill(FFN, r.hnormed[...], r.d_ffn[...])
    ring.scatter_step(FFN, 0)
    hnormed_sum.middle()
    fill(DOWN, r.cotangent[...], r.activated[...])
    ring.scatter_step(DOWN, 0)
    r.ffn_part[...] = dot(r.activated[...], r.f_down[...].reshape(down_shape), 1, 1)
    output_sum.begin()
    ring.scatter_step(FFN, 1)
    hnormed_sum.finish()
    ring.scatter_step(DOWN, 1)
    output_sum.middle()
    hnormed_sum.arrived()

    hidden = r.hidden[...]
    scale_ffn = rms_scale(hidden)
    hidden_hat = hidden * scale_ffn
    d_hnormed = r.total1[...]
    weighted = d_hnormed * r.gain_ffn[...]
    d_hidden = r.cotangent[...].astype(f32) + scale_ffn * (
        weighted - hidden_hat * jnp.mean(weighted * hidden_hat, axis=-1, keepdims=True)
    )
    r.d_hidden[...] = d_hidden
    r.d_hidden_b[...] = d_hidden.astype(bf16)
    fill(MIXED, r.d_hidden_b[...], r.mixed[...])
    ring.scatter_step(MIXED, 0)
    gain_ffn_grad = jnp.sum(d_hnormed * hidden_hat, axis=0, keepdims=True)
    chunks = width // LANES
    for k in range(chunks):
        r.small[chunks + k : chunks + k + 1, :] = gain_ffn_grad[:, k * LANES : (k + 1) * LANES]
    d_mixed = dot(r.d_hidden_b[...], r.f_mixed[...].reshape(mixed_shape))
    d_gated = d_mixed[:, :inner]
    d_attn = d_mixed[:, inner:].astype(bf16).astype(f32)

    r.do_pad[pl.ds(0, rows), :] = jnp.where(low_half, 0.0, half_turned(d_attn)).astype(bf16)
    r.do_pad[pl.ds(rows, rows), :] = jnp.where(low_half, 0.0, d_attn).astype(bf16)
    attn_b = r.mixed[:, pl.ds(inner, LANES)].astype(f32)
    products = d_attn * attn_b
    r.delta[pl.ds(0, rows), :] = jnp.sum(jnp.where(low_half, products, 0.0), axis=1, keepdims=True)
    r.delta[pl.ds(rows, rows), :] = jnp.sum(
        jnp.where(low_half, 0.0, products), axis=1, keepdims=True
    )
    r.attn_acc[...] = jnp.zeros_like(r.attn_acc)
    own_state = pl.ds(0, inner)
    for name in (KV, STATE):
        ring.gather_sent(name)

    def revisit(block, carry):
        probability = jnp.exp(block_scores(block) - r.row_max[...])
        keys_values = r.f_kv[block]
        d_probs = dot(r.do_pad[...], keys_values, 1, 1)
        d_scores = (probability * (d_probs - r.delta[...])).astype(bf16)
        r.attn_acc[...] = r.attn_acc[...] + dot(d_scores, keys_values)
        r.p_kv[block] = (
            dot(d_scores, r.q_pad[...], 0, 0)
            + dot(probability.astype(bf16), r.do_pad[...], 0, 0)
        ).astype(SUM_TYPE)
        return carry

    def blank(block, carry):
        r.p_kv[block] = jnp.zeros_like(r.p_kv[block])
        r.p_state[block, own_state, :] = jnp.zeros((inner, LANES), SUM_TYPE)
        return carry

    lax.fori_loop(0, seq + 1, revisit, 0)
    lax.fori_loop(seq + 1, count, blank, 0)
    r.p_state[seq, own_state, :] = jnp.zeros((inner, LANES), SUM_TYPE)
    ring.scatter_step(KV, 0)
    ring.scatter_step(FFN, 2)
    d_q = r.attn_acc[...] * HD ** (-0.5)
    d_q = jnp.where(low_half, d_q[:rows], half_turned(d_q[rows:]))
    r.d_rest[:, pl.ds(0, LANES)] = unturned(d_q).astype(bf16)

    z_proj = r.z_proj[...]
    open_z = sigmoid(z_proj)
    r.d_zx[:, pl.ds(0, inner)] = (
        d_gated * r.ssm[...] * open_z * (1.0 + z_proj * (1.0 - open_z))
    ).astype(bf16)
    d_ssm = d_gated * (z_proj * open_z)
    d_grown = d_ssm * r.grown[...]
    d_grown_b = d_grown.astype(bf16)
    direct = dot(d_grown_b, r.c_mat[...], 0, 0)
    r.direct[...] = direct

    def spread_state(block, carry):
        factor = tall(r.factors[pl.ds(block, 1), :])
        r.p_state[block, own_state, :] = (factor * r.direct[...]).astype(SUM_TYPE)
        return carry

    lax.fori_loop(0, seq, spread_state, 0)
    ring.scatter_step(STATE, 0)
    ring.scatter_step(KV, 1)
    ring.scatter_step(MIXED, 1)
    ring.scatter_step(DOWN, 2)

    r.d_cum[...] = head_sums(d_ssm * r.carried[...])
    skip_sums = jnp.sum(d_ssm * r.x_conv[...], axis=0, keepdims=True)
    skip_grad = head_sums(skip_sums)
    r.d_c[...] = dot(d_grown_b, r.start_state[...].astype(bf16))
    d_ssm_b = d_ssm.astype(bf16)
    r.d_x[...] = r.skip_row[...] * d_ssm
    r.d_overlap[...] = jnp.zeros_like(r.d_overlap)
    r.d_rows[...] = jnp.zeros_like(r.d_rows)
    r.d_cum_rows[...] = jnp.zeros_like(r.d_cum_rows)
    overlap = dot(r.c_mat[...], r.b_mat[...], 1, 1)
    for p in range(pairs):
        at = pl.ds(p * LANES, LANES)
        x_pair = r.x_bf[:, at]
        d_pair = jnp.zeros((rows, LANES), f32)
        for h in (2 * p, 2 * p + 1):
            own = low_half if h == 2 * p else jnp.logical_not(low_half)
            d_head = jnp.where(own, d_ssm[:, p * LANES : (p + 1) * LANES], 0.0).astype(bf16)
            d_mixing = dot(d_head, x_pair, 1, 1) * decays(h)
            step_row = r.step_t[h : h + 1, :]
            weighted = d_mixing * overlap
            from_step = jnp.sum(weighted, axis=0, keepdims=True)
            r.d_rows[h : h + 1, :] = from_step
            r.d_cum_rows[h : h + 1, :] = -from_step * step_row
            row_total = jnp.sum(weighted * step_row, axis=1, keepdims=True)
            r.d_cum[...] = r.d_cum[...] + jnp.where(lane_h == h, row_total, 0.0)
            r.d_overlap[...] = r.d_overlap[...] + d_mixing * step_row
            d_pair = d_pair + dot(r.mixing[h], d_head, 0, 0)
        r.d_x[:, at] = r.d_x[:, at] + d_pair
        if p == 0:
            ring.scatter_step(STATE, 1)
            ring.scatter_step(KV, 2)
        if p == 1:
            ring.scatter_step(STATE, 2)
            ring.scatter_step(KV, 3)
        if p == 2:
            ring.scatter_step(STATE, 3)
    d_overlap_b = r.d_overlap[...].astype(bf16)
    r.d_c[...] = r.d_c[...] + dot(d_overlap_b, r.b_mat[...])
    r.d_b[...] = dot(d_overlap_b, r.c_mat[...], 0, 0)
    ring.scatter_rest(KV, 4)
    ring.scatter_rest(STATE, 4)
    ring.scatter_rest(FFN, 3)
    ring.scatter_step(MIXED, 2)

    own_keys = ring.scatter_end(KV)
    unturned_keys = unturned(own_keys)
    zero = jnp.zeros((rows, LANES), f32)
    d_keys = jnp.where(low_half, unturned_keys, 0.0)
    d_values = jnp.where(low_half, 0.0, own_keys)
    d_keys = jnp.where(first_head, d_keys, half_turned(d_keys))
    d_values = jnp.where(first_head, half_turned(d_values), d_values)
    d_end = ring.scatter_end(STATE)
    d_end_b = d_end.astype(bf16)
    tail = r.tail[...]
    from_end = dot(r.b_mat[...], d_end_b, 1, 1)
    d_x = r.d_x[...] + from_end * tail
    d_tail = head_sums(from_end * r.x_conv[...])
    r.d_b[...] = r.d_b[...] + dot(r.x_tail[...], d_end_b)
    cumulative = r.cumulative[...]
    step_size = r.step_size[...]
    last = cumulative[rows - 1 : rows, :]
    tail_decay = jnp.exp(last - cumulative)
    through = d_tail * tail_decay * step_size
    held = jnp.sum(d_end * r.start_state[...], axis=1, keepdims=True)
    head_row = lax.broadcasted_iota(jnp.int32, (inner, LANES), 0)
    held_heads = jnp.sum(
        jnp.where(lax.div(head_row, SH) == lanes_of((inner, LANES)), held, 0.0),
        axis=0,
        keepdims=True,
    )
    d_last = jnp.sum(through, axis=0, keepdims=True) + jnp.exp(last) * held_heads
    tick_row = lax.broadcasted_iota(jnp.int32, (rows, LANES), 0)
    d_cum = r.d_cum[...] + r.d_cum_rows[...].T - through
    d_cum = d_cum + jnp.where(tick_row == rows - 1, d_last, 0.0)
    d_step = r.d_rows[...].T + d_tail * tail_decay
    rate = -jnp.exp(r.head_rows[1:2, :])
    upto = (tick_s >= tick_t).astype(f32)
    d_log_decay = dot(upto, d_cum, precision=highest)
    d_step = d_step + d_log_decay * rate
    d_dt = d_step * sigmoid(r.dt_in[...] + r.head_rows[0:1, :])
    d_dt = jnp.where(lane_h < heads, d_dt, 0.0)
    r.d_rest[:, pl.ds(2 * LANES, LANES)] = d_dt.astype(bf16)
    small_at = 2 * chunks + CONVK * (inner // LANES + bc_width // LANES)
    r.small[small_at : small_at + 1, :] = jnp.sum(d_dt, axis=0, keepdims=True)
    r.small[small_at + 1 : small_at + 2, :] = (
        jnp.sum(d_log_decay * step_size, axis=0, keepdims=True) * rate
    )
    r.small[small_at + 2 : small_at + 3, :] = skip_grad

    def silu_back(grad, pre):
        opened = sigmoid(pre)
        return grad * opened * (1.0 + pre * (1.0 - opened))

    pad = jnp.zeros((HALO, inner), f32)
    pad_bc = jnp.zeros((HALO, bc_width), f32)
    r.x_back[pl.ds(0, HALO), :] = pad
    r.x_back[pl.ds(HALO, rows), :] = silu_back(d_x, r.x_pre[...])
    r.x_back[pl.ds(HALO + rows, HALO), :] = pad
    d_bc = jnp.concatenate([r.d_b[...], r.d_c[...]], axis=1)
    r.bc_back[pl.ds(0, HALO), :] = pad_bc
    r.bc_back[pl.ds(HALO, rows), :] = silu_back(d_bc, r.bc_pre[...])
    r.bc_back[pl.ds(HALO + rows, HALO), :] = pad_bc

    def back(source, taps, start, length):
        running = taps[0:1, :] * source[pl.ds(start + EDGE, length), :]
        for k in range(1, CONVK):
            running = running + taps[k : k + 1, :] * source[pl.ds(start + EDGE - k, length), :]
        return running

    r.edge_out[:, pl.ds(0, inner)] = back(r.x_back, r.conv_x[...], 0, HALO)
    r.edge_out[:, pl.ds(inner, bc_width)] = back(r.bc_back, r.conv_bc[...], 0, HALO)
    edge = remote(r.edge_out, r.edge_in, r.edge_sems.at[2], r.edge_sems.at[3], preceding)
    edge.start()
    ring.scatter_rest(DOWN, 3)
    r.part3[pl.ds(rows, 2 * HALO), :] = jnp.zeros((2 * HALO, r.part3.shape[1]), f32)
    for k in range(CONVK):
        x_tap = jnp.sum(
            r.x_back[pl.ds(HALO, rows), :] * r.x_rows[pl.ds(HALO - EDGE + k, rows), :],
            axis=0,
            keepdims=True,
        )
        for m in range(inner // LANES):
            at = 2 * chunks + k * (inner // LANES) + m
            r.small[at : at + 1, :] = x_tap[:, m * LANES : (m + 1) * LANES]
        r.part3[rows + k : rows + k + 1, pl.ds(0, bc_width)] = jnp.sum(
            r.bc_back[pl.ds(HALO, rows), :] * r.bc_rows[pl.ds(HALO - EDGE + k, rows), :],
            axis=0,
            keepdims=True,
        )
    d_x_in = back(r.x_back, r.conv_x[...], HALO, rows)
    d_bc_in = back(r.bc_back, r.conv_bc[...], HALO, rows)
    edge.wait_recv()
    edges = jnp.where(seq < count - 1, r.edge_in[...], 0.0)
    above = rows - HALO
    r.d_zx[pl.ds(0, above), pl.ds(inner, inner)] = d_x_in[:above].astype(bf16)
    r.d_zx[pl.ds(above, HALO), pl.ds(inner, inner)] = (d_x_in[above:] + edges[:, :inner]).astype(
        bf16
    )
    r.d_blocks[pl.ds(0, above), pl.ds(0, bc_width)] = d_bc_in[:above]
    r.d_blocks[pl.ds(above, HALO), pl.ds(0, bc_width)] = d_bc_in[above:] + edges[:, inner:]
    r.d_blocks[:, pl.ds(bc_width, LANES)] = d_keys
    r.d_blocks[:, pl.ds(bc_width + LANES, LANES)] = d_values
    block_sum.begin()

    own_normed = pl.ds(HALO, rows)
    fill(ZX, r.normed[own_normed, :], r.d_zx[...])
    ring.scatter_step(ZX, 0)
    block_sum.middle()
    r.part3[pl.ds(0, rows), :] = dot(r.d_zx[...], r.f_zx[...].reshape(width, 2 * inner), 1, 1)
    r.d_rest[:, pl.ds(LANES, LANES)] = block_sum.result().astype(bf16)
    r.part3[pl.ds(0, rows), :] = r.part3[pl.ds(0, rows), :] + dot(
        r.d_rest[...], r.f_rest[...].reshape(width, r.f_rest.shape[2]), 1, 1
    )
    shared_sum.begin()
    fill(REST, r.normed[own_normed, :], r.d_rest[...])
    ring.scatter_step(REST, 0)
    ring.scatter_step(ZX, 1)
    shared_sum.middle()
    ring.scatter_rest(MIXED, 3)
    ring.scatter_step(REST, 1)
    ring.scatter_step(ZX, 2)
    shared_sum.finish()
    ring.scatter_step(REST, 2)
    shared_sum.arrived()
    bc_taps = r.total3[pl.ds(rows, 2 * CONVK), pl.ds(0, bc_width)]
    for k in range(CONVK):
        for m in range(bc_width // LANES):
            at = 2 * chunks + CONVK * (inner // LANES) + k * (bc_width // LANES) + m
            r.small[at : at + 1, :] = bc_taps[k : k + 1, m * LANES : (m + 1) * LANES]
    d_normed = r.total3[pl.ds(0, rows), :]
    tokens_wide = r.tokens[...].astype(f32)
    scale_mix = rms_scale(tokens_wide)
    tokens_hat = tokens_wide * scale_mix
    weighted = d_normed * r.gain_mix[...]
    r.grad_tokens[...] = r.d_hidden[...] + scale_mix * (
        weighted - tokens_hat * jnp.mean(weighted * tokens_hat, axis=-1, keepdims=True)
    )
    gain_mix_grad = jnp.sum(d_normed * tokens_hat, axis=0, keepdims=True)
    for k in range(chunks):
        r.small[k : k + 1, :] = gain_mix_grad[:, k * LANES : (k + 1) * LANES]
    used = small_at + 3
    r.small[used:SMALL_ROWS, :] = jnp.zeros((SMALL_ROWS - used, LANES), f32)
    small_copies = []
    for offset in range(1, count):
        copy = remote(
            r.small,
            r.small_slots.at[seq],
            r.small_send.at[offset - 1],
            r.small_receive.at[offset - 1],
            others[offset - 1],
        )
        copy.start()
        small_copies.append(copy)
    ring.scatter_rest(REST, 3)
    ring.scatter_rest(ZX, 3)
    r.output[...] = (r.hidden[:, output_sum.kept] + output_sum.result()).astype(bf16)
    for name in (DOWN, FFN, MIXED):
        getattr(r, "g_" + name)[...] = ring.scatter_end(name)
    own_rest = ring.scatter_end(REST)
    r.g_blocks[wa] = own_rest[:, LANES : 2 * LANES]
    block_grads.begin()
    r.g_rest[:, pl.ds(0, LANES)] = own_rest[:, :LANES]
    r.g_rest[:, pl.ds(LANES, LANES)] = own_rest[:, 2 * LANES :]
    for copy in small_copies:
        copy.wait()
    r.small_slots[pl.ds(seq, 1)] = r.small[...][None]
    total = r.small_slots[0]
    for other in range(1, count):
        total = total + r.small_slots[other]
    r.small_sum[...] = total
    block_grads.forward()
    r.g_zx[...] = ring.scatter_end(ZX)
    block_grads.arrived()

    halo.wait_send()
    edge.wait_send()
    for name in GATHERED[:5]:
        ring.gather_sent(name)
    for name in SCATTERED:
        ring.scatter_sent(name)
    for sums in (hnormed_sum, shared_sum, output_sum, block_sum, projected, block_grads):
        sums.sent()


def finish_kernel(*refs):
    output_in, tokens_in, small, g_zx, g_rest, g_blocks, g_mixed, g_ffn, g_down = refs[:9]
    z, x, bc, dt, out, q, kv, o, gate, up, down = refs[9:20]
    output, grad_tokens, gain_mix, gain_ffn, conv_x, conv_bc, dt_bias, a_log, d_skip = refs[20:]
    output[...] = output_in[...]
    grad_tokens[...] = tokens_in[...]
    inner = z.shape[1]
    z[...] = g_zx[:, pl.ds(0, inner)]
    x[...] = g_zx[:, pl.ds(inner, inner)]
    q[...] = g_rest[:, pl.ds(0, LANES)]
    dt[...] = g_rest[:, pl.ds(LANES, LANES)][:, : dt.shape[1]]
    for k in range(2):
        bc[:, pl.ds(k * LANES, LANES)] = g_blocks[k]
        kv[:, pl.ds(k * LANES, LANES)] = g_blocks[2 + k]
    ffn_width = gate.shape[1]
    gate[...] = g_ffn[:, pl.ds(0, ffn_width)]
    up[...] = g_ffn[:, pl.ds(ffn_width, ffn_width)]
    out[...] = g_mixed[:, pl.ds(0, inner)].T
    o[...] = g_mixed[:, pl.ds(inner, LANES)].T
    down[...] = g_down[...].T
    sums = small[...]
    at = 0
    for target in (gain_mix, gain_ffn):
        for k in range(target.shape[0] // LANES):
            target[pl.ds(k * LANES, LANES)] = sums[at]
            at += 1
    for target in (conv_x, conv_bc):
        for k in range(CONVK):
            for m in range(target.shape[1] // LANES):
                target[k : k + 1, pl.ds(m * LANES, LANES)] = sums[at : at + 1]
                at += 1
    for target in (dt_bias, a_log, d_skip):
        target[...] = sums[at, : target.shape[0]]
        at += 1


def per_device(
    tokens,
    gain_mix,
    w_z,
    w_x,
    w_bc,
    w_dt,
    conv_x,
    conv_bc,
    dt_bias,
    a_log,
    d_skip,
    w_out,
    w_q,
    w_kv,
    w_o,
    gain_ffn,
    w_gate,
    w_up,
    w_down,
    cotangent,
):
    count = lax.axis_size("seq")
    rows, width = tokens.shape
    depth = w_z.shape[0]
    inner = w_z.shape[1]
    heads = a_log.shape[0]
    ffn = w_gate.shape[1]
    bc_width = w_bc.shape[1]
    lane = np.arange(LANES) % (HD // 2)
    frequency = (ROPE_BASE ** (-(lane * 2.0 / HD))).astype(np.float32)[None]
    inputs = dict(
        tokens=tokens,
        gain_mix=gain_mix[None],
        w_z=w_z,
        w_x=w_x,
        w_bc=w_bc,
        w_dt=w_dt,
        conv_x=conv_x,
        conv_bc=conv_bc,
        dt_bias=dt_bias[None],
        a_log=a_log[None],
        d_skip=d_skip[None],
        w_out=w_out,
        w_q=w_q,
        w_kv=w_kv,
        w_o=w_o,
        gain_ffn=gain_ffn[None],
        w_gate=w_gate,
        w_up=w_up,
        w_down=w_down,
        cotangent=cotangent,
        frequency=jnp.asarray(frequency),
    )
    rest = 3 * LANES
    mixed = inner + w_o.shape[0]

    def shape(*dims, dtype=f32):
        return jax.ShapeDtypeStruct(dims, dtype)

    outputs = dict(
        output=shape(rows, width // 4, dtype=bf16),
        grad_tokens=shape(rows, width),
        small_sum=shape(SMALL_ROWS, LANES),
        g_zx=shape(depth, 2 * inner),
        g_rest=shape(depth, 2 * LANES),
        g_blocks=shape(4, depth, LANES),
        g_mixed=shape(depth, mixed),
        g_ffn=shape(depth, 2 * ffn),
        g_down=shape(depth, ffn),
    )
    scratch = {}

    def room(dtype, **shapes):
        for name, dims in shapes.items():
            scratch[name] = pltpu.VMEM(dims, dtype)

    pieces = dict(
        zx=(depth, 2 * inner),
        rest=(depth, rest),
        mixed=(depth, mixed),
        ffn=(depth, 2 * ffn),
        down=(depth, ffn),
        kv=(rows, LANES),
        state=(inner + 2 * HALO, LANES),
    )
    for name, dims in pieces.items():
        scratch["f_" + name] = pltpu.VMEM((count, *dims), bf16)
        if name == STATE:
            dims = (inner, LANES)
        if name not in (KV, STATE):
            scratch["p_" + name] = pltpu.VMEM((count, *dims), SUM_TYPE)
        scratch["s_" + name] = pltpu.VMEM((2, count // 2 - 1, *dims), SUM_TYPE)
        scratch["e_" + name] = pltpu.VMEM(dims, SUM_TYPE)
        scratch["h_" + name] = pltpu.VMEM((2, *dims), SUM_TYPE)
    tall, half = rows + 2 * HALO, rows // 2
    whole, wide, head, square = (rows, width), (rows, inner), (rows, LANES), (rows, rows)
    quarter, narrow, across = (rows, width // 4), (LANES, rows), (inner, NS)
    room(f32, part1=whole, total1=whole, near1=(half, width))
    room(f32, part3=(tall, width), total3=(tall, width), near3=(tall // 2, width))
    room(SUM_TYPE, fars1=(half, width), far1=(half, width), far2=(half, width))
    room(SUM_TYPE, fars3=(tall // 2, width), far3=(tall // 2, width))
    room(bf16, halo=(HALO, width), normed=(rows + HALO, width))
    room(f32, bc_rows=(rows + HALO, bc_width), x_rows=(rows + HALO, inner), bc_pre=(rows, bc_width))
    room(bf16, q_pad=(2 * rows, LANES), do_pad=(2 * rows, LANES))
    room(f32, dt_in=head, step_size=head, cumulative=head, d_cum=head, d_b=head, d_c=head)
    room(f32, z_proj=wide, x_pre=wide, x_conv=wide, tail=wide, ssm=wide)
    room(f32, grown=wide, carried=wide, d_x=wide)
    room(bf16, b_mat=(rows, NS), c_mat=(rows, NS), x_tail=wide, x_bf=wide)
    room(f32, cum_t=narrow, step_t=narrow, d_rows=narrow, d_cum_rows=narrow, d_overlap=square)
    room(bf16, mixing=(heads, rows, rows), mixed=(rows, mixed))
    room(f32, row_max=(2 * rows, 1), row_sum=(2 * rows, 1), delta=(2 * rows, 1))
    room(f32, attn_acc=(2 * rows, LANES), factors=(max(8, count), LANES))
    room(f32, start_state=across, direct=across)
    room(f32, hidden=whole, d_hidden=whole, ffn_part=whole)
    room(bf16, hnormed=whole, d_hidden_b=whole, d_ffn=(rows, 2 * ffn), activated=(rows, ffn))
    room(f32, ffn_near=(2, *quarter), blocks=(4, rows + HALO, LANES))
    room(SUM_TYPE, ffn_send=quarter, ffn_far=quarter, block_send=head, block_far=head)
    room(f32, d_blocks=(rows, 4 * LANES), block_near=(2, rows, LANES))
    room(bf16, d_zx=(rows, 2 * inner), d_rest=(rows, rest))
    room(f32, x_back=(tall, inner), bc_back=(tall, bc_width))
    room(f32, edge_out=(HALO, inner + bc_width), edge_in=(HALO, inner + bc_width))
    room(f32, cosine=head, sine=head, head_rows=(8, LANES), skip_row=(1, inner))
    room(f32, small=(SMALL_ROWS, LANES), small_slots=(count, SMALL_ROWS, LANES))
    sems = pltpu.SemaphoreType.DMA
    ring, pairwise, trio = (len(GATHERED), 2, count // 2), (3, 3, 4), (2, 3)
    scratch |= dict(
        gather_send=sems(ring),
        gather_receive=sems(ring),
        scatter_send=sems(ring),
        scatter_receive=sems(ring),
        wa_send=sems(pairwise),
        wa_receive=sems(pairwise),
        edge_sems=sems((4,)),
        ffn_sems=sems(trio),
        block_sems=sems(trio),
        share_sems=sems(trio),
        grad_sems=sems(trio),
        small_send=sems((count - 1,)),
        small_receive=sems((count - 1,)),
    )
    vmem = pl.BlockSpec(memory_space=pltpu.VMEM)
    results = pl.pallas_call(
        functools.partial(layer_kernel, count, (*inputs, *outputs, *scratch)),
        out_shape=list(outputs.values()),
        in_specs=[vmem] * len(inputs),
        out_specs=[vmem] * len(outputs),
        scratch_shapes=list(scratch.values()),
        compiler_params=pltpu.CompilerParams(
            collective_id=0, has_side_effects=True, vmem_limit_bytes=VMEM_LIMIT
        ),
    )(*inputs.values())
    placed = [w_z, w_x, w_bc, w_dt, w_out, w_q, w_kv, w_o, w_gate, w_up, w_down]
    vectors = [gain_mix, gain_ffn, conv_x, conv_bc, dt_bias, a_log, d_skip]
    kinds = [shape(*w.shape) for w in placed] + [jax.ShapeDtypeStruct(v.shape, v.dtype) for v in results[:2]]
    kinds += [shape(*v.shape) for v in vectors]
    finished = pl.pallas_call(
        finish_kernel,
        out_shape=kinds,
        in_specs=[vmem] * len(results),
        out_specs=[vmem] * len(kinds),
        compiler_params=pltpu.CompilerParams(vmem_limit_bytes=VMEM_LIMIT),
    )(*results)
    g_z, g_x, g_bc, g_dt, g_out, g_q, g_kv, g_o, g_gate, g_up, g_down = finished[:11]
    output, grad_tokens, g_gain_mix, g_gain_ffn, *rest_grads = finished[11:]
    return (
        output,
        grad_tokens,
        g_gain_mix,
        g_z,
        g_x,
        g_bc,
        g_dt,
        *rest_grads,
        g_out,
        g_q,
        g_kv,
        g_o,
        g_gain_ffn,
        g_gate,
        g_up,
        g_down,
    )


def solution(mesh):
    placed = (
        P("seq", None),
        P(),
        P("seq", "wa"),
        P("seq", "wa"),
        P("seq", None),
        P("seq", "wa"),
        P(None, "wa"),
        P(),
        P("wa"),
        P("wa"),
        P("wa"),
        P("wa", "seq"),
        P("seq", "wa"),
        P("seq", None),
        P("wa", "seq"),
        P(),
        P("seq", "wa"),
        P("seq", "wa"),
        P("wa", "seq"),
        P("seq", None),
    )
    return jax.shard_map(
        per_device,
        mesh=mesh,
        in_specs=placed,
        out_specs=(
            P("seq", "wa"),
            P("seq", None),
            P(),
            P("seq", "wa"),
            P("seq", "wa"),
            P("seq", None),
            P("seq", "wa"),
            P(None, "wa"),
            P(),
            P("wa"),
            P("wa"),
            P("wa"),
            P("wa", "seq"),
            P("seq", "wa"),
            P("seq", None),
            P("wa", "seq"),
            P(),
            P("seq", "wa"),
            P("seq", "wa"),
            P("wa", "seq"),
        ),
        check_vma=False,
    )
```

```python
import functools
import types

import jax
import jax.numpy as jnp
import numpy as np
from jax import lax
from jax.experimental import pallas as pl
from jax.experimental.pallas import tpu as pltpu
from jax.sharding import PartitionSpec as P

NS = 128
CONVK = 4
QH = 8
KVH = 2
HD = 64
SH = 64
HALO = 16
LANES = 128
EPS = 1e-05
ROPE_BASE = 100000000000.0
MASKED = -1e30
SUM_TYPE = jnp.bfloat16
MESH = pl.DeviceIdType.MESH
VMEM_LIMIT = 62 * 1024 * 1024
EDGE = CONVK - 1
f32 = jnp.float32
bf16 = jnp.bfloat16
highest = lax.Precision.HIGHEST

Z, X, REST, MIXED, FFN, DOWN, KV, STATE = GATHERED = (
    "z",
    "x",
    "rest",
    "mixed",
    "ffn",
    "down",
    "kv",
    "state",
)
SCATTERED = GATHERED


def ring_place(index, count):
    odd = lax.rem(index, 2)
    half = lax.div(index, 2)
    return (1 - odd) * half + odd * (count - 1 - half)


def ring_index(place, count):
    place = lax.rem(place + 2 * count, count)
    upper = lax.div(place, count // 2)
    return (1 - upper) * 2 * place + upper * (2 * (count - place) - 1)


def dot(left, right, left_dim=1, right_dim=0, precision=None):
    return lax.dot_general(
        left,
        right,
        (((left_dim,), (right_dim,)), ((), ())),
        precision=precision,
        preferred_element_type=f32,
    )


def remote(source, target, send, receive, peer):
    return pltpu.make_async_remote_copy(
        src_ref=source,
        dst_ref=target,
        send_sem=send,
        recv_sem=receive,
        device_id=peer,
        device_id_type=MESH,
    )


def sigmoid(values):
    return 1.0 / (1.0 + jnp.exp(-values))


def softplus(values):
    return jnp.maximum(values, 0.0) + jnp.log1p(jnp.exp(-jnp.abs(values)))


def rms_scale(rows):
    return lax.rsqrt(jnp.mean(rows * rows, axis=-1, keepdims=True) + EPS)


def lanes_of(shape):
    return lax.broadcasted_iota(jnp.int32, shape, 1)


def swapped(values):
    lane = lax.rem(lanes_of(values.shape), HD)
    ahead = pltpu.roll(values, LANES - HD // 2, 1)
    behind = pltpu.roll(values, HD // 2, 1)
    return jnp.where(lane < HD // 2, ahead, behind)


def half_turned(values):
    return pltpu.roll(values, HD, 1)


class Ring:
    def __init__(self, count, bufs, parts, slots, halves, holds, sems):
        self.count = count
        self.steps = count // 2
        self.seq = lax.axis_index("seq")
        self.place = ring_place(self.seq, count)
        self.sides = [
            {"seq": ring_index(self.place + 1, count)},
            {"seq": ring_index(self.place - 1, count)},
        ]
        self.bufs, self.parts, self.slots = bufs, parts, slots
        self.halves, self.holds = halves, holds
        self.gather_send, self.gather_receive, self.send, self.receive = sems

    def owner(self, offset):
        return ring_index(self.place + offset, self.count)

    def gather_copy(self, name, side, step, arriving):
        c = GATHERED.index(name)
        back = step + 1 if arriving else step
        owner = self.owner(back if side else -back)
        buf = self.bufs[name]
        if step < self.steps - 1:
            piece = buf.at[owner]
        else:
            rows = buf.shape[1] // 2
            piece = buf.at[owner, pl.ds(side * rows, rows)]
        return remote(
            piece,
            piece,
            self.gather_send.at[c, side, step],
            self.gather_receive.at[c, side, step],
            self.sides[side],
        )

    def gather_step(self, name, step):
        for side in range(2):
            if step:
                self.gather_copy(name, side, step - 1, True).wait_recv()
            self.gather_copy(name, side, step, False).start()

    def gather_rest(self, name, first):
        for step in range(first, self.steps):
            self.gather_step(name, step)

    def gather_end(self, name):
        for side in range(2):
            self.gather_copy(name, side, self.steps - 1, True).wait_recv()

    def gather_sent(self, name):
        for side in range(2):
            for step in range(self.steps):
                self.gather_copy(name, side, step, False).wait_send()

    def mine(self, name, side, step):
        rows = self.halves[name].shape[0]
        return self.parts[name].at[self.owner(-step if side else step), pl.ds(0, rows)]

    def slot(self, name, side, step):
        if step < self.steps:
            return self.slots[name].at[side, step - 1]
        rows = self.halves[name].shape[0] // 2
        return self.halves[name].at[pl.ds(side * rows, rows)]

    def scatter_copy(self, name, side, step):
        c = SCATTERED.index(name)
        if step == self.steps:
            rows = self.halves[name].shape[0] // 2
            origin = self.mine(name, side, step).at[pl.ds(side * rows, rows)]
        elif step == self.steps - 1:
            origin = self.holds[name].at[side]
        else:
            origin = self.slot(name, side, step + 1)
        return remote(
            origin,
            self.slot(name, side, step),
            self.send.at[c, side, step - 1],
            self.receive.at[c, side, step - 1],
            self.sides[side],
        )

    def scatter_step(self, name, turn):
        step = self.steps - turn
        rows = self.halves[name].shape[0] // 2
        for side in range(2):
            if turn:
                self.scatter_copy(name, side, step + 1).wait_recv()
                own = self.mine(name, side, step)
                slot = self.slot(name, side, step + 1)
                if turn == 1:
                    hold = self.holds[name].at[side]
                    near = pl.ds(side * rows, rows)
                    away = pl.ds((1 - side) * rows, rows)
                    hold[away, :] = own[away, :]
                    hold[near, :] = (own[near, :].astype(f32) + slot[...].astype(f32)).astype(
                        hold.dtype
                    )
                else:
                    slot[...] = (own[...].astype(f32) + slot[...].astype(f32)).astype(slot.dtype)
            self.scatter_copy(name, side, step).start()

    def scatter_rest(self, name, first):
        for turn in range(first, self.steps):
            self.scatter_step(name, turn)

    def scatter_end(self, name):
        for side in range(2):
            self.scatter_copy(name, side, 1).wait_recv()
        slots = self.slots[name]
        total = (
            self.parts[name][self.seq, pl.ds(0, self.halves[name].shape[0])].astype(f32)
            + slots[0, 0].astype(f32)
            + slots[1, 0].astype(f32)
        )
        return total

    def scatter_sent(self, name):
        for side in range(2):
            for step in range(1, self.steps + 1):
                self.scatter_copy(name, side, step).wait_send()


class Across:
    def __init__(self, value, out, near, far_send, far, send, receive, index, pieces):
        self.wa = lax.axis_index("wa")
        self.core = lax.rem(self.wa, 2)
        self.row = lax.div(self.wa, 2)
        self.mate = {"wa": 2 * self.row + 1 - self.core}
        self.across = {"wa": 2 * (1 - self.row) + self.core}
        self.value, self.out, self.near, self.far_send, self.far = value, out, near, far_send, far
        self.send, self.receive, self.index, self.pieces = send, receive, index, pieces
        self.rows = value.shape[0] // 2
        self.step = self.rows // pieces

    def half(self, core, p):
        return pl.ds(pl.multiple_of(core * self.rows + p * self.step, self.step), self.step)

    def sems(self, stage, p):
        return (self.send.at[self.index, stage, p], self.receive.at[self.index, stage, p])

    def first(self, p):
        at = pl.ds(p * self.step, self.step)
        return remote(
            self.value.at[self.half(1 - self.core, p)],
            self.near.at[at],
            *self.sems(0, p),
            self.mate,
        )

    def second(self, p):
        at = pl.ds(p * self.step, self.step)
        return remote(self.far_send.at[at], self.far.at[at], *self.sems(1, p), self.across)

    def third(self, p, arriving):
        at = self.half(1 - self.core if arriving else self.core, p)
        return remote(self.out.at[at], self.out.at[at], *self.sems(2, p), self.mate)

    def begin(self):
        for p in range(self.pieces):
            self.first(p).start()

    def middle(self):
        for p in range(self.pieces):
            self.first(p).wait_recv()
            at = pl.ds(p * self.step, self.step)
            own = self.half(self.core, p)
            self.far_send[at, :] = (self.value[own, :] + self.near[at, :]).astype(SUM_TYPE)
            self.second(p).start()

    def finish(self):
        for p in range(self.pieces):
            self.second(p).wait_recv()
            at = pl.ds(p * self.step, self.step)
            own = self.half(self.core, p)
            self.out[own, :] = self.far_send[at, :].astype(f32) + self.far[at, :].astype(f32)
            self.third(p, False).start()

    def arrived(self):
        for p in range(self.pieces):
            self.third(p, True).wait_recv()

    def sent(self):
        for p in range(self.pieces):
            self.first(p).wait_send()
            self.second(p).wait_send()
            self.third(p, False).wait_send()


class Split:
    def __init__(self, value, near, far_send, far, sems, wa):
        core, row = lax.rem(wa, 2), lax.div(wa, 2)
        mate, across = {"wa": 2 * row + 1 - core}, {"wa": 2 * (1 - row) + core}
        self.value, self.near, self.far_send, self.far, self.row = value, near, far_send, far, row
        wide = far.shape[1]

        def columns(block):
            return pl.ds(pl.multiple_of(block * wide, LANES), wide)

        self.kept, self.theirs = columns(2 * row + core), columns(2 * (1 - row) + core)
        self.firsts = [
            remote(
                value.at[:, columns(2 * k + 1 - core)], near.at[k], sems.at[0, k], sems.at[1, k], mate
            )
            for k in range(2)
        ]
        self.second = remote(far_send, far, sems.at[0, 2], sems.at[1, 2], across)

    def begin(self):
        for copy in self.firsts:
            copy.start()

    def middle(self):
        for copy in self.firsts:
            copy.wait_recv()
        self.far_send[...] = (self.value[:, self.theirs] + self.near[1 - self.row]).astype(SUM_TYPE)
        self.second.start()

    def result(self):
        self.second.wait_recv()
        return self.value[:, self.kept] + self.near[self.row] + self.far[...].astype(f32)

    def sent(self):
        for copy in self.firsts:
            copy.wait_send()
        self.second.wait_send()


class Share:
    def __init__(self, buf, sems, wa):
        core, row = lax.rem(wa, 2), lax.div(wa, 2)
        mate, across = 2 * row + 1 - core, 2 * (1 - row) + core

        def copy(block, k, peer):
            return remote(buf.at[block], buf.at[block], sems.at[0, k], sems.at[1, k], {"wa": peer})

        self.sends = [copy(wa, 0, across), copy(wa, 1, mate), copy(across, 2, mate)]
        self.arrivals = [
            copy(across, 0, across), copy(mate, 1, mate), copy(2 * (1 - row) + 1 - core, 2, mate)
        ]

    def begin(self):
        self.sends[0].start()
        self.sends[1].start()

    def forward(self):
        self.arrivals[0].wait_recv()
        self.sends[2].start()

    def arrived(self):
        self.arrivals[1].wait_recv()
        self.arrivals[2].wait_recv()

    def sent(self):
        for copy in self.sends:
            copy.wait_send()


SMALL_ROWS = 40


def layer_kernel(count, names, *refs):
    r = types.SimpleNamespace(**dict(zip(names, refs)))
    seq = lax.axis_index("seq")
    wa = lax.axis_index("wa")
    rows, width = r.tokens.shape
    inner = r.w_z.shape[1]
    heads = inner // SH
    pairs = heads // 2
    lane_h = lanes_of((rows, LANES))
    low_half = lane_h < HD
    kv_head = lax.div(wa * (r.w_q.shape[1] // HD), QH // KVH)

    def family(prefix):
        return {name: getattr(r, prefix + name) for name in GATHERED}

    r.p_kv, r.p_state = r.f_kv, r.f_state

    ring = Ring(
        count,
        *(family(prefix) for prefix in ("f_", "p_", "s_", "e_", "h_")),
        (r.gather_send, r.gather_receive, r.scatter_send, r.scatter_receive),
    )
    hidden_sum = Across(r.part1, r.total1, r.near1, r.fars1, r.far1, r.wa_send, r.wa_receive, 0, 4)
    hnormed_sum = Across(r.part1, r.total1, r.near1, r.fars1, r.far2, r.wa_send, r.wa_receive, 1, 4)
    shared_sum = Across(r.part3, r.total3, r.near3, r.fars3, r.far3, r.wa_send, r.wa_receive, 2, 3)
    mate, across = hidden_sum.mate, hidden_sum.across
    output_sum = Split(r.ffn_part, r.ffn_near, r.ffn_send, r.ffn_far, r.ffn_sems, wa)
    block_sum = Split(r.d_blocks, r.block_near, r.block_send, r.block_far, r.block_sems, wa)
    projected = Share(r.blocks, r.share_sems, wa)
    block_grads = Share(r.g_blocks, r.grad_sems, wa)
    others = [{"seq": lax.rem(seq + offset, count)} for offset in range(1, count)]
    following, preceding = others[0], others[-1]
    barrier = pltpu.get_barrier_semaphore()
    peers = others + [mate, across]
    for peer in peers:
        pl.semaphore_signal(barrier, inc=1, device_id=peer, device_id_type=MESH)

    r.f_z[seq] = r.w_z[...]
    r.f_x[seq] = r.w_x[...]
    depth = r.w_out.shape[1]
    eye = (
        lax.broadcasted_iota(jnp.int32, (depth, depth), 0) == lanes_of((depth, depth))
    ).astype(bf16)
    own_columns = jnp.where(
        wa < 2,
        jnp.where(wa == 0, r.w_bc[:, pl.ds(0, LANES)], r.w_bc[:, pl.ds(LANES, LANES)]),
        jnp.where(wa == 2, r.w_kv[:, pl.ds(0, LANES)], r.w_kv[:, pl.ds(LANES, LANES)]),
    )
    r.f_rest[seq] = jnp.concatenate([r.w_q[...], own_columns], axis=1)
    r.dt_pad[...] = jnp.zeros_like(r.dt_pad)
    r.dt_pad[pl.ds(0, heads), :] = r.w_dt[...].astype(f32)
    r.f_dt[seq] = r.dt_pad[...].astype(bf16)
    pl.semaphore_wait(barrier, len(peers))
    halo = remote(
        r.tokens.at[pl.ds(rows - HALO, HALO)], r.halo, r.edge_sems.at[0], r.edge_sems.at[1], following
    )
    halo.start()
    dt_sends = [
        remote(r.f_dt.at[seq], r.f_dt.at[seq], r.dt_sems.at[0, k], r.dt_sems.at[1, k], other)
        for k, other in enumerate(others)
    ]
    sources = [lax.rem(seq + count - offset, count) for offset in range(1, count)]
    dt_arrivals = [
        remote(r.f_dt.at[k], r.f_dt.at[k], r.dt_sems.at[0, m], r.dt_sems.at[1, m], others[m])
        for m, k in enumerate(sources)
    ]
    for copy in dt_sends:
        copy.start()
    ring.gather_step(REST, 0)
    ring.gather_step(X, 0)
    ring.gather_step(Z, 0)
    r.f_mixed[seq] = jnp.concatenate(
        [dot(eye, r.w_out[...], 1, 1).astype(bf16), dot(eye, r.w_o[...], 1, 1).astype(bf16)], axis=1
    )
    r.f_down[seq] = dot(eye, r.w_down[...], 1, 1).astype(bf16)
    r.f_ffn[seq] = jnp.concatenate([r.w_gate[...], r.w_up[...]], axis=1)
    tokens_wide = r.tokens[...].astype(f32)
    scale_mix = rms_scale(tokens_wide)
    r.normed[pl.ds(HALO, rows), :] = (tokens_wide * scale_mix * r.gain_mix[...]).astype(bf16)
    halo.wait_recv()
    before = jnp.where(seq > 0, r.halo[...].astype(f32), 0.0)
    r.normed[pl.ds(0, HALO), :] = (before * rms_scale(before) * r.gain_mix[...]).astype(bf16)
    positions = seq * rows + lax.broadcasted_iota(jnp.int32, (rows, LANES), 0)
    angles = positions.astype(f32) * r.frequency[...]
    r.cosine[...] = jnp.cos(angles)
    sine = jnp.sin(angles)
    r.sine[...] = jnp.where(lax.rem(lane_h, HD) < HD // 2, -sine, sine)
    r.head_rows[...] = jnp.zeros_like(r.head_rows)
    for k, source in enumerate((r.dt_bias, r.a_log, r.d_skip)):
        r.head_rows[k : k + 1, pl.ds(0, heads)] = source[...]
    for step in range(1, ring.steps):
        ring.gather_step(REST, step)
        ring.gather_step(X, step)
        ring.gather_step(Z, step)
    ring.gather_step(MIXED, 0)
    ring.gather_step(FFN, 0)
    ring.gather_step(DOWN, 0)

    bc_width = r.conv_bc.shape[1]
    ring.gather_end(REST)
    rest = dot(r.normed[...], r.f_rest[...].reshape(width, r.f_rest.shape[2]))
    r.blocks[wa] = rest[:, LANES : 2 * LANES]
    projected.begin()
    cosine, sine = r.cosine[...], r.sine[...]

    def turned(values):
        return values * cosine + swapped(values) * sine

    def unturned(values):
        return values * cosine - swapped(values) * sine

    q_rot = (turned(rest[HALO:, :LANES]) * HD ** (-0.5)).astype(bf16).astype(f32)
    r.q_pad[pl.ds(0, rows), :] = jnp.where(low_half, q_rot, 0.0).astype(bf16)
    r.q_pad[pl.ds(rows, rows), :] = jnp.where(low_half, half_turned(q_rot), 0.0).astype(bf16)
    for copy in dt_arrivals:
        copy.wait_recv()
    dt_proj = jnp.zeros((rows, HALO), f32)
    for k in range(count):
        normed_part = r.normed[pl.ds(HALO, rows), pl.ds(k * depth, depth)]
        dt_proj = dt_proj + dot(normed_part, r.f_dt[k], 1, 1)
    r.dt_in[...] = jnp.zeros_like(r.dt_in)
    r.dt_in[:, pl.ds(0, HALO)] = dt_proj
    projected.forward()
    ring.gather_end(X)
    r.x_rows[...] = dot(r.normed[...], r.f_x[...].reshape(width, inner))
    projected.arrived()
    keys = turned(r.blocks[2, pl.ds(HALO, rows), :])
    values = r.blocks[3, pl.ds(HALO, rows), :]
    first_head = kv_head == 0
    r.f_kv[seq] = jnp.where(
        low_half,
        jnp.where(first_head, keys, half_turned(keys)),
        jnp.where(first_head, half_turned(values), values),
    ).astype(bf16)
    ring.gather_step(KV, 0)
    r.bc_rows[:, pl.ds(0, LANES)] = r.blocks[0]
    r.bc_rows[:, pl.ds(LANES, LANES)] = r.blocks[1]

    def convolved(source, taps):
        running = taps[0:1, :] * source[pl.ds(HALO - EDGE, rows), :]
        for k in range(1, CONVK):
            running = running + taps[k : k + 1, :] * source[pl.ds(HALO - EDGE + k, rows), :]
        return running

    x_pre = convolved(r.x_rows, r.conv_x[...])
    bc_pre = convolved(r.bc_rows, r.conv_bc[...])
    r.x_pre[...] = x_pre
    r.bc_pre[...] = bc_pre
    x_conv = x_pre * sigmoid(x_pre)
    r.x_conv[...] = x_conv
    bc_conv = bc_pre * sigmoid(bc_pre)
    r.b_mat[...] = bc_conv[:, :NS].astype(bf16)
    r.c_mat[...] = bc_conv[:, NS:].astype(bf16)
    rate = -jnp.exp(r.head_rows[1:2, :])
    step_size = softplus(r.dt_in[...] + r.head_rows[0:1, :])
    r.step_size[...] = step_size
    tick_t = lax.broadcasted_iota(jnp.int32, (rows, rows), 0)
    tick_s = lanes_of((rows, rows))
    causal = tick_t >= tick_s
    cumulative = dot(causal.astype(f32), rate * step_size, precision=highest)
    r.cumulative[...] = cumulative
    r.cum_t[...] = cumulative.T
    r.step_t[...] = step_size.T
    pick_row = lax.broadcasted_iota(jnp.int32, (LANES, inner), 0)
    pick_lane = lax.div(lanes_of((LANES, inner)), SH)
    pick = (pick_row == pick_lane).astype(f32)

    def spread(per_head):
        return dot(per_head, pick, precision=highest)

    def head_sums(wide):
        return dot(wide, pick, 1, 1, precision=highest)

    r.skip_row[...] = spread(r.head_rows[...])[2:3, :]
    last = cumulative[rows - 1 : rows, :]
    tail_decay = jnp.exp(last - cumulative)
    tail = spread(tail_decay * step_size)
    r.tail[...] = tail
    x_tail = (x_conv * tail).astype(bf16)
    r.x_tail[...] = x_tail
    local_state = dot(x_tail, r.b_mat[...], 0, 0)
    high = last.astype(bf16).astype(f32)
    middle = (last - high).astype(bf16).astype(f32)
    low = last - high - middle
    row_of = lax.broadcasted_iota(jnp.int32, (2 * HALO, LANES), 0)
    split_rows = jnp.where(
        row_of == 0, high, jnp.where(row_of == 1, middle, jnp.where(row_of == 2, low, 0.0))
    )
    r.f_state[seq, pl.ds(0, inner), :] = local_state.astype(bf16)
    r.f_state[seq, pl.ds(inner, 2 * HALO), :] = split_rows.astype(bf16)
    ring.gather_step(STATE, 0)
    overlap = dot(r.c_mat[...], r.b_mat[...], 1, 1)
    x_bf = x_conv.astype(bf16)
    r.x_bf[...] = x_bf

    def decays(h):
        gap = r.cumulative[:, h : h + 1] - r.cum_t[h : h + 1, :]
        return jnp.exp(jnp.where(causal, gap, MASKED))

    for p in range(pairs):
        at = pl.ds(p * LANES, LANES)
        outs = []
        for h in (2 * p, 2 * p + 1):
            mixing = (decays(h) * overlap * r.step_t[h : h + 1, :]).astype(bf16)
            r.mixing[h] = mixing
            outs.append(dot(mixing, r.x_bf[:, at]))
        r.ssm[:, at] = jnp.where(low_half, outs[0], outs[1])
        if p == 0:
            ring.gather_step(KV, 1)
            ring.gather_step(STATE, 1)
    ring.gather_step(MIXED, 1)
    ring.gather_step(KV, 2)
    ring.gather_step(STATE, 2)
    ring.gather_step(MIXED, 2)
    ring.gather_rest(KV, 3)
    ring.gather_rest(STATE, 3)
    ring.gather_step(FFN, 1)

    ring.gather_end(KV)
    ring.gather_rest(MIXED, 3)

    def block_scores(block):
        scores = dot(r.q_pad[...], r.f_kv[block], 1, 1)
        shape = (2 * rows, rows)
        query = seq * rows + lax.rem(lax.broadcasted_iota(jnp.int32, shape, 0), rows)
        key = block * rows + lanes_of(shape)
        return jnp.where(key <= query, scores, MASKED)

    r.row_max[...] = jnp.full_like(r.row_max, MASKED)
    r.row_sum[...] = jnp.zeros_like(r.row_sum)
    r.attn_acc[...] = jnp.zeros_like(r.attn_acc)

    def visit(block, carry):
        scores = block_scores(block)
        old = r.row_max[...]
        new = jnp.maximum(old, jnp.max(scores, axis=1, keepdims=True))
        weights = jnp.exp(scores - new)
        shrink = jnp.exp(old - new)
        r.row_sum[...] = r.row_sum[...] * shrink + jnp.sum(weights, axis=1, keepdims=True)
        r.attn_acc[...] = r.attn_acc[...] * shrink + dot(weights.astype(bf16), r.f_kv[block])
        r.row_max[...] = new
        return carry

    middle_block = lax.div(seq + 1, 2)
    lax.fori_loop(0, middle_block, visit, 0)
    ring.gather_step(FFN, 2)
    ring.gather_step(DOWN, 1)
    lax.fori_loop(middle_block, seq + 1, visit, 0)
    attn = r.attn_acc[...] / r.row_sum[...]
    r.row_max[...] = r.row_max[...] + jnp.log(r.row_sum[...])
    attn_out = jnp.where(low_half, half_turned(attn[:rows]), attn[rows:])
    r.mixed[:, pl.ds(inner, LANES)] = attn_out.astype(bf16)

    ring.gather_end(STATE)
    reach = jnp.zeros((1, LANES), f32)
    for block in range(count - 1, -1, -1):
        earlier = block < seq
        r.factors[block : block + 1, :] = jnp.where(earlier, jnp.exp(reach), 0.0)
        totals = jnp.sum(
            r.f_state[block, pl.ds(inner, HALO), :].astype(f32), axis=0, keepdims=True
        )
        reach = reach + jnp.where(earlier, totals, 0.0)
    r.start_state[...] = jnp.zeros_like(r.start_state)

    def tall(per_head_row):
        return jnp.concatenate(
            [jnp.broadcast_to(per_head_row[:, h : h + 1], (SH, NS)) for h in range(heads)], axis=0
        )

    def add_state(block, carry):
        factor = tall(r.factors[pl.ds(block, 1), :])
        r.start_state[...] = r.start_state[...] + factor * r.f_state[
            block, pl.ds(0, inner), :
        ].astype(f32)
        return carry

    lax.fori_loop(0, seq, add_state, 0)
    start_b = r.start_state[...].astype(bf16)
    reached = dot(r.c_mat[...], start_b, 1, 1)
    grown = spread(jnp.exp(r.cumulative[...]))
    r.grown[...] = grown
    carried = reached * grown
    r.carried[...] = carried
    ssm = r.ssm[...] + carried + r.skip_row[...] * r.x_conv[...]
    r.ssm[...] = ssm
    ring.gather_end(Z)
    z_proj = dot(r.normed[pl.ds(HALO, rows), :], r.f_z[...].reshape(width, inner))
    r.z_proj[...] = z_proj
    r.mixed[:, pl.ds(0, inner)] = (ssm * (z_proj * sigmoid(z_proj))).astype(bf16)

    ring.gather_end(MIXED)
    mixed_shape = (width, r.f_mixed.shape[2])
    r.part1[...] = dot(r.mixed[...], r.f_mixed[...].reshape(mixed_shape), 1, 1)
    hidden_sum.begin()
    hidden_sum.middle()
    ring.gather_rest(FFN, 3)
    ring.gather_step(DOWN, 2)
    hidden_sum.finish()
    ring.gather_rest(DOWN, 3)
    down_shape = (width, r.f_down.shape[2])
    ffn_shape = (width, r.f_ffn.shape[2])
    ffn_width = r.f_down.shape[2]
    hidden_sum.arrived()
    hidden_sum.sent()

    hidden = r.tokens[...].astype(f32) + r.total1[...]
    r.hidden[...] = hidden
    scale_ffn = rms_scale(hidden)
    r.hnormed[...] = (hidden * scale_ffn * r.gain_ffn[...]).astype(bf16)
    ring.gather_end(FFN)
    gate_up = dot(r.hnormed[...], r.f_ffn[...].reshape(ffn_shape))
    gate, up = gate_up[:, :ffn_width], gate_up[:, ffn_width:]
    open_gate = sigmoid(gate)
    ring.gather_end(DOWN)
    d_act = dot(r.cotangent[...], r.f_down[...].reshape(down_shape))
    r.d_ffn[:, pl.ds(0, ffn_width)] = (
        d_act * up * open_gate * (1.0 + gate * (1.0 - open_gate))
    ).astype(bf16)
    r.d_ffn[:, pl.ds(ffn_width, ffn_width)] = (d_act * gate * open_gate).astype(bf16)
    r.activated[...] = (gate * open_gate * up).astype(bf16)
    r.part1[...] = dot(r.d_ffn[...], r.f_ffn[...].reshape(ffn_shape), 1, 1)
    hnormed_sum.begin()

    def fill(name, left, right):
        parts = getattr(r, "p_" + name)
        parts[...] = dot(left, right, 0, 0).astype(SUM_TYPE).reshape(parts.shape)

    fill(FFN, r.hnormed[...], r.d_ffn[...])
    ring.scatter_step(FFN, 0)
    hnormed_sum.middle()
    fill(DOWN, r.cotangent[...], r.activated[...])
    ring.scatter_step(DOWN, 0)
    r.ffn_part[...] = dot(r.activated[...], r.f_down[...].reshape(down_shape), 1, 1)
    output_sum.begin()
    ring.scatter_step(FFN, 1)
    hnormed_sum.finish()
    ring.scatter_step(DOWN, 1)
    output_sum.middle()
    hnormed_sum.arrived()

    hidden = r.hidden[...]
    scale_ffn = rms_scale(hidden)
    hidden_hat = hidden * scale_ffn
    d_hnormed = r.total1[...]
    weighted = d_hnormed * r.gain_ffn[...]
    d_hidden = r.cotangent[...].astype(f32) + scale_ffn * (
        weighted - hidden_hat * jnp.mean(weighted * hidden_hat, axis=-1, keepdims=True)
    )
    r.d_hidden[...] = d_hidden
    r.d_hidden_b[...] = d_hidden.astype(bf16)
    fill(MIXED, r.d_hidden_b[...], r.mixed[...])
    ring.scatter_step(MIXED, 0)
    gain_ffn_grad = jnp.sum(d_hnormed * hidden_hat, axis=0, keepdims=True)
    chunks = width // LANES
    for k in range(chunks):
        r.small[chunks + k : chunks + k + 1, :] = gain_ffn_grad[:, k * LANES : (k + 1) * LANES]
    d_mixed = dot(r.d_hidden_b[...], r.f_mixed[...].reshape(mixed_shape))
    d_gated = d_mixed[:, :inner]
    d_attn = d_mixed[:, inner:].astype(bf16).astype(f32)

    r.do_pad[pl.ds(0, rows), :] = jnp.where(low_half, 0.0, half_turned(d_attn)).astype(bf16)
    r.do_pad[pl.ds(rows, rows), :] = jnp.where(low_half, 0.0, d_attn).astype(bf16)
    attn_b = r.mixed[:, pl.ds(inner, LANES)].astype(f32)
    products = d_attn * attn_b
    r.delta[pl.ds(0, rows), :] = jnp.sum(jnp.where(low_half, products, 0.0), axis=1, keepdims=True)
    r.delta[pl.ds(rows, rows), :] = jnp.sum(
        jnp.where(low_half, 0.0, products), axis=1, keepdims=True
    )
    r.attn_acc[...] = jnp.zeros_like(r.attn_acc)
    own_state = pl.ds(0, inner)
    for name in (KV, STATE):
        ring.gather_sent(name)

    def revisit(block, carry):
        probability = jnp.exp(block_scores(block) - r.row_max[...])
        keys_values = r.f_kv[block]
        d_probs = dot(r.do_pad[...], keys_values, 1, 1)
        d_scores = (probability * (d_probs - r.delta[...])).astype(bf16)
        r.attn_acc[...] = r.attn_acc[...] + dot(d_scores, keys_values)
        r.p_kv[block] = (
            dot(d_scores, r.q_pad[...], 0, 0)
            + dot(probability.astype(bf16), r.do_pad[...], 0, 0)
        ).astype(SUM_TYPE)
        return carry

    def blank(block, carry):
        r.p_kv[block] = jnp.zeros_like(r.p_kv[block])
        r.p_state[block, own_state, :] = jnp.zeros((inner, LANES), SUM_TYPE)
        return carry

    back_block = lax.div(seq + 1, 2)
    lax.fori_loop(0, back_block, revisit, 0)
    ring.scatter_step(FFN, 2)
    ring.scatter_step(DOWN, 2)
    lax.fori_loop(back_block, seq + 1, revisit, 0)
    lax.fori_loop(seq + 1, count, blank, 0)
    r.p_state[seq, own_state, :] = jnp.zeros((inner, LANES), SUM_TYPE)
    ring.scatter_step(KV, 0)
    d_q = r.attn_acc[...] * HD ** (-0.5)
    d_q = jnp.where(low_half, d_q[:rows], half_turned(d_q[rows:]))
    r.d_rest[:, pl.ds(0, LANES)] = unturned(d_q).astype(bf16)

    z_proj = r.z_proj[...]
    open_z = sigmoid(z_proj)
    r.d_z[...] = (
        d_gated * r.ssm[...] * open_z * (1.0 + z_proj * (1.0 - open_z))
    ).astype(bf16)
    d_ssm = d_gated * (z_proj * open_z)
    d_grown = d_ssm * r.grown[...]
    d_grown_b = d_grown.astype(bf16)
    direct = dot(d_grown_b, r.c_mat[...], 0, 0)
    r.direct[...] = direct

    def spread_state(block, carry):
        factor = tall(r.factors[pl.ds(block, 1), :])
        r.p_state[block, own_state, :] = (factor * r.direct[...]).astype(SUM_TYPE)
        return carry

    lax.fori_loop(0, seq, spread_state, 0)
    ring.scatter_step(STATE, 0)
    own_normed = pl.ds(HALO, rows)
    fill(Z, r.normed[own_normed, :], r.d_z[...])
    ring.scatter_step(Z, 0)
    ring.scatter_step(KV, 1)
    ring.scatter_step(MIXED, 1)

    r.d_cum[...] = head_sums(d_ssm * r.carried[...])
    skip_sums = jnp.sum(d_ssm * r.x_conv[...], axis=0, keepdims=True)
    skip_grad = head_sums(skip_sums)
    r.d_c[...] = dot(d_grown_b, r.start_state[...].astype(bf16))
    d_ssm_b = d_ssm.astype(bf16)
    r.d_x[...] = r.skip_row[...] * d_ssm
    r.d_overlap[...] = jnp.zeros_like(r.d_overlap)
    r.d_rows[...] = jnp.zeros_like(r.d_rows)
    r.d_cum_rows[...] = jnp.zeros_like(r.d_cum_rows)
    overlap = dot(r.c_mat[...], r.b_mat[...], 1, 1)
    for p in range(pairs):
        at = pl.ds(p * LANES, LANES)
        x_pair = r.x_bf[:, at]
        d_pair = jnp.zeros((rows, LANES), f32)
        for h in (2 * p, 2 * p + 1):
            own = low_half if h == 2 * p else jnp.logical_not(low_half)
            d_head = jnp.where(own, d_ssm[:, p * LANES : (p + 1) * LANES], 0.0).astype(bf16)
            d_mixing = dot(d_head, x_pair, 1, 1) * decays(h)
            step_row = r.step_t[h : h + 1, :]
            weighted = d_mixing * overlap
            from_step = jnp.sum(weighted, axis=0, keepdims=True)
            r.d_rows[h : h + 1, :] = from_step
            r.d_cum_rows[h : h + 1, :] = -from_step * step_row
            row_total = jnp.sum(weighted * step_row, axis=1, keepdims=True)
            r.d_cum[...] = r.d_cum[...] + jnp.where(lane_h == h, row_total, 0.0)
            r.d_overlap[...] = r.d_overlap[...] + d_mixing * step_row
            d_pair = d_pair + dot(r.mixing[h], d_head, 0, 0)
        r.d_x[:, at] = r.d_x[:, at] + d_pair
        if p == 0:
            ring.scatter_step(STATE, 1)
            ring.scatter_step(KV, 2)
        if p == 1:
            ring.scatter_step(STATE, 2)
            ring.scatter_step(KV, 3)
        if p == 2:
            ring.scatter_step(STATE, 3)
    d_overlap_b = r.d_overlap[...].astype(bf16)
    r.d_c[...] = r.d_c[...] + dot(d_overlap_b, r.b_mat[...])
    r.d_b[...] = dot(d_overlap_b, r.c_mat[...], 0, 0)
    ring.scatter_rest(KV, 4)
    ring.scatter_rest(STATE, 4)
    ring.scatter_rest(FFN, 3)
    ring.scatter_step(Z, 1)
    ring.scatter_step(MIXED, 2)

    own_keys = ring.scatter_end(KV)
    unturned_keys = unturned(own_keys)
    zero = jnp.zeros((rows, LANES), f32)
    d_keys = jnp.where(low_half, unturned_keys, 0.0)
    d_values = jnp.where(low_half, 0.0, own_keys)
    d_keys = jnp.where(first_head, d_keys, half_turned(d_keys))
    d_values = jnp.where(first_head, half_turned(d_values), d_values)
    d_end = ring.scatter_end(STATE)
    d_end_b = d_end.astype(bf16)
    tail = r.tail[...]
    from_end = dot(r.b_mat[...], d_end_b, 1, 1)
    d_x = r.d_x[...] + from_end * tail
    d_tail = head_sums(from_end * r.x_conv[...])
    r.d_b[...] = r.d_b[...] + dot(r.x_tail[...], d_end_b)
    cumulative = r.cumulative[...]
    step_size = r.step_size[...]
    last = cumulative[rows - 1 : rows, :]
    tail_decay = jnp.exp(last - cumulative)
    through = d_tail * tail_decay * step_size
    held = jnp.sum(d_end * r.start_state[...], axis=1, keepdims=True)
    head_row = lax.broadcasted_iota(jnp.int32, (inner, LANES), 0)
    held_heads = jnp.sum(
        jnp.where(lax.div(head_row, SH) == lanes_of((inner, LANES)), held, 0.0),
        axis=0,
        keepdims=True,
    )
    d_last = jnp.sum(through, axis=0, keepdims=True) + jnp.exp(last) * held_heads
    tick_row = lax.broadcasted_iota(jnp.int32, (rows, LANES), 0)
    d_cum = r.d_cum[...] + r.d_cum_rows[...].T - through
    d_cum = d_cum + jnp.where(tick_row == rows - 1, d_last, 0.0)
    d_step = r.d_rows[...].T + d_tail * tail_decay
    rate = -jnp.exp(r.head_rows[1:2, :])
    upto = (tick_s >= tick_t).astype(f32)
    d_log_decay = dot(upto, d_cum, precision=highest)
    d_step = d_step + d_log_decay * rate
    d_dt = d_step * sigmoid(r.dt_in[...] + r.head_rows[0:1, :])
    d_dt = jnp.where(lane_h < heads, d_dt, 0.0)
    r.d_dt[...] = d_dt[:, :HALO].astype(bf16)
    dt_grad = dot(r.d_dt[...], r.normed[pl.ds(HALO, rows), :], 0, 0)
    for k in range(count):
        r.p_dt[k] = dt_grad[:, k * depth : (k + 1) * depth]
    dt_parts = []
    for k, other in enumerate(others):
        target = lax.rem(seq + k + 1, count)
        copy = remote(
            r.p_dt.at[target], r.s_dt.at[seq], r.dt_sems.at[2, k], r.dt_sems.at[3, k], other
        )
        copy.start()
        dt_parts.append(copy)
    small_at = 2 * chunks + CONVK * (inner // LANES + bc_width // LANES)
    r.small[small_at : small_at + 1, :] = jnp.sum(d_dt, axis=0, keepdims=True)
    r.small[small_at + 1 : small_at + 2, :] = (
        jnp.sum(d_log_decay * step_size, axis=0, keepdims=True) * rate
    )
    r.small[small_at + 2 : small_at + 3, :] = skip_grad

    def silu_back(grad, pre):
        opened = sigmoid(pre)
        return grad * opened * (1.0 + pre * (1.0 - opened))

    pad = jnp.zeros((HALO, inner), f32)
    pad_bc = jnp.zeros((HALO, bc_width), f32)
    r.x_back[pl.ds(0, HALO), :] = pad
    r.x_back[pl.ds(HALO, rows), :] = silu_back(d_x, r.x_pre[...])
    r.x_back[pl.ds(HALO + rows, HALO), :] = pad
    d_bc = jnp.concatenate([r.d_b[...], r.d_c[...]], axis=1)
    r.bc_back[pl.ds(0, HALO), :] = pad_bc
    r.bc_back[pl.ds(HALO, rows), :] = silu_back(d_bc, r.bc_pre[...])
    r.bc_back[pl.ds(HALO + rows, HALO), :] = pad_bc

    def back(source, taps, start, length):
        running = taps[0:1, :] * source[pl.ds(start + EDGE, length), :]
        for k in range(1, CONVK):
            running = running + taps[k : k + 1, :] * source[pl.ds(start + EDGE - k, length), :]
        return running

    r.edge_out[:, pl.ds(0, inner)] = back(r.x_back, r.conv_x[...], 0, HALO)
    r.edge_out[:, pl.ds(inner, bc_width)] = back(r.bc_back, r.conv_bc[...], 0, HALO)
    edge = remote(r.edge_out, r.edge_in, r.edge_sems.at[2], r.edge_sems.at[3], preceding)
    edge.start()
    ring.scatter_rest(DOWN, 3)
    ring.scatter_step(Z, 2)
    r.part3[pl.ds(rows, 2 * HALO), :] = jnp.zeros((2 * HALO, r.part3.shape[1]), f32)
    for k in range(CONVK):
        x_tap = jnp.sum(
            r.x_back[pl.ds(HALO, rows), :] * r.x_rows[pl.ds(HALO - EDGE + k, rows), :],
            axis=0,
            keepdims=True,
        )
        for m in range(inner // LANES):
            at = 2 * chunks + k * (inner // LANES) + m
            r.small[at : at + 1, :] = x_tap[:, m * LANES : (m + 1) * LANES]
        r.part3[rows + k : rows + k + 1, pl.ds(0, bc_width)] = jnp.sum(
            r.bc_back[pl.ds(HALO, rows), :] * r.bc_rows[pl.ds(HALO - EDGE + k, rows), :],
            axis=0,
            keepdims=True,
        )
    d_x_in = back(r.x_back, r.conv_x[...], HALO, rows)
    d_bc_in = back(r.bc_back, r.conv_bc[...], HALO, rows)
    edge.wait_recv()
    edges = jnp.where(seq < count - 1, r.edge_in[...], 0.0)
    above = rows - HALO
    r.d_x_b[pl.ds(0, above), :] = d_x_in[:above].astype(bf16)
    r.d_x_b[pl.ds(above, HALO), :] = (d_x_in[above:] + edges[:, :inner]).astype(
        bf16
    )
    r.d_blocks[pl.ds(0, above), pl.ds(0, bc_width)] = d_bc_in[:above]
    r.d_blocks[pl.ds(above, HALO), pl.ds(0, bc_width)] = d_bc_in[above:] + edges[:, inner:]
    r.d_blocks[:, pl.ds(bc_width, LANES)] = d_keys
    r.d_blocks[:, pl.ds(bc_width + LANES, LANES)] = d_values
    block_sum.begin()

    fill(X, r.normed[own_normed, :], r.d_x_b[...])
    ring.scatter_step(X, 0)
    block_sum.middle()
    r.part3[pl.ds(0, rows), :] = dot(r.d_z[...], r.f_z[...].reshape(width, inner), 1, 1) + dot(
        r.d_x_b[...], r.f_x[...].reshape(width, inner), 1, 1
    )
    r.d_rest[:, pl.ds(LANES, LANES)] = block_sum.result().astype(bf16)
    r.part3[pl.ds(0, rows), :] = r.part3[pl.ds(0, rows), :] + dot(
        r.d_rest[...], r.f_rest[...].reshape(width, r.f_rest.shape[2]), 1, 1
    )
    for k in range(count):
        at = (pl.ds(0, rows), pl.ds(k * depth, depth))
        r.part3[at] = r.part3[at] + dot(r.d_dt[...], r.f_dt[k])
    shared_sum.begin()
    fill(REST, r.normed[own_normed, :], r.d_rest[...])
    ring.scatter_step(REST, 0)
    ring.scatter_step(X, 1)
    shared_sum.middle()
    ring.scatter_rest(MIXED, 3)
    ring.scatter_rest(Z, 3)
    ring.scatter_step(REST, 1)
    ring.scatter_step(X, 2)
    shared_sum.finish()
    ring.scatter_step(REST, 2)
    shared_sum.arrived()
    bc_taps = r.total3[pl.ds(rows, 2 * CONVK), pl.ds(0, bc_width)]
    for k in range(CONVK):
        for m in range(bc_width // LANES):
            at = 2 * chunks + CONVK * (inner // LANES) + k * (bc_width // LANES) + m
            r.small[at : at + 1, :] = bc_taps[k : k + 1, m * LANES : (m + 1) * LANES]
    d_normed = r.total3[pl.ds(0, rows), :]
    tokens_wide = r.tokens[...].astype(f32)
    scale_mix = rms_scale(tokens_wide)
    tokens_hat = tokens_wide * scale_mix
    weighted = d_normed * r.gain_mix[...]
    r.grad_tokens[...] = r.d_hidden[...] + scale_mix * (
        weighted - tokens_hat * jnp.mean(weighted * tokens_hat, axis=-1, keepdims=True)
    )
    gain_mix_grad = jnp.sum(d_normed * tokens_hat, axis=0, keepdims=True)
    for k in range(chunks):
        r.small[k : k + 1, :] = gain_mix_grad[:, k * LANES : (k + 1) * LANES]
    used = small_at + 3
    r.small[used:SMALL_ROWS, :] = jnp.zeros((SMALL_ROWS - used, LANES), f32)
    small_copies = []
    for offset in range(1, count):
        copy = remote(
            r.small,
            r.small_slots.at[seq],
            r.small_send.at[offset - 1],
            r.small_receive.at[offset - 1],
            others[offset - 1],
        )
        copy.start()
        small_copies.append(copy)
    ring.scatter_rest(REST, 3)
    ring.scatter_rest(X, 3)
    r.output[...] = (r.hidden[:, output_sum.kept] + output_sum.result()).astype(bf16)
    for name in (DOWN, FFN, MIXED, Z):
        getattr(r, "g_" + name)[...] = ring.scatter_end(name)
    own_rest = ring.scatter_end(REST)
    r.g_blocks[wa] = own_rest[:, LANES : 2 * LANES]
    block_grads.begin()
    r.g_rest[...] = own_rest[:, :LANES]
    for copy in dt_parts:
        copy.wait()
    r.s_dt[pl.ds(seq, 1)] = r.p_dt[pl.ds(seq, 1)]
    dt_total = r.s_dt[0]
    for other in range(1, count):
        dt_total = dt_total + r.s_dt[other]
    r.g_dt[...] = dt_total
    for copy in small_copies:
        copy.wait()
    r.small_slots[pl.ds(seq, 1)] = r.small[...][None]
    total = r.small_slots[0]
    for other in range(1, count):
        total = total + r.small_slots[other]
    r.small_sum[...] = total
    block_grads.forward()
    r.g_x[...] = ring.scatter_end(X)
    block_grads.arrived()

    halo.wait_send()
    for copy in dt_sends:
        copy.wait_send()
    edge.wait_send()
    for name in GATHERED[:6]:
        ring.gather_sent(name)
    for name in SCATTERED:
        ring.scatter_sent(name)
    for sums in (hnormed_sum, shared_sum, output_sum, block_sum, projected, block_grads):
        sums.sent()


def finish_kernel(*refs):
    output_in, tokens_in, small, g_z, g_x, g_rest, g_dt, g_blocks = refs[:8]
    g_mixed, g_ffn, g_down = refs[8:11]
    z, x, bc, dt, out, q, kv, o, gate, up, down = refs[11:22]
    output, grad_tokens, gain_mix, gain_ffn, conv_x, conv_bc, dt_bias, a_log, d_skip = refs[22:]
    output[...] = output_in[...]
    grad_tokens[...] = tokens_in[...]
    inner = z.shape[1]
    z[...] = g_z[...]
    x[...] = g_x[...]
    q[...] = g_rest[...]
    dt[...] = g_dt[pl.ds(0, dt.shape[0]), :]
    for k in range(2):
        bc[:, pl.ds(k * LANES, LANES)] = g_blocks[k]
        kv[:, pl.ds(k * LANES, LANES)] = g_blocks[2 + k]
    ffn_width = gate.shape[1]
    gate[...] = g_ffn[:, pl.ds(0, ffn_width)]
    up[...] = g_ffn[:, pl.ds(ffn_width, ffn_width)]
    out[...] = g_mixed[:, pl.ds(0, inner)].T
    o[...] = g_mixed[:, pl.ds(inner, LANES)].T
    down[...] = g_down[...].T
    sums = small[...]
    at = 0
    for target in (gain_mix, gain_ffn):
        for k in range(target.shape[0] // LANES):
            target[pl.ds(k * LANES, LANES)] = sums[at]
            at += 1
    for target in (conv_x, conv_bc):
        for k in range(CONVK):
            for m in range(target.shape[1] // LANES):
                target[k : k + 1, pl.ds(m * LANES, LANES)] = sums[at : at + 1]
                at += 1
    for target in (dt_bias, a_log, d_skip):
        target[...] = sums[at, : target.shape[0]]
        at += 1


def per_device(
    tokens,
    gain_mix,
    w_z,
    w_x,
    w_bc,
    w_dt,
    conv_x,
    conv_bc,
    dt_bias,
    a_log,
    d_skip,
    w_out,
    w_q,
    w_kv,
    w_o,
    gain_ffn,
    w_gate,
    w_up,
    w_down,
    cotangent,
):
    count = lax.axis_size("seq")
    rows, width = tokens.shape
    depth = w_z.shape[0]
    inner = w_z.shape[1]
    heads = a_log.shape[0]
    ffn = w_gate.shape[1]
    bc_width = w_bc.shape[1]
    lane = np.arange(LANES) % (HD // 2)
    frequency = (ROPE_BASE ** (-(lane * 2.0 / HD))).astype(np.float32)[None]
    inputs = dict(
        tokens=tokens,
        gain_mix=gain_mix[None],
        w_z=w_z,
        w_x=w_x,
        w_bc=w_bc,
        w_dt=w_dt.T,
        conv_x=conv_x,
        conv_bc=conv_bc,
        dt_bias=dt_bias[None],
        a_log=a_log[None],
        d_skip=d_skip[None],
        w_out=w_out,
        w_q=w_q,
        w_kv=w_kv,
        w_o=w_o,
        gain_ffn=gain_ffn[None],
        w_gate=w_gate,
        w_up=w_up,
        w_down=w_down,
        cotangent=cotangent,
        frequency=jnp.asarray(frequency),
    )
    rest = 2 * LANES
    mixed = inner + w_o.shape[0]

    def shape(*dims, dtype=f32):
        return jax.ShapeDtypeStruct(dims, dtype)

    outputs = dict(
        output=shape(rows, width // 4, dtype=bf16),
        grad_tokens=shape(rows, width),
        small_sum=shape(SMALL_ROWS, LANES),
        g_z=shape(depth, inner),
        g_x=shape(depth, inner),
        g_rest=shape(depth, LANES),
        g_dt=shape(HALO, depth),
        g_blocks=shape(4, depth, LANES),
        g_mixed=shape(depth, mixed),
        g_ffn=shape(depth, 2 * ffn),
        g_down=shape(depth, ffn),
    )
    scratch = {}

    def room(dtype, **shapes):
        for name, dims in shapes.items():
            scratch[name] = pltpu.VMEM(dims, dtype)

    pieces = dict(
        z=(depth, inner),
        x=(depth, inner),
        rest=(depth, rest),
        mixed=(depth, mixed),
        ffn=(depth, 2 * ffn),
        down=(depth, ffn),
        kv=(rows, LANES),
        state=(inner + 2 * HALO, LANES),
    )
    for name, dims in pieces.items():
        scratch["f_" + name] = pltpu.VMEM((count, *dims), bf16)
        if name == STATE:
            dims = (inner, LANES)
        if name not in (KV, STATE):
            scratch["p_" + name] = pltpu.VMEM((count, *dims), SUM_TYPE)
        scratch["s_" + name] = pltpu.VMEM((2, count // 2 - 1, *dims), SUM_TYPE)
        scratch["e_" + name] = pltpu.VMEM(dims, SUM_TYPE)
        scratch["h_" + name] = pltpu.VMEM((2, *dims), SUM_TYPE)
    tall, half = rows + 2 * HALO, rows // 2
    whole, wide, head, square = (rows, width), (rows, inner), (rows, LANES), (rows, rows)
    quarter, narrow, across = (rows, width // 4), (LANES, rows), (inner, NS)
    room(f32, part1=whole, total1=whole, near1=(half, width))
    room(f32, part3=(tall, width), total3=(tall, width), near3=(tall // 2, width))
    room(SUM_TYPE, fars1=(half, width), far1=(half, width), far2=(half, width))
    room(SUM_TYPE, fars3=(tall // 2, width), far3=(tall // 2, width))
    room(bf16, halo=(HALO, width), normed=(rows + HALO, width))
    room(f32, bc_rows=(rows + HALO, bc_width), x_rows=(rows + HALO, inner), bc_pre=(rows, bc_width))
    room(bf16, q_pad=(2 * rows, LANES), do_pad=(2 * rows, LANES))
    room(f32, dt_in=head, step_size=head, cumulative=head, d_cum=head, d_b=head, d_c=head)
    room(f32, z_proj=wide, x_pre=wide, x_conv=wide, tail=wide, ssm=wide)
    room(f32, grown=wide, carried=wide, d_x=wide)
    room(bf16, b_mat=(rows, NS), c_mat=(rows, NS), x_tail=wide, x_bf=wide)
    room(f32, cum_t=narrow, step_t=narrow, d_rows=narrow, d_cum_rows=narrow, d_overlap=square)
    room(bf16, mixing=(heads, rows, rows), mixed=(rows, mixed))
    room(f32, row_max=(2 * rows, 1), row_sum=(2 * rows, 1), delta=(2 * rows, 1))
    room(f32, attn_acc=(2 * rows, LANES), factors=(max(8, count), LANES))
    room(f32, start_state=across, direct=across)
    room(f32, hidden=whole, d_hidden=whole, ffn_part=whole)
    room(bf16, hnormed=whole, d_hidden_b=whole, d_ffn=(rows, 2 * ffn), activated=(rows, ffn))
    room(f32, ffn_near=(2, *quarter), blocks=(4, rows + HALO, LANES))
    room(SUM_TYPE, ffn_send=quarter, ffn_far=quarter, block_send=head, block_far=head)
    room(f32, d_blocks=(rows, 4 * LANES), block_near=(2, rows, LANES))
    room(bf16, f_dt=(count, HALO, depth), d_dt=(rows, HALO))
    room(f32, dt_pad=(HALO, depth), p_dt=(count, HALO, depth), s_dt=(count, HALO, depth))
    room(bf16, d_z=wide, d_x_b=wide, d_rest=(rows, rest))
    room(f32, x_back=(tall, inner), bc_back=(tall, bc_width))
    room(f32, edge_out=(HALO, inner + bc_width), edge_in=(HALO, inner + bc_width))
    room(f32, cosine=head, sine=head, head_rows=(8, LANES), skip_row=(1, inner))
    room(f32, small=(SMALL_ROWS, LANES), small_slots=(count, SMALL_ROWS, LANES))
    sems = pltpu.SemaphoreType.DMA
    ring, pairwise, trio = (len(GATHERED), 2, count // 2), (3, 3, 4), (2, 3)
    scratch |= dict(
        gather_send=sems(ring),
        gather_receive=sems(ring),
        scatter_send=sems(ring),
        scatter_receive=sems(ring),
        wa_send=sems(pairwise),
        wa_receive=sems(pairwise),
        edge_sems=sems((4,)),
        dt_sems=sems((4, count - 1)),
        ffn_sems=sems(trio),
        block_sems=sems(trio),
        share_sems=sems(trio),
        grad_sems=sems(trio),
        small_send=sems((count - 1,)),
        small_receive=sems((count - 1,)),
    )
    vmem = pl.BlockSpec(memory_space=pltpu.VMEM)
    results = pl.pallas_call(
        functools.partial(layer_kernel, count, (*inputs, *outputs, *scratch)),
        out_shape=list(outputs.values()),
        in_specs=[vmem] * len(inputs),
        out_specs=[vmem] * len(outputs),
        scratch_shapes=list(scratch.values()),
        compiler_params=pltpu.CompilerParams(
            collective_id=0, has_side_effects=True, vmem_limit_bytes=VMEM_LIMIT
        ),
    )(*inputs.values())
    placed = [w_z, w_x, w_bc, w_dt.T, w_out, w_q, w_kv, w_o, w_gate, w_up, w_down]
    vectors = [gain_mix, gain_ffn, conv_x, conv_bc, dt_bias, a_log, d_skip]
    kinds = [shape(*w.shape) for w in placed] + [jax.ShapeDtypeStruct(v.shape, v.dtype) for v in results[:2]]
    kinds += [shape(*v.shape) for v in vectors]
    finished = pl.pallas_call(
        finish_kernel,
        out_shape=kinds,
        in_specs=[vmem] * len(results),
        out_specs=[vmem] * len(kinds),
        compiler_params=pltpu.CompilerParams(vmem_limit_bytes=VMEM_LIMIT),
    )(*results)
    g_z, g_x, g_bc, g_dt, g_out, g_q, g_kv, g_o, g_gate, g_up, g_down = finished[:11]
    output, grad_tokens, g_gain_mix, g_gain_ffn, *rest_grads = finished[11:]
    return (
        output,
        grad_tokens,
        g_gain_mix,
        g_z,
        g_x,
        g_bc,
        g_dt.T,
        *rest_grads,
        g_out,
        g_q,
        g_kv,
        g_o,
        g_gain_ffn,
        g_gate,
        g_up,
        g_down,
    )


def solution(mesh):
    placed = (
        P("seq", None),
        P(),
        P("seq", "wa"),
        P("seq", "wa"),
        P("seq", None),
        P("seq", "wa"),
        P(None, "wa"),
        P(),
        P("wa"),
        P("wa"),
        P("wa"),
        P("wa", "seq"),
        P("seq", "wa"),
        P("seq", None),
        P("wa", "seq"),
        P(),
        P("seq", "wa"),
        P("seq", "wa"),
        P("wa", "seq"),
        P("seq", None),
    )
    return jax.shard_map(
        per_device,
        mesh=mesh,
        in_specs=placed,
        out_specs=(
            P("seq", "wa"),
            P("seq", None),
            P(),
            P("seq", "wa"),
            P("seq", "wa"),
            P("seq", None),
            P("seq", "wa"),
            P(None, "wa"),
            P(),
            P("wa"),
            P("wa"),
            P("wa"),
            P("wa", "seq"),
            P("seq", "wa"),
            P("seq", None),
            P("wa", "seq"),
            P(),
            P("seq", "wa"),
            P("seq", "wa"),
            P("wa", "seq"),
        ),
        check_vma=False,
    )
```

```python
import functools
import types

import jax
import jax.numpy as jnp
import numpy as np
from jax import lax
from jax.experimental import pallas as pl
from jax.experimental.pallas import tpu as pltpu
from jax.sharding import PartitionSpec as P

NS = 128
CONVK = 4
QH = 8
KVH = 2
HD = 64
SH = 64
HALO = 16
LANES = 128
EPS = 1e-05
ROPE_BASE = 100000000000.0
MASKED = -1e30
SUM_TYPE = jnp.bfloat16
MESH = pl.DeviceIdType.MESH
VMEM_LIMIT = 62 * 1024 * 1024
EDGE = CONVK - 1
f32 = jnp.float32
bf16 = jnp.bfloat16
highest = lax.Precision.HIGHEST

Z, X, REST, MIXED, FFN, DOWN, KV, STATE = GATHERED = (
    "z",
    "x",
    "rest",
    "mixed",
    "ffn",
    "down",
    "kv",
    "state",
)
SCATTERED = GATHERED


def ring_place(index, count):
    odd = lax.rem(index, 2)
    half = lax.div(index, 2)
    return (1 - odd) * half + odd * (count - 1 - half)


def ring_index(place, count):
    place = lax.rem(place + 2 * count, count)
    upper = lax.div(place, count // 2)
    return (1 - upper) * 2 * place + upper * (2 * (count - place) - 1)


def dot(left, right, left_dim=1, right_dim=0, precision=None):
    return lax.dot_general(
        left,
        right,
        (((left_dim,), (right_dim,)), ((), ())),
        precision=precision,
        preferred_element_type=f32,
    )


def remote(source, target, send, receive, peer):
    return pltpu.make_async_remote_copy(
        src_ref=source,
        dst_ref=target,
        send_sem=send,
        recv_sem=receive,
        device_id=peer,
        device_id_type=MESH,
    )


def sigmoid(values):
    return 1.0 / (1.0 + jnp.exp(-values))


def softplus(values):
    return jnp.maximum(values, 0.0) + jnp.log1p(jnp.exp(-jnp.abs(values)))


def rms_scale(rows):
    return lax.rsqrt(jnp.mean(rows * rows, axis=-1, keepdims=True) + EPS)


def lanes_of(shape):
    return lax.broadcasted_iota(jnp.int32, shape, 1)


def swapped(values):
    lane = lax.rem(lanes_of(values.shape), HD)
    ahead = pltpu.roll(values, LANES - HD // 2, 1)
    behind = pltpu.roll(values, HD // 2, 1)
    return jnp.where(lane < HD // 2, ahead, behind)


def half_turned(values):
    return pltpu.roll(values, HD, 1)


class Ring:
    def __init__(self, count, bufs, parts, slots, halves, holds, sems):
        self.count = count
        self.steps = count // 2
        self.seq = lax.axis_index("seq")
        self.place = ring_place(self.seq, count)
        self.sides = [
            {"seq": ring_index(self.place + 1, count)},
            {"seq": ring_index(self.place - 1, count)},
        ]
        self.bufs, self.parts, self.slots = bufs, parts, slots
        self.halves, self.holds = halves, holds
        self.gather_send, self.gather_receive, self.send, self.receive = sems

    def owner(self, offset):
        return ring_index(self.place + offset, self.count)

    def gather_copy(self, name, side, step, arriving):
        c = GATHERED.index(name)
        back = step + 1 if arriving else step
        owner = self.owner(back if side else -back)
        buf = self.bufs[name]
        if step < self.steps - 1:
            piece = buf.at[owner]
        else:
            rows = buf.shape[1] // 2
            piece = buf.at[owner, pl.ds(side * rows, rows)]
        return remote(
            piece,
            piece,
            self.gather_send.at[c, side, step],
            self.gather_receive.at[c, side, step],
            self.sides[side],
        )

    def gather_step(self, name, step):
        for side in range(2):
            if step:
                self.gather_copy(name, side, step - 1, True).wait_recv()
            self.gather_copy(name, side, step, False).start()

    def gather_rest(self, name, first):
        for step in range(first, self.steps):
            self.gather_step(name, step)

    def gather_end(self, name):
        for side in range(2):
            self.gather_copy(name, side, self.steps - 1, True).wait_recv()

    def gather_sent(self, name):
        for side in range(2):
            for step in range(self.steps):
                self.gather_copy(name, side, step, False).wait_send()

    def mine(self, name, side, step):
        rows = self.halves[name].shape[0]
        return self.parts[name].at[self.owner(-step if side else step), pl.ds(0, rows)]

    def slot(self, name, side, step):
        if step < self.steps:
            return self.slots[name].at[side, step - 1]
        rows = self.halves[name].shape[0] // 2
        return self.halves[name].at[pl.ds(side * rows, rows)]

    def scatter_copy(self, name, side, step):
        c = SCATTERED.index(name)
        if step == self.steps:
            rows = self.halves[name].shape[0] // 2
            origin = self.mine(name, side, step).at[pl.ds(side * rows, rows)]
        elif step == self.steps - 1:
            origin = self.holds[name].at[side]
        else:
            origin = self.slot(name, side, step + 1)
        return remote(
            origin,
            self.slot(name, side, step),
            self.send.at[c, side, step - 1],
            self.receive.at[c, side, step - 1],
            self.sides[side],
        )

    def scatter_step(self, name, turn):
        step = self.steps - turn
        rows = self.halves[name].shape[0] // 2
        for side in range(2):
            if turn:
                self.scatter_copy(name, side, step + 1).wait_recv()
                own = self.mine(name, side, step)
                slot = self.slot(name, side, step + 1)
                if turn == 1:
                    hold = self.holds[name].at[side]
                    near = pl.ds(side * rows, rows)
                    away = pl.ds((1 - side) * rows, rows)
                    hold[away, :] = own[away, :]
                    hold[near, :] = (own[near, :].astype(f32) + slot[...].astype(f32)).astype(
                        hold.dtype
                    )
                else:
                    slot[...] = (own[...].astype(f32) + slot[...].astype(f32)).astype(slot.dtype)
            self.scatter_copy(name, side, step).start()

    def scatter_rest(self, name, first):
        for turn in range(first, self.steps):
            self.scatter_step(name, turn)

    def scatter_end(self, name):
        for side in range(2):
            self.scatter_copy(name, side, 1).wait_recv()
        slots = self.slots[name]
        total = (
            self.parts[name][self.seq, pl.ds(0, self.halves[name].shape[0])].astype(f32)
            + slots[0, 0].astype(f32)
            + slots[1, 0].astype(f32)
        )
        return total

    def scatter_sent(self, name):
        for side in range(2):
            for step in range(1, self.steps + 1):
                self.scatter_copy(name, side, step).wait_send()


class Across:
    def __init__(self, value, out, near, far_send, far, send, receive, index, pieces):
        self.wa = lax.axis_index("wa")
        self.core = lax.rem(self.wa, 2)
        self.row = lax.div(self.wa, 2)
        self.mate = {"wa": 2 * self.row + 1 - self.core}
        self.across = {"wa": 2 * (1 - self.row) + self.core}
        self.value, self.out, self.near, self.far_send, self.far = value, out, near, far_send, far
        self.send, self.receive, self.index, self.pieces = send, receive, index, pieces
        self.rows = value.shape[0] // 2
        self.step = self.rows // pieces

    def half(self, core, p):
        return pl.ds(pl.multiple_of(core * self.rows + p * self.step, self.step), self.step)

    def sems(self, stage, p):
        return (self.send.at[self.index, stage, p], self.receive.at[self.index, stage, p])

    def first(self, p):
        at = pl.ds(p * self.step, self.step)
        return remote(
            self.value.at[self.half(1 - self.core, p)],
            self.near.at[at],
            *self.sems(0, p),
            self.mate,
        )

    def second(self, p):
        at = pl.ds(p * self.step, self.step)
        return remote(self.far_send.at[at], self.far.at[at], *self.sems(1, p), self.across)

    def third(self, p, arriving):
        at = self.half(1 - self.core if arriving else self.core, p)
        return remote(self.out.at[at], self.out.at[at], *self.sems(2, p), self.mate)

    def begin(self):
        for p in range(self.pieces):
            self.first(p).start()

    def middle(self):
        for p in range(self.pieces):
            self.first(p).wait_recv()
            at = pl.ds(p * self.step, self.step)
            own = self.half(self.core, p)
            self.far_send[at, :] = (self.value[own, :] + self.near[at, :]).astype(SUM_TYPE)
            self.second(p).start()

    def finish(self):
        for p in range(self.pieces):
            self.second(p).wait_recv()
            at = pl.ds(p * self.step, self.step)
            own = self.half(self.core, p)
            self.out[own, :] = self.far_send[at, :].astype(f32) + self.far[at, :].astype(f32)
            self.third(p, False).start()

    def arrived(self):
        for p in range(self.pieces):
            self.third(p, True).wait_recv()

    def sent(self):
        for p in range(self.pieces):
            self.first(p).wait_send()
            self.second(p).wait_send()
            self.third(p, False).wait_send()


class Split:
    def __init__(self, value, near, far_send, far, sems, wa):
        core, row = lax.rem(wa, 2), lax.div(wa, 2)
        mate, across = {"wa": 2 * row + 1 - core}, {"wa": 2 * (1 - row) + core}
        self.value, self.near, self.far_send, self.far, self.row = value, near, far_send, far, row
        wide = far.shape[1]

        def columns(block):
            return pl.ds(pl.multiple_of(block * wide, LANES), wide)

        self.kept, self.theirs = columns(2 * row + core), columns(2 * (1 - row) + core)
        self.firsts = [
            remote(
                value.at[:, columns(2 * k + 1 - core)], near.at[k], sems.at[0, k], sems.at[1, k], mate
            )
            for k in range(2)
        ]
        self.second = remote(far_send, far, sems.at[0, 2], sems.at[1, 2], across)

    def begin(self):
        for copy in self.firsts:
            copy.start()

    def middle(self):
        for copy in self.firsts:
            copy.wait_recv()
        self.far_send[...] = (self.value[:, self.theirs] + self.near[1 - self.row]).astype(SUM_TYPE)
        self.second.start()

    def result(self):
        self.second.wait_recv()
        return self.value[:, self.kept] + self.near[self.row] + self.far[...].astype(f32)

    def sent(self):
        for copy in self.firsts:
            copy.wait_send()
        self.second.wait_send()


class Share:
    def __init__(self, buf, sems, wa):
        core, row = lax.rem(wa, 2), lax.div(wa, 2)
        mate, across = 2 * row + 1 - core, 2 * (1 - row) + core

        def copy(block, k, peer):
            return remote(buf.at[block], buf.at[block], sems.at[0, k], sems.at[1, k], {"wa": peer})

        self.sends = [copy(wa, 0, across), copy(wa, 1, mate), copy(across, 2, mate)]
        self.arrivals = [
            copy(across, 0, across), copy(mate, 1, mate), copy(2 * (1 - row) + 1 - core, 2, mate)
        ]

    def begin(self):
        self.sends[0].start()
        self.sends[1].start()

    def forward(self):
        self.arrivals[0].wait_recv()
        self.sends[2].start()

    def arrived(self):
        self.arrivals[1].wait_recv()
        self.arrivals[2].wait_recv()

    def sent(self):
        for copy in self.sends:
            copy.wait_send()


SMALL_ROWS = 40


def layer_kernel(count, names, *refs):
    r = types.SimpleNamespace(**dict(zip(names, refs)))
    seq = lax.axis_index("seq")
    wa = lax.axis_index("wa")
    rows, width = r.tokens.shape
    inner = r.w_z.shape[1]
    heads = inner // SH
    pairs = heads // 2
    lane_h = lanes_of((rows, LANES))
    low_half = lane_h < HD
    kv_head = lax.div(wa * (r.w_q.shape[1] // HD), QH // KVH)

    def family(prefix):
        return {name: getattr(r, prefix + name) for name in GATHERED}

    r.p_kv, r.p_state = r.f_kv, r.f_state

    ring = Ring(
        count,
        *(family(prefix) for prefix in ("f_", "p_", "s_", "e_", "h_")),
        (r.gather_send, r.gather_receive, r.scatter_send, r.scatter_receive),
    )
    hidden_sum = Across(r.part1, r.total1, r.near1, r.fars1, r.far1, r.wa_send, r.wa_receive, 0, 4)
    hnormed_sum = Across(r.part1, r.total1, r.near1, r.fars1, r.far2, r.wa_send, r.wa_receive, 1, 4)
    shared_sum = Across(r.part3, r.total3, r.near3, r.fars3, r.far3, r.wa_send, r.wa_receive, 2, 3)
    mate, across = hidden_sum.mate, hidden_sum.across
    output_sum = Split(r.ffn_part, r.ffn_near, r.ffn_send, r.ffn_far, r.ffn_sems, wa)
    block_sum = Split(r.d_blocks, r.block_near, r.block_send, r.block_far, r.block_sems, wa)
    projected = Share(r.blocks, r.share_sems, wa)
    block_grads = Share(r.g_blocks, r.grad_sems, wa)
    others = [{"seq": lax.rem(seq + offset, count)} for offset in range(1, count)]
    following, preceding = others[0], others[-1]
    barrier = pltpu.get_barrier_semaphore()
    peers = others + [mate, across]
    for peer in peers:
        pl.semaphore_signal(barrier, inc=1, device_id=peer, device_id_type=MESH)

    r.f_z[seq] = r.w_z[...]
    r.f_x[seq] = r.w_x[...]
    depth = r.w_out.shape[1]
    eye = (
        lax.broadcasted_iota(jnp.int32, (depth, depth), 0) == lanes_of((depth, depth))
    ).astype(bf16)
    own_columns = jnp.where(
        wa < 2,
        jnp.where(wa == 0, r.w_bc[:, pl.ds(0, LANES)], r.w_bc[:, pl.ds(LANES, LANES)]),
        jnp.where(wa == 2, r.w_kv[:, pl.ds(0, LANES)], r.w_kv[:, pl.ds(LANES, LANES)]),
    )
    r.f_rest[seq] = jnp.concatenate([r.w_q[...], own_columns], axis=1)
    r.dt_pad[...] = jnp.zeros_like(r.dt_pad)
    r.dt_pad[pl.ds(0, heads), :] = r.w_dt[...].astype(f32)
    r.f_dt[seq] = r.dt_pad[...].astype(bf16)
    pl.semaphore_wait(barrier, len(peers))
    halo = remote(
        r.tokens.at[pl.ds(rows - HALO, HALO)], r.halo, r.edge_sems.at[0], r.edge_sems.at[1], following
    )
    halo.start()
    dt_sends = [
        remote(r.f_dt.at[seq], r.f_dt.at[seq], r.dt_sems.at[0, k], r.dt_sems.at[1, k], other)
        for k, other in enumerate(others)
    ]
    sources = [lax.rem(seq + count - offset, count) for offset in range(1, count)]
    dt_arrivals = [
        remote(r.f_dt.at[k], r.f_dt.at[k], r.dt_sems.at[0, m], r.dt_sems.at[1, m], others[m])
        for m, k in enumerate(sources)
    ]
    for copy in dt_sends:
        copy.start()
    ring.gather_step(REST, 0)
    ring.gather_step(X, 0)
    ring.gather_step(Z, 0)
    r.f_mixed[seq] = jnp.concatenate(
        [dot(eye, r.w_out[...], 1, 1).astype(bf16), dot(eye, r.w_o[...], 1, 1).astype(bf16)], axis=1
    )
    r.f_down[seq] = dot(eye, r.w_down[...], 1, 1).astype(bf16)
    r.f_ffn[seq] = jnp.concatenate([r.w_gate[...], r.w_up[...]], axis=1)
    tokens_wide = r.tokens[...].astype(f32)
    scale_mix = rms_scale(tokens_wide)
    r.normed[pl.ds(HALO, rows), :] = (tokens_wide * scale_mix * r.gain_mix[...]).astype(bf16)
    halo.wait_recv()
    before = jnp.where(seq > 0, r.halo[...].astype(f32), 0.0)
    r.normed[pl.ds(0, HALO), :] = (before * rms_scale(before) * r.gain_mix[...]).astype(bf16)
    positions = seq * rows + lax.broadcasted_iota(jnp.int32, (rows, LANES), 0)
    angles = positions.astype(f32) * r.frequency[...]
    r.cosine[...] = jnp.cos(angles)
    sine = jnp.sin(angles)
    r.sine[...] = jnp.where(lax.rem(lane_h, HD) < HD // 2, -sine, sine)
    r.head_rows[...] = jnp.zeros_like(r.head_rows)
    for k, source in enumerate((r.dt_bias, r.a_log, r.d_skip)):
        r.head_rows[k : k + 1, pl.ds(0, heads)] = source[...]
    for step in range(1, ring.steps):
        ring.gather_step(REST, step)
        ring.gather_step(X, step)
        ring.gather_step(Z, step)
    ring.gather_step(MIXED, 0)
    ring.gather_step(FFN, 0)
    ring.gather_step(DOWN, 0)

    bc_width = r.conv_bc.shape[1]
    ring.gather_end(REST)
    rest = dot(r.normed[...], r.f_rest[...].reshape(width, r.f_rest.shape[2]))
    r.blocks[wa] = rest[:, LANES : 2 * LANES]
    projected.begin()
    cosine, sine = r.cosine[...], r.sine[...]

    def turned(values):
        return values * cosine + swapped(values) * sine

    def unturned(values):
        return values * cosine - swapped(values) * sine

    q_rot = (turned(rest[HALO:, :LANES]) * HD ** (-0.5)).astype(bf16).astype(f32)
    r.q_pad[pl.ds(0, rows), :] = jnp.where(low_half, q_rot, 0.0).astype(bf16)
    r.q_pad[pl.ds(rows, rows), :] = jnp.where(low_half, half_turned(q_rot), 0.0).astype(bf16)
    for copy in dt_arrivals:
        copy.wait_recv()
    dt_proj = jnp.zeros((rows, HALO), f32)
    for k in range(count):
        normed_part = r.normed[pl.ds(HALO, rows), pl.ds(k * depth, depth)]
        dt_proj = dt_proj + dot(normed_part, r.f_dt[k], 1, 1)
    r.dt_in[...] = jnp.zeros_like(r.dt_in)
    r.dt_in[:, pl.ds(0, HALO)] = dt_proj
    projected.forward()
    ring.gather_end(X)
    r.x_rows[...] = dot(r.normed[...], r.f_x[...].reshape(width, inner))
    projected.arrived()
    keys = turned(r.blocks[2, pl.ds(HALO, rows), :])
    values = r.blocks[3, pl.ds(HALO, rows), :]
    first_head = kv_head == 0
    r.f_kv[seq] = jnp.where(
        low_half,
        jnp.where(first_head, keys, half_turned(keys)),
        jnp.where(first_head, half_turned(values), values),
    ).astype(bf16)
    ring.gather_step(KV, 0)
    r.bc_rows[:, pl.ds(0, LANES)] = r.blocks[0]
    r.bc_rows[:, pl.ds(LANES, LANES)] = r.blocks[1]

    def convolved(source, taps):
        running = taps[0:1, :] * source[pl.ds(HALO - EDGE, rows), :]
        for k in range(1, CONVK):
            running = running + taps[k : k + 1, :] * source[pl.ds(HALO - EDGE + k, rows), :]
        return running

    x_pre = convolved(r.x_rows, r.conv_x[...])
    bc_pre = convolved(r.bc_rows, r.conv_bc[...])
    r.x_pre[...] = x_pre
    r.bc_pre[...] = bc_pre
    x_conv = x_pre * sigmoid(x_pre)
    r.x_conv[...] = x_conv
    bc_conv = bc_pre * sigmoid(bc_pre)
    r.b_mat[...] = bc_conv[:, :NS].astype(bf16)
    r.c_mat[...] = bc_conv[:, NS:].astype(bf16)
    rate = -jnp.exp(r.head_rows[1:2, :])
    step_size = softplus(r.dt_in[...] + r.head_rows[0:1, :])
    r.step_size[...] = step_size
    tick_t = lax.broadcasted_iota(jnp.int32, (rows, rows), 0)
    tick_s = lanes_of((rows, rows))
    causal = tick_t >= tick_s
    cumulative = dot(causal.astype(f32), rate * step_size, precision=highest)
    r.cumulative[...] = cumulative
    r.cum_t[...] = cumulative.T
    r.step_t[...] = step_size.T
    pick_row = lax.broadcasted_iota(jnp.int32, (LANES, inner), 0)
    pick_lane = lax.div(lanes_of((LANES, inner)), SH)
    pick = (pick_row == pick_lane).astype(f32)

    def spread(per_head):
        return dot(per_head, pick, precision=highest)

    def head_sums(wide):
        return dot(wide, pick, 1, 1, precision=highest)

    r.skip_row[...] = spread(r.head_rows[...])[2:3, :]
    last = cumulative[rows - 1 : rows, :]
    tail_decay = jnp.exp(last - cumulative)
    tail = spread(tail_decay * step_size)
    r.tail[...] = tail
    x_tail = (x_conv * tail).astype(bf16)
    r.x_tail[...] = x_tail
    local_state = dot(x_tail, r.b_mat[...], 0, 0)
    high = last.astype(bf16).astype(f32)
    middle = (last - high).astype(bf16).astype(f32)
    low = last - high - middle
    row_of = lax.broadcasted_iota(jnp.int32, (2 * HALO, LANES), 0)
    split_rows = jnp.where(
        row_of == 0, high, jnp.where(row_of == 1, middle, jnp.where(row_of == 2, low, 0.0))
    )
    r.f_state[seq, pl.ds(0, inner), :] = local_state.astype(bf16)
    r.f_state[seq, pl.ds(inner, 2 * HALO), :] = split_rows.astype(bf16)
    ring.gather_step(STATE, 0)
    overlap = dot(r.c_mat[...], r.b_mat[...], 1, 1)
    x_bf = x_conv.astype(bf16)
    r.x_bf[...] = x_bf

    def decays(h):
        gap = r.cumulative[:, h : h + 1] - r.cum_t[h : h + 1, :]
        return jnp.exp(jnp.where(causal, gap, MASKED))

    for p in range(pairs):
        at = pl.ds(p * LANES, LANES)
        outs = []
        for h in (2 * p, 2 * p + 1):
            mixing = (decays(h) * overlap * r.step_t[h : h + 1, :]).astype(bf16)
            r.mixing[h] = mixing
            outs.append(dot(mixing, r.x_bf[:, at]))
        r.ssm[:, at] = jnp.where(low_half, outs[0], outs[1])
        if p == 0:
            ring.gather_step(KV, 1)
            ring.gather_step(STATE, 1)
    ring.gather_step(MIXED, 1)
    ring.gather_step(KV, 2)
    ring.gather_step(STATE, 2)
    ring.gather_step(MIXED, 2)
    ring.gather_rest(KV, 3)
    ring.gather_rest(STATE, 3)
    ring.gather_step(FFN, 1)

    ring.gather_end(KV)
    ring.gather_rest(MIXED, 3)

    def block_scores(block):
        scores = dot(r.q_pad[...], r.f_kv[block], 1, 1)
        shape = (2 * rows, rows)
        query = seq * rows + lax.rem(lax.broadcasted_iota(jnp.int32, shape, 0), rows)
        key = block * rows + lanes_of(shape)
        return jnp.where(key <= query, scores, MASKED)

    r.row_max[...] = jnp.full_like(r.row_max, MASKED)
    r.row_sum[...] = jnp.zeros_like(r.row_sum)
    r.attn_acc[...] = jnp.zeros_like(r.attn_acc)

    def visit(block, carry):
        scores = block_scores(block)
        old = r.row_max[...]
        new = jnp.maximum(old, jnp.max(scores, axis=1, keepdims=True))
        weights = jnp.exp(scores - new)
        shrink = jnp.exp(old - new)
        r.row_sum[...] = r.row_sum[...] * shrink + jnp.sum(weights, axis=1, keepdims=True)
        r.attn_acc[...] = r.attn_acc[...] * shrink + dot(weights.astype(bf16), r.f_kv[block])
        r.row_max[...] = new
        return carry

    middle_block = lax.div(seq + 1, 2)
    lax.fori_loop(0, middle_block, visit, 0)
    ring.gather_step(FFN, 2)
    ring.gather_step(DOWN, 1)
    lax.fori_loop(middle_block, seq + 1, visit, 0)
    attn = r.attn_acc[...] / r.row_sum[...]
    r.row_max[...] = r.row_max[...] + jnp.log(r.row_sum[...])
    attn_out = jnp.where(low_half, half_turned(attn[:rows]), attn[rows:])
    r.mixed[:, pl.ds(inner, LANES)] = attn_out.astype(bf16)

    ring.gather_end(STATE)
    reach = jnp.zeros((1, LANES), f32)
    for block in range(count - 1, -1, -1):
        earlier = block < seq
        r.factors[block : block + 1, :] = jnp.where(earlier, jnp.exp(reach), 0.0)
        totals = jnp.sum(
            r.f_state[block, pl.ds(inner, HALO), :].astype(f32), axis=0, keepdims=True
        )
        reach = reach + jnp.where(earlier, totals, 0.0)
    r.start_state[...] = jnp.zeros_like(r.start_state)

    def tall(per_head_row):
        return jnp.concatenate(
            [jnp.broadcast_to(per_head_row[:, h : h + 1], (SH, NS)) for h in range(heads)], axis=0
        )

    def add_state(block, carry):
        factor = tall(r.factors[pl.ds(block, 1), :])
        r.start_state[...] = r.start_state[...] + factor * r.f_state[
            block, pl.ds(0, inner), :
        ].astype(f32)
        return carry

    lax.fori_loop(0, seq, add_state, 0)
    start_b = r.start_state[...].astype(bf16)
    reached = dot(r.c_mat[...], start_b, 1, 1)
    grown = spread(jnp.exp(r.cumulative[...]))
    r.grown[...] = grown
    carried = reached * grown
    r.carried[...] = carried
    ssm = r.ssm[...] + carried + r.skip_row[...] * r.x_conv[...]
    r.ssm[...] = ssm
    ring.gather_end(Z)
    z_proj = dot(r.normed[pl.ds(HALO, rows), :], r.f_z[...].reshape(width, inner))
    r.z_proj[...] = z_proj
    r.mixed[:, pl.ds(0, inner)] = (ssm * (z_proj * sigmoid(z_proj))).astype(bf16)

    ring.gather_end(MIXED)
    mixed_shape = (width, r.f_mixed.shape[2])
    r.part1[...] = dot(r.mixed[...], r.f_mixed[...].reshape(mixed_shape), 1, 1)
    hidden_sum.begin()
    hidden_sum.middle()
    ring.gather_rest(FFN, 3)
    ring.gather_step(DOWN, 2)
    hidden_sum.finish()
    ring.gather_rest(DOWN, 3)
    down_shape = (width, r.f_down.shape[2])
    ffn_shape = (width, r.f_ffn.shape[2])
    ffn_width = r.f_down.shape[2]
    hidden_sum.arrived()
    hidden_sum.sent()

    hidden = r.tokens[...].astype(f32) + r.total1[...]
    r.hidden[...] = hidden
    scale_ffn = rms_scale(hidden)
    r.hnormed[...] = (hidden * scale_ffn * r.gain_ffn[...]).astype(bf16)
    ring.gather_end(FFN)
    gate_up = dot(r.hnormed[...], r.f_ffn[...].reshape(ffn_shape))
    gate, up = gate_up[:, :ffn_width], gate_up[:, ffn_width:]
    open_gate = sigmoid(gate)
    ring.gather_end(DOWN)
    d_act = dot(r.cotangent[...], r.f_down[...].reshape(down_shape))
    r.d_ffn[:, pl.ds(0, ffn_width)] = (
        d_act * up * open_gate * (1.0 + gate * (1.0 - open_gate))
    ).astype(bf16)
    r.d_ffn[:, pl.ds(ffn_width, ffn_width)] = (d_act * gate * open_gate).astype(bf16)
    r.activated[...] = (gate * open_gate * up).astype(bf16)
    r.part1[...] = dot(r.d_ffn[...], r.f_ffn[...].reshape(ffn_shape), 1, 1)
    hnormed_sum.begin()

    def fill(name, left, right):
        parts = getattr(r, "p_" + name)
        parts[...] = dot(left, right, 0, 0).astype(SUM_TYPE).reshape(parts.shape)

    fill(FFN, r.hnormed[...], r.d_ffn[...])
    ring.scatter_step(FFN, 0)
    hnormed_sum.middle()
    fill(DOWN, r.cotangent[...], r.activated[...])
    ring.scatter_step(DOWN, 0)
    r.ffn_part[...] = dot(r.activated[...], r.f_down[...].reshape(down_shape), 1, 1)
    output_sum.begin()
    ring.scatter_step(FFN, 1)
    hnormed_sum.finish()
    ring.scatter_step(DOWN, 1)
    output_sum.middle()
    hnormed_sum.arrived()

    hidden = r.hidden[...]
    scale_ffn = rms_scale(hidden)
    hidden_hat = hidden * scale_ffn
    d_hnormed = r.total1[...]
    weighted = d_hnormed * r.gain_ffn[...]
    d_hidden = r.cotangent[...].astype(f32) + scale_ffn * (
        weighted - hidden_hat * jnp.mean(weighted * hidden_hat, axis=-1, keepdims=True)
    )
    r.d_hidden[...] = d_hidden
    r.d_hidden_b[...] = d_hidden.astype(bf16)
    fill(MIXED, r.d_hidden_b[...], r.mixed[...])
    ring.scatter_step(MIXED, 0)
    gain_ffn_grad = jnp.sum(d_hnormed * hidden_hat, axis=0, keepdims=True)
    chunks = width // LANES
    for k in range(chunks):
        r.small[chunks + k : chunks + k + 1, :] = gain_ffn_grad[:, k * LANES : (k + 1) * LANES]
    d_mixed = dot(r.d_hidden_b[...], r.f_mixed[...].reshape(mixed_shape))
    d_gated = d_mixed[:, :inner]
    d_attn = d_mixed[:, inner:].astype(bf16).astype(f32)

    r.do_pad[pl.ds(0, rows), :] = jnp.where(low_half, 0.0, half_turned(d_attn)).astype(bf16)
    r.do_pad[pl.ds(rows, rows), :] = jnp.where(low_half, 0.0, d_attn).astype(bf16)
    attn_b = r.mixed[:, pl.ds(inner, LANES)].astype(f32)
    products = d_attn * attn_b
    r.delta[pl.ds(0, rows), :] = jnp.sum(jnp.where(low_half, products, 0.0), axis=1, keepdims=True)
    r.delta[pl.ds(rows, rows), :] = jnp.sum(
        jnp.where(low_half, 0.0, products), axis=1, keepdims=True
    )
    r.attn_acc[...] = jnp.zeros_like(r.attn_acc)
    own_state = pl.ds(0, inner)
    for name in (KV, STATE):
        ring.gather_sent(name)

    def revisit(block, carry):
        probability = jnp.exp(block_scores(block) - r.row_max[...])
        keys_values = r.f_kv[block]
        d_probs = dot(r.do_pad[...], keys_values, 1, 1)
        d_scores = (probability * (d_probs - r.delta[...])).astype(bf16)
        r.attn_acc[...] = r.attn_acc[...] + dot(d_scores, keys_values)
        r.p_kv[block] = (
            dot(d_scores, r.q_pad[...], 0, 0)
            + dot(probability.astype(bf16), r.do_pad[...], 0, 0)
        ).astype(SUM_TYPE)
        return carry

    def blank(block, carry):
        r.p_kv[block] = jnp.zeros_like(r.p_kv[block])
        r.p_state[block, own_state, :] = jnp.zeros((inner, LANES), SUM_TYPE)
        return carry

    back_block = lax.div(seq + 1, 2)
    lax.fori_loop(0, back_block, revisit, 0)
    ring.scatter_step(FFN, 2)
    ring.scatter_step(DOWN, 2)
    lax.fori_loop(back_block, seq + 1, revisit, 0)
    lax.fori_loop(seq + 1, count, blank, 0)
    r.p_state[seq, own_state, :] = jnp.zeros((inner, LANES), SUM_TYPE)
    ring.scatter_step(KV, 0)
    d_q = r.attn_acc[...] * HD ** (-0.5)
    d_q = jnp.where(low_half, d_q[:rows], half_turned(d_q[rows:]))
    r.d_rest[:, pl.ds(0, LANES)] = unturned(d_q).astype(bf16)

    z_proj = r.z_proj[...]
    open_z = sigmoid(z_proj)
    r.d_z[...] = (
        d_gated * r.ssm[...] * open_z * (1.0 + z_proj * (1.0 - open_z))
    ).astype(bf16)
    d_ssm = d_gated * (z_proj * open_z)
    d_grown = d_ssm * r.grown[...]
    d_grown_b = d_grown.astype(bf16)
    direct = dot(d_grown_b, r.c_mat[...], 0, 0)
    r.direct[...] = direct

    def spread_state(block, carry):
        factor = tall(r.factors[pl.ds(block, 1), :])
        r.p_state[block, own_state, :] = (factor * r.direct[...]).astype(SUM_TYPE)
        return carry

    lax.fori_loop(0, seq, spread_state, 0)
    ring.scatter_step(STATE, 0)
    own_normed = pl.ds(HALO, rows)
    fill(Z, r.normed[own_normed, :], r.d_z[...])
    ring.scatter_step(Z, 0)
    ring.scatter_step(KV, 1)
    ring.scatter_step(MIXED, 1)

    r.d_cum[...] = head_sums(d_ssm * r.carried[...])
    skip_sums = jnp.sum(d_ssm * r.x_conv[...], axis=0, keepdims=True)
    skip_grad = head_sums(skip_sums)
    r.d_c[...] = dot(d_grown_b, r.start_state[...].astype(bf16))
    d_ssm_b = d_ssm.astype(bf16)
    r.d_x[...] = r.skip_row[...] * d_ssm
    r.d_overlap[...] = jnp.zeros_like(r.d_overlap)
    r.d_rows[...] = jnp.zeros_like(r.d_rows)
    r.d_cum_rows[...] = jnp.zeros_like(r.d_cum_rows)
    overlap = dot(r.c_mat[...], r.b_mat[...], 1, 1)
    for p in range(pairs):
        at = pl.ds(p * LANES, LANES)
        x_pair = r.x_bf[:, at]
        d_pair = jnp.zeros((rows, LANES), f32)
        for h in (2 * p, 2 * p + 1):
            own = low_half if h == 2 * p else jnp.logical_not(low_half)
            d_head = jnp.where(own, d_ssm[:, p * LANES : (p + 1) * LANES], 0.0).astype(bf16)
            d_mixing = dot(d_head, x_pair, 1, 1) * decays(h)
            step_row = r.step_t[h : h + 1, :]
            weighted = d_mixing * overlap
            from_step = jnp.sum(weighted, axis=0, keepdims=True)
            r.d_rows[h : h + 1, :] = from_step
            r.d_cum_rows[h : h + 1, :] = -from_step * step_row
            row_total = jnp.sum(weighted * step_row, axis=1, keepdims=True)
            r.d_cum[...] = r.d_cum[...] + jnp.where(lane_h == h, row_total, 0.0)
            r.d_overlap[...] = r.d_overlap[...] + d_mixing * step_row
            d_pair = d_pair + dot(r.mixing[h], d_head, 0, 0)
        r.d_x[:, at] = r.d_x[:, at] + d_pair
        if p == 0:
            ring.scatter_step(STATE, 1)
            ring.scatter_step(KV, 2)
        if p == 1:
            ring.scatter_step(STATE, 2)
            ring.scatter_step(KV, 3)
        if p == 2:
            ring.scatter_step(STATE, 3)
    d_overlap_b = r.d_overlap[...].astype(bf16)
    r.d_c[...] = r.d_c[...] + dot(d_overlap_b, r.b_mat[...])
    r.d_b[...] = dot(d_overlap_b, r.c_mat[...], 0, 0)
    ring.scatter_rest(KV, 4)
    ring.scatter_rest(STATE, 4)
    ring.scatter_rest(FFN, 3)
    ring.scatter_step(Z, 1)
    ring.scatter_step(MIXED, 2)

    own_keys = ring.scatter_end(KV)
    unturned_keys = unturned(own_keys)
    zero = jnp.zeros((rows, LANES), f32)
    d_keys = jnp.where(low_half, unturned_keys, 0.0)
    d_values = jnp.where(low_half, 0.0, own_keys)
    d_keys = jnp.where(first_head, d_keys, half_turned(d_keys))
    d_values = jnp.where(first_head, half_turned(d_values), d_values)
    d_end = ring.scatter_end(STATE)
    d_end_b = d_end.astype(bf16)
    tail = r.tail[...]
    from_end = dot(r.b_mat[...], d_end_b, 1, 1)
    d_x = r.d_x[...] + from_end * tail
    d_tail = head_sums(from_end * r.x_conv[...])
    r.d_b[...] = r.d_b[...] + dot(r.x_tail[...], d_end_b)
    cumulative = r.cumulative[...]
    step_size = r.step_size[...]
    last = cumulative[rows - 1 : rows, :]
    tail_decay = jnp.exp(last - cumulative)
    through = d_tail * tail_decay * step_size
    held = jnp.sum(d_end * r.start_state[...], axis=1, keepdims=True)
    head_row = lax.broadcasted_iota(jnp.int32, (inner, LANES), 0)
    held_heads = jnp.sum(
        jnp.where(lax.div(head_row, SH) == lanes_of((inner, LANES)), held, 0.0),
        axis=0,
        keepdims=True,
    )
    d_last = jnp.sum(through, axis=0, keepdims=True) + jnp.exp(last) * held_heads
    tick_row = lax.broadcasted_iota(jnp.int32, (rows, LANES), 0)
    d_cum = r.d_cum[...] + r.d_cum_rows[...].T - through
    d_cum = d_cum + jnp.where(tick_row == rows - 1, d_last, 0.0)
    d_step = r.d_rows[...].T + d_tail * tail_decay
    rate = -jnp.exp(r.head_rows[1:2, :])
    upto = (tick_s >= tick_t).astype(f32)
    d_log_decay = dot(upto, d_cum, precision=highest)
    d_step = d_step + d_log_decay * rate
    d_dt = d_step * sigmoid(r.dt_in[...] + r.head_rows[0:1, :])
    d_dt = jnp.where(lane_h < heads, d_dt, 0.0)
    r.d_dt[...] = d_dt[:, :HALO].astype(bf16)
    dt_grad = dot(r.d_dt[...], r.normed[pl.ds(HALO, rows), :], 0, 0)
    for k in range(count):
        r.p_dt[k] = dt_grad[:, k * depth : (k + 1) * depth]
    dt_parts = []
    for k, other in enumerate(others):
        target = lax.rem(seq + k + 1, count)
        copy = remote(
            r.p_dt.at[target], r.s_dt.at[seq], r.dt_sems.at[2, k], r.dt_sems.at[3, k], other
        )
        copy.start()
        dt_parts.append(copy)
    small_at = 2 * chunks + CONVK * (inner // LANES + bc_width // LANES)
    r.small[small_at : small_at + 1, :] = jnp.sum(d_dt, axis=0, keepdims=True)
    r.small[small_at + 1 : small_at + 2, :] = (
        jnp.sum(d_log_decay * step_size, axis=0, keepdims=True) * rate
    )
    r.small[small_at + 2 : small_at + 3, :] = skip_grad

    def silu_back(grad, pre):
        opened = sigmoid(pre)
        return grad * opened * (1.0 + pre * (1.0 - opened))

    pad = jnp.zeros((HALO, inner), f32)
    pad_bc = jnp.zeros((HALO, bc_width), f32)
    r.x_back[pl.ds(0, HALO), :] = pad
    r.x_back[pl.ds(HALO, rows), :] = silu_back(d_x, r.x_pre[...])
    r.x_back[pl.ds(HALO + rows, HALO), :] = pad
    d_bc = jnp.concatenate([r.d_b[...], r.d_c[...]], axis=1)
    r.bc_back[pl.ds(0, HALO), :] = pad_bc
    r.bc_back[pl.ds(HALO, rows), :] = silu_back(d_bc, r.bc_pre[...])
    r.bc_back[pl.ds(HALO + rows, HALO), :] = pad_bc

    def back(source, taps, start, length):
        running = taps[0:1, :] * source[pl.ds(start + EDGE, length), :]
        for k in range(1, CONVK):
            running = running + taps[k : k + 1, :] * source[pl.ds(start + EDGE - k, length), :]
        return running

    r.edge_out[:, pl.ds(0, inner)] = back(r.x_back, r.conv_x[...], 0, HALO)
    r.edge_out[:, pl.ds(inner, bc_width)] = back(r.bc_back, r.conv_bc[...], 0, HALO)
    edge = remote(r.edge_out, r.edge_in, r.edge_sems.at[2], r.edge_sems.at[3], preceding)
    edge.start()
    ring.scatter_rest(DOWN, 3)
    ring.scatter_step(Z, 2)
    r.part3[pl.ds(rows, 2 * HALO), :] = jnp.zeros((2 * HALO, r.part3.shape[1]), f32)
    for k in range(CONVK):
        x_tap = jnp.sum(
            r.x_back[pl.ds(HALO, rows), :] * r.x_rows[pl.ds(HALO - EDGE + k, rows), :],
            axis=0,
            keepdims=True,
        )
        for m in range(inner // LANES):
            at = 2 * chunks + k * (inner // LANES) + m
            r.small[at : at + 1, :] = x_tap[:, m * LANES : (m + 1) * LANES]
        r.part3[rows + k : rows + k + 1, pl.ds(0, bc_width)] = jnp.sum(
            r.bc_back[pl.ds(HALO, rows), :] * r.bc_rows[pl.ds(HALO - EDGE + k, rows), :],
            axis=0,
            keepdims=True,
        )
    d_x_in = back(r.x_back, r.conv_x[...], HALO, rows)
    d_bc_in = back(r.bc_back, r.conv_bc[...], HALO, rows)
    edge.wait_recv()
    edges = jnp.where(seq < count - 1, r.edge_in[...], 0.0)
    above = rows - HALO
    r.d_x_b[pl.ds(0, above), :] = d_x_in[:above].astype(bf16)
    r.d_x_b[pl.ds(above, HALO), :] = (d_x_in[above:] + edges[:, :inner]).astype(
        bf16
    )
    r.d_blocks[pl.ds(0, above), pl.ds(0, bc_width)] = d_bc_in[:above]
    r.d_blocks[pl.ds(above, HALO), pl.ds(0, bc_width)] = d_bc_in[above:] + edges[:, inner:]
    r.d_blocks[:, pl.ds(bc_width, LANES)] = d_keys
    r.d_blocks[:, pl.ds(bc_width + LANES, LANES)] = d_values
    block_sum.begin()

    fill(X, r.normed[own_normed, :], r.d_x_b[...])
    ring.scatter_step(X, 0)
    block_sum.middle()
    r.part3[pl.ds(0, rows), :] = dot(r.d_z[...], r.f_z[...].reshape(width, inner), 1, 1) + dot(
        r.d_x_b[...], r.f_x[...].reshape(width, inner), 1, 1
    )
    r.d_rest[:, pl.ds(LANES, LANES)] = block_sum.result().astype(bf16)
    r.part3[pl.ds(0, rows), :] = r.part3[pl.ds(0, rows), :] + dot(
        r.d_rest[...], r.f_rest[...].reshape(width, r.f_rest.shape[2]), 1, 1
    )
    for k in range(count):
        at = (pl.ds(0, rows), pl.ds(k * depth, depth))
        r.part3[at] = r.part3[at] + dot(r.d_dt[...], r.f_dt[k])
    shared_sum.begin()
    fill(REST, r.normed[own_normed, :], r.d_rest[...])
    ring.scatter_step(REST, 0)
    ring.scatter_step(X, 1)
    shared_sum.middle()
    ring.scatter_step(REST, 1)
    ring.scatter_rest(MIXED, 3)
    ring.scatter_rest(Z, 3)
    ring.scatter_step(X, 2)
    shared_sum.finish()
    ring.scatter_step(REST, 2)
    shared_sum.arrived()
    bc_taps = r.total3[pl.ds(rows, 2 * CONVK), pl.ds(0, bc_width)]
    for k in range(CONVK):
        for m in range(bc_width // LANES):
            at = 2 * chunks + CONVK * (inner // LANES) + k * (bc_width // LANES) + m
            r.small[at : at + 1, :] = bc_taps[k : k + 1, m * LANES : (m + 1) * LANES]
    d_normed = r.total3[pl.ds(0, rows), :]
    tokens_wide = r.tokens[...].astype(f32)
    scale_mix = rms_scale(tokens_wide)
    tokens_hat = tokens_wide * scale_mix
    weighted = d_normed * r.gain_mix[...]
    r.grad_tokens[...] = r.d_hidden[...] + scale_mix * (
        weighted - tokens_hat * jnp.mean(weighted * tokens_hat, axis=-1, keepdims=True)
    )
    gain_mix_grad = jnp.sum(d_normed * tokens_hat, axis=0, keepdims=True)
    for k in range(chunks):
        r.small[k : k + 1, :] = gain_mix_grad[:, k * LANES : (k + 1) * LANES]
    used = small_at + 3
    r.small[used:SMALL_ROWS, :] = jnp.zeros((SMALL_ROWS - used, LANES), f32)
    small_copies = []
    for offset in range(1, count):
        copy = remote(
            r.small,
            r.small_slots.at[seq],
            r.small_send.at[offset - 1],
            r.small_receive.at[offset - 1],
            others[offset - 1],
        )
        copy.start()
        small_copies.append(copy)
    ring.scatter_rest(REST, 3)
    ring.scatter_rest(X, 3)
    r.output[...] = (r.hidden[:, output_sum.kept] + output_sum.result()).astype(bf16)
    for name in (DOWN, FFN, MIXED, Z):
        getattr(r, "g_" + name)[...] = ring.scatter_end(name)
    own_rest = ring.scatter_end(REST)
    r.g_blocks[wa] = own_rest[:, LANES : 2 * LANES]
    block_grads.begin()
    r.g_rest[...] = own_rest[:, :LANES]
    for copy in dt_parts:
        copy.wait()
    r.s_dt[pl.ds(seq, 1)] = r.p_dt[pl.ds(seq, 1)]
    dt_total = r.s_dt[0]
    for other in range(1, count):
        dt_total = dt_total + r.s_dt[other]
    r.g_dt[...] = dt_total
    for copy in small_copies:
        copy.wait()
    r.small_slots[pl.ds(seq, 1)] = r.small[...][None]
    total = r.small_slots[0]
    for other in range(1, count):
        total = total + r.small_slots[other]
    r.small_sum[...] = total
    block_grads.forward()
    r.g_x[...] = ring.scatter_end(X)
    block_grads.arrived()

    halo.wait_send()
    for copy in dt_sends:
        copy.wait_send()
    edge.wait_send()
    for name in GATHERED[:6]:
        ring.gather_sent(name)
    for name in SCATTERED:
        ring.scatter_sent(name)
    for sums in (hnormed_sum, shared_sum, output_sum, block_sum, projected, block_grads):
        sums.sent()


def finish_kernel(*refs):
    output_in, tokens_in, small, g_z, g_x, g_rest, g_dt, g_blocks = refs[:8]
    g_mixed, g_ffn, g_down = refs[8:11]
    z, x, bc, dt, out, q, kv, o, gate, up, down = refs[11:22]
    output, grad_tokens, gain_mix, gain_ffn, conv_x, conv_bc, dt_bias, a_log, d_skip = refs[22:]
    output[...] = output_in[...]
    grad_tokens[...] = tokens_in[...]
    inner = z.shape[1]
    z[...] = g_z[...]
    x[...] = g_x[...]
    q[...] = g_rest[...]
    dt[...] = g_dt[pl.ds(0, dt.shape[0]), :]
    for k in range(2):
        bc[:, pl.ds(k * LANES, LANES)] = g_blocks[k]
        kv[:, pl.ds(k * LANES, LANES)] = g_blocks[2 + k]
    ffn_width = gate.shape[1]
    gate[...] = g_ffn[:, pl.ds(0, ffn_width)]
    up[...] = g_ffn[:, pl.ds(ffn_width, ffn_width)]
    out[...] = g_mixed[:, pl.ds(0, inner)].T
    o[...] = g_mixed[:, pl.ds(inner, LANES)].T
    down[...] = g_down[...].T
    sums = small[...]
    at = 0
    for target in (gain_mix, gain_ffn):
        for k in range(target.shape[0] // LANES):
            target[pl.ds(k * LANES, LANES)] = sums[at]
            at += 1
    for target in (conv_x, conv_bc):
        for k in range(CONVK):
            for m in range(target.shape[1] // LANES):
                target[k : k + 1, pl.ds(m * LANES, LANES)] = sums[at : at + 1]
                at += 1
    for target in (dt_bias, a_log, d_skip):
        target[...] = sums[at, : target.shape[0]]
        at += 1


def per_device(
    tokens,
    gain_mix,
    w_z,
    w_x,
    w_bc,
    w_dt,
    conv_x,
    conv_bc,
    dt_bias,
    a_log,
    d_skip,
    w_out,
    w_q,
    w_kv,
    w_o,
    gain_ffn,
    w_gate,
    w_up,
    w_down,
    cotangent,
):
    count = lax.axis_size("seq")
    rows, width = tokens.shape
    depth = w_z.shape[0]
    inner = w_z.shape[1]
    heads = a_log.shape[0]
    ffn = w_gate.shape[1]
    bc_width = w_bc.shape[1]
    lane = np.arange(LANES) % (HD // 2)
    frequency = (ROPE_BASE ** (-(lane * 2.0 / HD))).astype(np.float32)[None]
    inputs = dict(
        tokens=tokens,
        gain_mix=gain_mix[None],
        w_z=w_z,
        w_x=w_x,
        w_bc=w_bc,
        w_dt=w_dt.T,
        conv_x=conv_x,
        conv_bc=conv_bc,
        dt_bias=dt_bias[None],
        a_log=a_log[None],
        d_skip=d_skip[None],
        w_out=w_out,
        w_q=w_q,
        w_kv=w_kv,
        w_o=w_o,
        gain_ffn=gain_ffn[None],
        w_gate=w_gate,
        w_up=w_up,
        w_down=w_down,
        cotangent=cotangent,
        frequency=jnp.asarray(frequency),
    )
    rest = 2 * LANES
    mixed = inner + w_o.shape[0]

    def shape(*dims, dtype=f32):
        return jax.ShapeDtypeStruct(dims, dtype)

    outputs = dict(
        output=shape(rows, width // 4, dtype=bf16),
        grad_tokens=shape(rows, width),
        small_sum=shape(SMALL_ROWS, LANES),
        g_z=shape(depth, inner),
        g_x=shape(depth, inner),
        g_rest=shape(depth, LANES),
        g_dt=shape(HALO, depth),
        g_blocks=shape(4, depth, LANES),
        g_mixed=shape(depth, mixed),
        g_ffn=shape(depth, 2 * ffn),
        g_down=shape(depth, ffn),
    )
    scratch = {}

    def room(dtype, **shapes):
        for name, dims in shapes.items():
            scratch[name] = pltpu.VMEM(dims, dtype)

    pieces = dict(
        z=(depth, inner),
        x=(depth, inner),
        rest=(depth, rest),
        mixed=(depth, mixed),
        ffn=(depth, 2 * ffn),
        down=(depth, ffn),
        kv=(rows, LANES),
        state=(inner + 2 * HALO, LANES),
    )
    for name, dims in pieces.items():
        scratch["f_" + name] = pltpu.VMEM((count, *dims), bf16)
        if name == STATE:
            dims = (inner, LANES)
        if name not in (KV, STATE):
            scratch["p_" + name] = pltpu.VMEM((count, *dims), SUM_TYPE)
        scratch["s_" + name] = pltpu.VMEM((2, count // 2 - 1, *dims), SUM_TYPE)
        scratch["e_" + name] = pltpu.VMEM(dims, SUM_TYPE)
        scratch["h_" + name] = pltpu.VMEM((2, *dims), SUM_TYPE)
    tall, half = rows + 2 * HALO, rows // 2
    whole, wide, head, square = (rows, width), (rows, inner), (rows, LANES), (rows, rows)
    quarter, narrow, across = (rows, width // 4), (LANES, rows), (inner, NS)
    room(f32, part1=whole, total1=whole, near1=(half, width))
    room(f32, part3=(tall, width), total3=(tall, width), near3=(tall // 2, width))
    room(SUM_TYPE, fars1=(half, width), far1=(half, width), far2=(half, width))
    room(SUM_TYPE, fars3=(tall // 2, width), far3=(tall // 2, width))
    room(bf16, halo=(HALO, width), normed=(rows + HALO, width))
    room(f32, bc_rows=(rows + HALO, bc_width), x_rows=(rows + HALO, inner), bc_pre=(rows, bc_width))
    room(bf16, q_pad=(2 * rows, LANES), do_pad=(2 * rows, LANES))
    room(f32, dt_in=head, step_size=head, cumulative=head, d_cum=head, d_b=head, d_c=head)
    room(f32, z_proj=wide, x_pre=wide, x_conv=wide, tail=wide, ssm=wide)
    room(f32, grown=wide, carried=wide, d_x=wide)
    room(bf16, b_mat=(rows, NS), c_mat=(rows, NS), x_tail=wide, x_bf=wide)
    room(f32, cum_t=narrow, step_t=narrow, d_rows=narrow, d_cum_rows=narrow, d_overlap=square)
    room(bf16, mixing=(heads, rows, rows), mixed=(rows, mixed))
    room(f32, row_max=(2 * rows, 1), row_sum=(2 * rows, 1), delta=(2 * rows, 1))
    room(f32, attn_acc=(2 * rows, LANES), factors=(max(8, count), LANES))
    room(f32, start_state=across, direct=across)
    room(f32, hidden=whole, d_hidden=whole, ffn_part=whole)
    room(bf16, hnormed=whole, d_hidden_b=whole, d_ffn=(rows, 2 * ffn), activated=(rows, ffn))
    room(f32, ffn_near=(2, *quarter), blocks=(4, rows + HALO, LANES))
    room(SUM_TYPE, ffn_send=quarter, ffn_far=quarter, block_send=head, block_far=head)
    room(f32, d_blocks=(rows, 4 * LANES), block_near=(2, rows, LANES))
    room(bf16, f_dt=(count, HALO, depth), d_dt=(rows, HALO))
    room(f32, dt_pad=(HALO, depth), p_dt=(count, HALO, depth), s_dt=(count, HALO, depth))
    room(bf16, d_z=wide, d_x_b=wide, d_rest=(rows, rest))
    room(f32, x_back=(tall, inner), bc_back=(tall, bc_width))
    room(f32, edge_out=(HALO, inner + bc_width), edge_in=(HALO, inner + bc_width))
    room(f32, cosine=head, sine=head, head_rows=(8, LANES), skip_row=(1, inner))
    room(f32, small=(SMALL_ROWS, LANES), small_slots=(count, SMALL_ROWS, LANES))
    sems = pltpu.SemaphoreType.DMA
    ring, pairwise, trio = (len(GATHERED), 2, count // 2), (3, 3, 4), (2, 3)
    scratch |= dict(
        gather_send=sems(ring),
        gather_receive=sems(ring),
        scatter_send=sems(ring),
        scatter_receive=sems(ring),
        wa_send=sems(pairwise),
        wa_receive=sems(pairwise),
        edge_sems=sems((4,)),
        dt_sems=sems((4, count - 1)),
        ffn_sems=sems(trio),
        block_sems=sems(trio),
        share_sems=sems(trio),
        grad_sems=sems(trio),
        small_send=sems((count - 1,)),
        small_receive=sems((count - 1,)),
    )
    vmem = pl.BlockSpec(memory_space=pltpu.VMEM)
    results = pl.pallas_call(
        functools.partial(layer_kernel, count, (*inputs, *outputs, *scratch)),
        out_shape=list(outputs.values()),
        in_specs=[vmem] * len(inputs),
        out_specs=[vmem] * len(outputs),
        scratch_shapes=list(scratch.values()),
        compiler_params=pltpu.CompilerParams(
            collective_id=0, has_side_effects=True, vmem_limit_bytes=VMEM_LIMIT
        ),
    )(*inputs.values())
    placed = [w_z, w_x, w_bc, w_dt.T, w_out, w_q, w_kv, w_o, w_gate, w_up, w_down]
    vectors = [gain_mix, gain_ffn, conv_x, conv_bc, dt_bias, a_log, d_skip]
    kinds = [shape(*w.shape) for w in placed] + [jax.ShapeDtypeStruct(v.shape, v.dtype) for v in results[:2]]
    kinds += [shape(*v.shape) for v in vectors]
    finished = pl.pallas_call(
        finish_kernel,
        out_shape=kinds,
        in_specs=[vmem] * len(results),
        out_specs=[vmem] * len(kinds),
        compiler_params=pltpu.CompilerParams(vmem_limit_bytes=VMEM_LIMIT),
    )(*results)
    g_z, g_x, g_bc, g_dt, g_out, g_q, g_kv, g_o, g_gate, g_up, g_down = finished[:11]
    output, grad_tokens, g_gain_mix, g_gain_ffn, *rest_grads = finished[11:]
    return (
        output,
        grad_tokens,
        g_gain_mix,
        g_z,
        g_x,
        g_bc,
        g_dt.T,
        *rest_grads,
        g_out,
        g_q,
        g_kv,
        g_o,
        g_gain_ffn,
        g_gate,
        g_up,
        g_down,
    )


def solution(mesh):
    placed = (
        P("seq", None),
        P(),
        P("seq", "wa"),
        P("seq", "wa"),
        P("seq", None),
        P("seq", "wa"),
        P(None, "wa"),
        P(),
        P("wa"),
        P("wa"),
        P("wa"),
        P("wa", "seq"),
        P("seq", "wa"),
        P("seq", None),
        P("wa", "seq"),
        P(),
        P("seq", "wa"),
        P("seq", "wa"),
        P("wa", "seq"),
        P("seq", None),
    )
    return jax.shard_map(
        per_device,
        mesh=mesh,
        in_specs=placed,
        out_specs=(
            P("seq", "wa"),
            P("seq", None),
            P(),
            P("seq", "wa"),
            P("seq", "wa"),
            P("seq", None),
            P("seq", "wa"),
            P(None, "wa"),
            P(),
            P("wa"),
            P("wa"),
            P("wa"),
            P("wa", "seq"),
            P("seq", "wa"),
            P("seq", None),
            P("wa", "seq"),
            P(),
            P("seq", "wa"),
            P("seq", "wa"),
            P("wa", "seq"),
        ),
        check_vma=False,
    )
```
